32 devices in a mesh: trk: 8 (over z, x), sub: 4 (over y, core).
Axes of the slice: x: 2, y: 2, z: 4, core: 2. Of those that a mesh axis runs over, the one named last changes fastest.
Arguments:
- particle_cells: int32 [3, 262144], P(None, ('trk', 'sub')), may hold values from 0 to 126, as said below
- offsets: float32 [3, 262144], P(None, ('trk', 'sub')), may hold values from 0 to 1
- momenta: float32 [3, 262144], P(None, ('trk', 'sub')), may hold values from -3 to 3
- live_counts: int32 [32], P(('trk', 'sub')), may hold values from 1024 to 8192, as said below
- green_hat: float32 [256, 256, 256], P('trk', None, 'sub'), may hold values from 0.001953125 to 2560, as said below
- orders: int32 [4], replicated, may hold values from 2 to 5
- strengths: float32 [4], replicated, may hold values from -1 to 1
Outputs:
- new_coords: float32 [3, 262144], P(None, ('trk', 'sub'))
- new_momenta: float32 [3, 262144], P(None, ('trk', 'sub'))
The draws below stay inside these ranges and needn't reach their ends.
Inputs may be any that keep to these rules, and one draw needn't show every extreme that they name: cells[0] and cells[1] are at most 126; rows r of particle_cells have a z cell in [s * 16, (s + 1) * 16) with s = r // 32768, and at most 126. `live_counts`: some entry equals 8192 in every draw. `green_hat`: positive.
All inputs are finite; a program needn't handle non-finite values.
Results may differ from the reference program's by a relative error of at most 0.0003.
Values sent between devices are 32-bit elements; how exact they have to be, the bound alone decides.
No kernel may reach another device: no remote copies, remote signals or barrier semaphores. Data moves between devices by JAX's collectives and lax.ppermute only.
A program may use at most 64 MiB of HBM per device.

```python
import jax
import jax.numpy as jnp

NG = 128
PART_DEV = 8192
MAGNETS = 4
SLAB = 16
ROWS_SLAB = 32768
PARTS_SIZE = 262144
N_TRK = 8
N_SUB = 4


def draw_particle_cells(key, part):
    key_x, key_y, key_z = jax.random.split(key, 3)
    row_ids = jnp.arange(PARTS_SIZE, dtype=jnp.int32)
    slab_ids = row_ids // ROWS_SLAB
    cell_x = jax.random.randint(key_x, (PARTS_SIZE,), 0, NG - 1, dtype=jnp.int32)
    cell_y = jax.random.randint(key_y, (PARTS_SIZE,), 0, NG - 1, dtype=jnp.int32)
    upper = jnp.where(slab_ids == N_TRK - 1, SLAB - 1, SLAB)
    cell_z = slab_ids * SLAB + jax.random.randint(key_z, (PARTS_SIZE,), 0, upper, dtype=jnp.int32)
    cell_x = cell_x.at[0].set(NG - 2)
    cell_y = cell_y.at[0].set(NG - 2)
    cell_z = cell_z.at[PARTS_SIZE - 1].set(NG - 2)
    return jnp.stack([cell_x, cell_y, cell_z]).astype(jnp.int32)


def draw_live_counts(key, part):
    device_ids = jnp.arange(N_TRK * N_SUB, dtype=jnp.int32)
    slab_ids = device_ids // N_SUB
    member = device_ids % N_SUB
    distance = jnp.maximum(jnp.abs(2 * slab_ids + 1 - N_TRK) - 1, 0)
    dropped = 3 * PART_DEV // 4 * distance // max(N_TRK - 2, 1)
    jitter = jax.random.randint(key, (N_TRK * N_SUB,), 0, PART_DEV // 8 + 1, dtype=jnp.int32)
    jitter = jnp.where(member == 0, 0, jitter)
    return (PART_DEV - dropped - jitter).astype(jnp.int32)


def draw_green_hat(key, part):
    freq = jnp.arange(2 * NG, dtype=jnp.float32)
    sines = jnp.sin(jnp.pi * freq / (2 * NG)) ** 2
    eigen = 4.0 * (sines[:, None, None] + sines[None, :, None] + sines[None, None, :])
    shape = (2 * NG, 2 * NG, 2 * NG)
    rough = jnp.exp(0.3 * jnp.clip(jax.random.normal(key, shape, jnp.float32), -3.0, 3.0))
    return (8.0 * rough / (NG * (eigen + 1.0 / (NG * NG)))).astype(jnp.float32)


def place_ends(values, rng, smallest, high):
    extent = values.shape
    spot = [jax.random.randint(jax.random.fold_in(rng, axis), (), 0, extent[axis]) for axis in range(len(extent))]
    values = values.at[tuple(spot)].set(smallest)
    longest = extent.index(max(extent))
    spot[longest] = (spot[longest] + 1) % extent[longest]
    return values.at[tuple(spot)].set(high)


def block_scale(stream_key, dims, cuts, least, high):
    factor_of = 1.0
    for dim, parts in cuts:
        steps = jax.random.uniform(jax.random.fold_in(jax.random.fold_in(stream_key, 6), dim), (parts,), jnp.float32, least / len(cuts), high / len(cuts))
        factor_of = factor_of * jnp.repeat(jnp.exp(steps), dims[dim] // parts).reshape((-1,) + (1,) * (len(dims) - 1 - dim))
    return factor_of


def noise(key, dims, deviation, bound, cuts=(), kind=jnp.bfloat16):
    level = block_scale(key, dims, cuts, -0.22, 0.18) if cuts else 1.0
    array = jax.random.normal(key, dims, jnp.float32) * deviation * level
    return jnp.minimum(jnp.maximum(array, -bound), bound).astype(kind)


def setup_inputs(seed: int = 0) -> dict:
    keys = jax.random.split(jax.random.key(seed), 8)
    return {
        "particle_cells": draw_particle_cells(jax.random.fold_in(keys[7], 71), 0),
        "offsets": jnp.clip(1.0 * jax.random.uniform(keys[1], (3, PARTS_SIZE), jnp.float32) ** block_scale(keys[1], (3, PARTS_SIZE), ((1, 32),), -0.2, 0.2), 0.0, 1.0),
        "momenta": noise(keys[2], (3, PARTS_SIZE), 0.5, 3.0, ((1, 32),), jnp.float32),
        "live_counts": draw_live_counts(jax.random.fold_in(keys[7], 71), 0),
        "green_hat": draw_green_hat(jax.random.fold_in(keys[7], 71), 0),
        "orders": place_ends(jax.random.randint(keys[5], (MAGNETS,), 2, 6), jax.random.fold_in(keys[5], 1), 2, 5).astype(jnp.int32),
        "strengths": jnp.clip(jax.random.uniform(keys[6], (MAGNETS,), jnp.float32, -1.0, 1.0), -1.0, 1.0),
    }


def corner_list(offsets):
    lower = 1.0 - offsets
    result = []
    for shift_x in (0, 1):
        for shift_y in (0, 1):
            for shift_z in (0, 1):
                weight_x = offsets[0] if shift_x else lower[0]
                weight_y = offsets[1] if shift_y else lower[1]
                weight_z = offsets[2] if shift_z else lower[2]
                result.append((weight_x * weight_y * weight_z, shift_x, shift_y, shift_z))
    return result


def multipole_push(particle_cells, offsets, orders, strengths):
    centre = 0.5 * NG
    real_u = (particle_cells[0].astype(jnp.float32) + offsets[0] - centre) / centre
    imag_u = (particle_cells[1].astype(jnp.float32) + offsets[1] - centre) / centre
    power_re = real_u
    power_im = imag_u
    push_x = jnp.zeros_like(real_u)
    push_y = jnp.zeros_like(real_u)
    for degree in range(1, 5):
        coeff = jnp.sum(jnp.where(orders - 1 == degree, strengths, jnp.zeros_like(strengths)))
        push_x = push_x - coeff * power_re
        push_y = push_y + coeff * power_im
        power_re, power_im = power_re * real_u - power_im * imag_u, power_re * imag_u + power_im * real_u
    return push_x, push_y


def reference(particle_cells, offsets, momenta, live_counts, green_hat, orders, strengths):
    count_all = particle_cells.shape[1]
    row_ids = jnp.arange(count_all, dtype=jnp.int32)
    alive = (row_ids % PART_DEV) < live_counts[row_ids // PART_DEV]
    unit_charge = float(NG ** 3) / float(PARTS_SIZE)
    charge = jnp.where(alive, jnp.full((count_all,), unit_charge, jnp.float32), jnp.zeros((count_all,), jnp.float32))
    corners = corner_list(offsets)
    cell_x = particle_cells[0]
    cell_y = particle_cells[1]
    cell_z = particle_cells[2]
    density = jnp.zeros((NG * NG * NG,), jnp.float32)
    places = []
    for weight, shift_x, shift_y, shift_z in corners:
        place = ((cell_x + shift_x) * NG + cell_z + shift_z) * NG + cell_y + shift_y
        places.append(place)
        density = density.at[place].add(charge * weight)
    density = density.reshape(NG, NG, NG)
    padded = jnp.zeros((2 * NG, 2 * NG, 2 * NG), jnp.float32).at[:NG, :NG, :NG].set(density)
    spectrum = jnp.fft.fftn(padded) * green_hat
    potential = jnp.real(jnp.fft.ifftn(spectrum))[:NG, :NG, :NG].astype(jnp.float32)
    beside_all = jnp.pad(potential, 1)
    field_x = -0.5 * (beside_all[2:, 1:-1, 1:-1] - beside_all[:-2, 1:-1, 1:-1])
    field_z = -0.5 * (beside_all[1:-1, 2:, 1:-1] - beside_all[1:-1, :-2, 1:-1])
    field_y = -0.5 * (beside_all[1:-1, 1:-1, 2:] - beside_all[1:-1, 1:-1, :-2])
    field_all = jnp.stack([field_x, field_y, field_z]).reshape(3, -1)
    kick = jnp.zeros((3, count_all), jnp.float32)
    for entry, place in zip(corners, places):
        kick = kick + entry[0] * field_all[:, place]
    push_x, push_y = multipole_push(particle_cells, offsets, orders, strengths)
    push = jnp.stack([push_x, push_y, jnp.zeros_like(push_x)])
    new_momenta = momenta + kick + push
    new_coords = particle_cells.astype(jnp.float32) + offsets + new_momenta
    return (new_coords, new_momenta)
```

```python
import math

import jax
import jax.numpy as jnp
import ml_dtypes
import numpy as np
from jax import lax
from jax.experimental import pallas as pl
from jax.experimental.pallas import tpu as pltpu
from jax.sharding import PartitionSpec as P

NG = 128


HIGHEST = lax.Precision.HIGHEST


def multipole_push(particle_cells, offsets, orders, strengths):
    centre = 0.5 * NG
    real_u = (particle_cells[0].astype(jnp.float32) + offsets[0] - centre) / centre
    imag_u = (particle_cells[1].astype(jnp.float32) + offsets[1] - centre) / centre
    power_re = real_u
    power_im = imag_u
    push_x = jnp.zeros_like(real_u)
    push_y = jnp.zeros_like(real_u)
    for degree in range(1, 5):
        coeff = jnp.sum(jnp.where(orders - 1 == degree, strengths, jnp.zeros_like(strengths)))
        push_x = push_x - coeff * power_re
        push_y = push_y + coeff * power_im
        power_re, power_im = (
            power_re * real_u - power_im * imag_u,
            power_re * imag_u + power_im * real_u,
        )
    return (push_x, push_y)


def wave_table(freq_ids, place_ids, length):
    phase_int = freq_ids[:, None] * place_ids[None, :] % length
    angle = 2.0 * math.pi / length * phase_int.astype(jnp.float32)
    return (jnp.cos(angle), jnp.sin(angle))


def tent_weights(cells, fraction, length):
    places = jnp.arange(length, dtype=jnp.int32)
    lower = jnp.where(places[None, :] == cells[:, None], (1.0 - fraction)[:, None], 0.0)
    upper = jnp.where(places[None, :] == cells[:, None] + 1, fraction[:, None], 0.0)
    return lower + upper


def block_weights(cells_x, cells_y, cells_z, frac_x, frac_y, frac_z, depth):
    weight_x = tent_weights(cells_x, frac_x, NG)
    weight_y = tent_weights(cells_y, frac_y, NG)
    weight_z = tent_weights(cells_z, frac_z, depth)
    plane_xz = (weight_x[:, :, None] * weight_z[:, None, :]).reshape(cells_x.shape[0], -1)
    return (plane_xz, weight_y)


def per_device(particle_cells, offsets, momenta, live_counts, green_hat, orders, strengths):
    trk_count = lax.axis_size("trk")
    sub_count = lax.axis_size("sub")
    slab_depth = NG // trk_count
    depth = slab_depth + 1
    doubled = 2 * NG
    count_here = particle_cells.shape[1]
    count_all = count_here * trk_count * sub_count
    row_ids = jnp.arange(count_here, dtype=jnp.int32)
    unit_charge = float(NG**3) / float(count_all)
    charge = jnp.where(
        row_ids < live_counts[0],
        jnp.full((count_here,), unit_charge, jnp.float32),
        jnp.zeros((count_here,), jnp.float32),
    )
    local_z = particle_cells[2] - lax.axis_index("trk") * slab_depth
    block_len = math.gcd(count_here, 512)
    block_count = count_here // block_len
    blocked_x = particle_cells[0].reshape(block_count, block_len)
    blocked_y = particle_cells[1].reshape(block_count, block_len)
    blocked_z = local_z.reshape(block_count, block_len)
    blocked_off = offsets.reshape(3, block_count, block_len).transpose(1, 0, 2)
    blocked_charge = charge.reshape(block_count, block_len)

    def deposit_step(total, items):
        bx, by, bz, boff, bcharge = items
        plane_xz, weight_y = block_weights(bx, by, bz, boff[0], boff[1], boff[2], depth)
        charged = plane_xz * bcharge[:, None]
        return (total + jnp.einsum("pa,py->ay", charged, weight_y, precision=HIGHEST), None)

    start_total = jnp.zeros((NG * depth, NG), jnp.float32)
    deposit, _ = lax.scan(
        deposit_step, start_total, (blocked_x, blocked_y, blocked_z, blocked_off, blocked_charge)
    )
    deposit = deposit.reshape(NG, depth, NG)
    density = lax.psum_scatter(deposit, "sub", scatter_dimension=0, tiled=True)
    freq_all = jnp.arange(doubled, dtype=jnp.int32)
    cell_ids = jnp.arange(NG, dtype=jnp.int32)
    cos_cells, sin_cells = wave_table(freq_all, cell_ids, doubled)
    spec_re = jnp.einsum("xzy,ky->xzk", density, cos_cells, precision=HIGHEST)
    spec_im = -jnp.einsum("xzy,ky->xzk", density, sin_cells, precision=HIGHEST)
    part_re = lax.all_to_all(spec_re, "sub", split_axis=2, concat_axis=0, tiled=True)
    part_im = lax.all_to_all(spec_im, "sub", split_axis=2, concat_axis=0, tiled=True)
    out_re = jnp.einsum("kn,nzq->kzq", cos_cells, part_re, precision=HIGHEST) + jnp.einsum(
        "kn,nzq->kzq", sin_cells, part_im, precision=HIGHEST
    )
    out_im = jnp.einsum("kn,nzq->kzq", cos_cells, part_im, precision=HIGHEST) - jnp.einsum(
        "kn,nzq->kzq", sin_cells, part_re, precision=HIGHEST
    )
    xspec_re = out_re
    xspec_im = out_im
    slab_starts = jnp.arange(trk_count, dtype=jnp.int32)[:, None] * slab_depth
    forward_places = (slab_starts + jnp.arange(slab_depth + 1, dtype=jnp.int32)[None, :]).reshape(
        -1
    )
    cos_fwd, sin_fwd = wave_table(freq_all, forward_places, doubled)
    part_re = lax.all_to_all(xspec_re, "trk", split_axis=0, concat_axis=1, tiled=True)
    part_im = lax.all_to_all(xspec_im, "trk", split_axis=0, concat_axis=1, tiled=True)
    out_re = jnp.einsum("kn,xnq->xkq", cos_fwd, part_re, precision=HIGHEST) + jnp.einsum(
        "kn,xnq->xkq", sin_fwd, part_im, precision=HIGHEST
    )
    out_im = jnp.einsum("kn,xnq->xkq", cos_fwd, part_im, precision=HIGHEST) - jnp.einsum(
        "kn,xnq->xkq", sin_fwd, part_re, precision=HIGHEST
    )
    zspec_re = out_re
    zspec_im = out_im
    scaled_re = zspec_re * green_hat
    scaled_im = zspec_im * green_hat
    back_places = (slab_starts - 1 + jnp.arange(slab_depth + 3, dtype=jnp.int32)[None, :]).reshape(
        -1
    )
    inside = ((back_places >= 0) & (back_places < NG)).astype(jnp.float32) / doubled
    cos_back, sin_back = wave_table(back_places, freq_all, doubled)
    cos_back = cos_back * inside[:, None]
    sin_back = sin_back * inside[:, None]
    plane_re = jnp.einsum("nk,xkq->xnq", cos_back, scaled_re, precision=HIGHEST) - jnp.einsum(
        "nk,xkq->xnq", sin_back, scaled_im, precision=HIGHEST
    )
    plane_im = jnp.einsum("nk,xkq->xnq", sin_back, scaled_re, precision=HIGHEST) + jnp.einsum(
        "nk,xkq->xnq", cos_back, scaled_im, precision=HIGHEST
    )
    cos_inverse = jnp.transpose(cos_cells) / doubled
    sin_inverse = jnp.transpose(sin_cells) / doubled
    part_re = lax.all_to_all(plane_re, "trk", split_axis=1, concat_axis=0, tiled=True)
    part_im = lax.all_to_all(plane_im, "trk", split_axis=1, concat_axis=0, tiled=True)
    out_re = jnp.einsum("nk,kzq->nzq", cos_inverse, part_re, precision=HIGHEST) - jnp.einsum(
        "nk,kzq->nzq", sin_inverse, part_im, precision=HIGHEST
    )
    out_im = jnp.einsum("nk,kzq->nzq", sin_inverse, part_re, precision=HIGHEST) + jnp.einsum(
        "nk,kzq->nzq", cos_inverse, part_im, precision=HIGHEST
    )
    cos_final = cos_cells / doubled
    sin_final = sin_cells / doubled
    part_re = lax.all_to_all(out_re, "sub", split_axis=0, concat_axis=2, tiled=True)
    part_im = lax.all_to_all(out_im, "sub", split_axis=0, concat_axis=2, tiled=True)
    block_rows = jnp.einsum("xzk,ky->xzy", part_re, cos_final, precision=HIGHEST) - jnp.einsum(
        "xzk,ky->xzy", part_im, sin_final, precision=HIGHEST
    )
    potential = lax.all_gather(block_rows, "sub", axis=0, tiled=True)
    middle = potential[:, 1 : slab_depth + 2]
    around_x = jnp.pad(middle, ((1, 1), (0, 0), (0, 0)))
    field_x = -0.5 * (around_x[2:] - around_x[:-2])
    around_y = jnp.pad(middle, ((0, 0), (0, 0), (1, 1)))
    field_y = -0.5 * (around_y[:, :, 2:] - around_y[:, :, :-2])
    field_z = -0.5 * (potential[:, 2 : slab_depth + 3] - potential[:, : slab_depth + 1])
    field_table = jnp.stack([field_x, field_y, field_z], axis=2).reshape(NG * depth, 3 * NG)

    def sample_step(carry, items):
        bx, by, bz, boff = items
        plane_xz, weight_y = block_weights(bx, by, bz, boff[0], boff[1], boff[2], depth)
        lines = jnp.dot(plane_xz, field_table, precision=HIGHEST).reshape(bx.shape[0], 3, NG)
        return (carry, jnp.sum(lines * weight_y[:, None, :], axis=2))

    _, sampled = lax.scan(
        sample_step, jnp.zeros((), jnp.float32), (blocked_x, blocked_y, blocked_z, blocked_off)
    )
    kick = sampled.reshape(count_here, 3).transpose(1, 0)
    push_x, push_y = multipole_push(particle_cells, offsets, orders, strengths)
    push = jnp.stack([push_x, push_y, jnp.zeros_like(push_x)])
    new_momenta = momenta + kick + push
    new_coords = particle_cells.astype(jnp.float32) + offsets + new_momenta
    return (new_coords, new_momenta)


def halves(values):
    upper = values.astype(jnp.bfloat16)
    return (upper, (values - upper.astype(jnp.float32)).astype(jnp.bfloat16))


def table_halves(table):
    upper = table.astype(ml_dtypes.bfloat16)
    lower = (table - upper.astype(np.float64)).astype(ml_dtypes.bfloat16)
    return (jnp.asarray(upper), jnp.asarray(lower))


def mm(left, right):
    return jnp.dot(left, right, preferred_element_type=jnp.float32)


def mm_t(left, right):
    return lax.dot_general(left, right, (((1,), (1,)), ((), ())), preferred_element_type=jnp.float32)


def mm3(left, right):
    return mm(left[0], right[0]) + (mm(left[0], right[1]) + mm(left[1], right[0]))


def turn_blocks(parts):
    lanes = lax.broadcasted_iota(jnp.int32, parts[0].shape, 1)
    low = lanes < 64
    even = (lanes // 32) % 2 == 0
    pairs = []
    for first, second in ((parts[0], parts[2]), (parts[1], parts[3])):
        pairs.append(
            (
                jnp.where(low, first, pltpu.roll(second, 64, 1)),
                jnp.where(low, pltpu.roll(first, 64, 1), second),
            )
        )
    result = []
    for half in (0, 1):
        first, second = pairs[0][half], pairs[1][half]
        result.append(jnp.where(even, first, pltpu.roll(second, 32, 1)))
        result.append(jnp.where(even, pltpu.roll(first, 96, 1), second))
    return result


def tent(places, cells, fraction):
    away = places - cells
    return jnp.where(away == 0.0, 1.0 - fraction, jnp.where(away == 1.0, fraction, 0.0))


QUAD = 4
PLANES = 5
WIDE = 32
GROUPS = 9
SLOTS = 4 * GROUPS
FWD_ROWS = GROUPS * 2 * QUAD
BACK_ROWS = FWD_ROWS + 24
LOT = 512
PACK = 256
BIG = 56 * 1024 * 1024


def deposit_block(acc_ref, rows, zoff, count):
    y_ids = lax.broadcasted_iota(jnp.int32, (NG, LOT), 0).astype(jnp.float32)
    weight_x = halves(tent(y_ids, rows[0:1], rows[3:4]))
    right = jnp.concatenate([weight_x[0], weight_x[1]], axis=0)
    weight_y = tent(y_ids, rows[1:2], rows[4:5])
    cell_z = rows[2:3] - zoff
    for z in range(count):
        here = float(z)
        weight_z = jnp.where(
            cell_z == here, 1.0 - rows[5:6], jnp.where(cell_z == here - 1.0, rows[5:6], 0.0)
        )
        left = halves(weight_y * weight_z)
        acc_ref[z * NG : (z + 1) * NG, :] += mm_t(left[0], right) + mm_t(left[1], right)


def deposit_own(place_ref, rows_ref, acc_ref):
    acc_ref[...] = jnp.zeros_like(acc_ref)
    zoff = (place_ref[0] * QUAD).astype(jnp.float32)

    def step(lot, carry):
        rows = rows_ref[:, pl.ds(pl.multiple_of(lot * LOT, LOT), LOT)]
        deposit_block(acc_ref, rows, zoff, PLANES)
        return carry

    lax.fori_loop(0, rows_ref.shape[1] // LOT, step, 0)


def deposit_rest(place_ref, rows_ref, start_ref, dens_ref, acc_ref):
    acc_ref[...] = start_ref[...]
    me = place_ref[0]
    members = rows_ref.shape[0] // 8
    zoff = (me * QUAD).astype(jnp.float32)
    lots = rows_ref.shape[1] // LOT

    def step(item, carry):
        owner = lax.rem(me + 1 + item // lots, members)
        lot = lax.rem(item, lots)
        rows = rows_ref[
            pl.ds(pl.multiple_of(owner * 8, 8), 8), pl.ds(pl.multiple_of(lot * LOT, LOT), LOT)
        ]
        deposit_block(acc_ref, rows, zoff, PLANES)
        return carry

    lax.fori_loop(0, lots * (members - 1), step, 0)
    dens_ref[...] = acc_ref[:, 0:NG] + acc_ref[:, NG : 2 * NG]


def forward_planes(dens_ref, rim_ref, ty_hi, ty_lo, tx_hi, tx_lo, out_ref, left_ref, right_ref):
    half = 16 * GROUPS
    for z in range(QUAD):
        plane = dens_ref[z * NG : (z + 1) * NG, :]
        if z == 0:
            plane = plane + rim_ref[...]
        lines = mm3((ty_hi[...], ty_lo[...]), halves(plane))
        real, imag = lines[0:half], lines[half : 2 * half]
        left_ref[pl.ds(2 * z, half, stride=8), :] = real
        right_ref[pl.ds(2 * z, half, stride=8), :] = imag
        left_ref[pl.ds(2 * z + 1, half, stride=8), :] = imag
        right_ref[pl.ds(2 * z + 1, half, stride=8), :] = -real
    for s in range(4):
        whole = []
        for i in range(4):
            start = (i * 4 + s) * FWD_ROWS
            piece = slice(start, start + FWD_ROWS)
            lines = jnp.concatenate([left_ref[piece, :], right_ref[piece, :]], axis=1)
            whole.append(mm3(halves(lines), (tx_hi[...], tx_lo[...])))
        for th in range(2):
            turned = turn_blocks([part[:, th * NG : (th + 1) * NG] for part in whole])
            for t in range(4):
                out_ref[(th * 4 + t) * 4 + s] = turned[t]


def green_pairs(own_ref, far_ref, edge_ref, pick_ref, out_ref, *parts):
    for side in range(2):
        lanes = slice(side * NG, (side + 1) * NG)
        parts[side][...] = own_ref[:, lanes]
        parts[2 + side][...] = far_ref[:, lanes]

    def pull(refs, start, stride):
        return jnp.concatenate(
            [ref[pl.ds(start, WIDE, stride=stride), :] for ref in refs], axis=1
        )

    for group in range(GROUPS):
        near, away = [], []
        for i in range(4):
            j = group * 4 + i
            if j > WIDE:
                near.append(jnp.zeros((WIDE, 2 * NG), jnp.float32))
                away.append(jnp.zeros((WIDE, 2 * NG), jnp.float32))
                continue
            near.append(pull(parts[0:2], j, 2 * WIDE))
            away.append(edge_ref[...] if j == 0 else pull(parts[2:4], WIDE - j, WIDE))
        both = jnp.concatenate(
            [jnp.concatenate(near, axis=0), jnp.concatenate(away, axis=0)], axis=1
        )
        high = both.astype(jnp.bfloat16)
        left = both - high.astype(jnp.float32)
        mid = left.astype(jnp.bfloat16)
        low = (left - mid.astype(jnp.float32)).astype(jnp.bfloat16)
        pick = pick_ref[...]
        out_ref[:, group * NG : (group + 1) * NG] = 0.5 * (
            mm_t(pick, high) + (mm_t(pick, mid) + mm_t(pick, low))
        )


def spectrum_stage(in_ref, green_ref, wf_hi, wf_lo, wb_hi, wb_lo, out_ref):
    slabs = in_ref.shape[0]
    half = 2 * NG
    for first in range(0, GROUPS, 2):
        groups = [g for g in (first, first + 1) if g < GROUPS]
        data = [in_ref[:, g * 8 : (g + 1) * 8, :].reshape(slabs * 8, NG) for g in groups]
        data = data[0] if len(data) == 1 else jnp.concatenate(data, axis=1)
        spec = mm3((wf_hi[...], wf_lo[...]), halves(data))
        green = green_ref[:, first * NG : (first + len(groups)) * NG]
        scaled = jnp.concatenate([spec[0:half] * green, spec[half : 2 * half] * green], axis=0)
        back = mm3((wb_hi[...], wb_lo[...]), halves(scaled))
        for place, g in enumerate(groups):
            part = back[:, place * NG : (place + 1) * NG]
            for slab in range(slabs):
                row = slab * BACK_ROWS + g * 8
                out_ref[row : row + 8, :] = part[slab * 8 : slab * 8 + 8]
            for c in range(2):
                start = slabs * (8 + c)
                out_ref[pl.ds(FWD_ROWS + 2 * g + c, slabs, stride=BACK_ROWS), :] = part[
                    start : start + slabs
                ]
    for row in range(FWD_ROWS + 2 * GROUPS, BACK_ROWS):
        out_ref[pl.ds(row, slabs, stride=BACK_ROWS), :] = jnp.zeros((slabs, NG), jnp.float32)


def inverse_planes(
    in_ref, tx_hi, tx_lo, ty_hi, ty_lo, te_hi, te_lo, out_ref, mid_cos, mid_sin, top_cos, top_sin
):
    extra = BACK_ROWS - FWD_ROWS
    for s in range(4):
        main, rest = [[], [], [], []], [[], [], [], []]
        for th in range(2):
            parts = [in_ref[(th * 4 + t) * 4 + s, 0:FWD_ROWS, :] for t in range(4)]
            tops = [in_ref[(th * 4 + t) * 4 + s, FWD_ROWS:BACK_ROWS, :] for t in range(4)]
            for i, block in enumerate(turn_blocks(parts)):
                main[i].append(block)
            for i, block in enumerate(turn_blocks(tops)):
                rest[i].append(block)
        for i in range(4):
            row = (i * 4 + s) * FWD_ROWS
            lines = jnp.concatenate(main[i], axis=1)
            lines = mm3(halves(lines), (tx_hi[...], tx_lo[...]))
            mid_cos[row : row + FWD_ROWS, :] = lines[:, 0:NG]
            mid_sin[row : row + FWD_ROWS, :] = lines[:, NG : 2 * NG]
            row = (i * 4 + s) * extra
            lines = jnp.concatenate(rest[i], axis=1)
            lines = mm3(halves(lines), (tx_hi[...], tx_lo[...]))
            top_cos[row : row + extra, :] = lines[:, 0:NG]
            top_sin[row : row + extra, :] = lines[:, NG : 2 * NG]

    def finish(cos_ref, sin_ref, start, count, stride, table):
        real, imag = pl.ds(start, count, stride=stride), pl.ds(start + 1, count, stride=stride)
        lines = jnp.concatenate(
            [cos_ref[real, :] - sin_ref[imag, :], sin_ref[real, :] + cos_ref[imag, :]], axis=0
        )
        return mm3((table[0][...], table[1][...]), halves(lines))

    for z in range(QUAD):
        out_ref[z] = finish(mid_cos, mid_sin, 2 * z, 16 * GROUPS, 8, (ty_hi, ty_lo))
    out_ref[QUAD] = finish(top_cos, top_sin, 0, 8 * extra, 2, (te_hi, te_lo))


SORT_BITS = 13


def sort_network(items):
    shape = (8, NG)
    lanes = lax.broadcasted_iota(jnp.int32, shape, 1)
    subs = lax.broadcasted_iota(jnp.int32, shape, 0)
    ranks = [
        v + subs * 8 + (lanes // 64) * 64 + (lanes % 64) * 128 for v in range(8)
    ]

    def across(values, bit):
        if bit < 3:
            return [values[v ^ (1 << bit)] for v in range(8)]
        if bit < 6:
            index = subs ^ (1 << (bit - 3))
            return [jnp.take_along_axis(value, index, axis=0) for value in values]
        index = lanes ^ (64 if bit == 6 else 1 << (bit - 7))
        return [jnp.take_along_axis(value, index, axis=1) for value in values]

    for size in range(SORT_BITS):
        for bit in range(size, -1, -1):
            others = [across(item, bit) for item in items]
            fresh = [[] for _ in items]
            for v in range(8):
                keep = (((ranks[v] >> bit) ^ (ranks[v] >> (size + 1))) & 1) == 0
                take = (others[0][v] < items[0][v]) == keep
                for n in range(len(items)):
                    fresh[n].append(jnp.where(take, others[n][v], items[n][v]))
            items = fresh
    return items


def laid_out(values):
    turned = jnp.transpose(jnp.concatenate(values, axis=0), (1, 0))
    return jnp.concatenate([turned[0:64], turned[64:128]], axis=1)


def sort_particles(cells_ref, offs_ref, out_int, out_off):
    shape = (8, NG)
    lanes = lax.broadcasted_iota(jnp.int32, shape, 1)
    subs = lax.broadcasted_iota(jnp.int32, shape, 0)
    keys, packs, offs = [], [], [[], [], []]
    for v in range(8):
        rows = slice(v * 8, v * 8 + 8)
        label = (
            (subs + v * 8) * 128 + (lanes // 64) * 64 + (lanes % 8) * 8 + (lanes // 8) % 8
        )
        keys.append(cells_ref[1, rows, :] * 8192 + label)
        packs.append(cells_ref[0, rows, :] * 64 + cells_ref[2, rows, :])
        for d in range(3):
            offs[d].append(offs_ref[d, rows, :])
    items = [laid_out(item) for item in sort_network([keys, packs] + offs)]
    out_int[0] = items[0] // 8192
    out_int[1] = items[0] % 8192
    out_int[2] = items[1] // 64
    out_int[3] = items[1] % 64
    for d in range(3):
        out_off[d] = items[2 + d]


def sample(low_ref, high_ref, pot_ref, int_ref, off_ref, out_ref, field_ref, kick_ref):
    depth = field_ref.shape[1]
    rows = lax.broadcasted_iota(jnp.int32, (NG, NG), 0)
    lanes = lax.broadcasted_iota(jnp.int32, (NG, NG), 1)
    for z in range(depth):
        plane = pot_ref[z + 1]
        right = jnp.where(lanes == NG - 1, 0.0, pltpu.roll(plane, NG - 1, 1))
        left = jnp.where(lanes == 0, 0.0, pltpu.roll(plane, 1, 1))
        field_ref[0, z] = -0.5 * (right - left)
        right = jnp.where(rows == NG - 1, 0.0, pltpu.roll(plane, NG - 1, 0))
        left = jnp.where(rows == 0, 0.0, pltpu.roll(plane, 1, 0))
        field_ref[1, z] = -0.5 * (right - left)
        field_ref[2, z] = -0.5 * (pot_ref[z + 2] - pot_ref[z])

    x_ids = lax.broadcasted_iota(jnp.int32, (NG, PACK), 0)
    z_ids = lax.broadcasted_iota(jnp.int32, (24, PACK), 0)
    y_ids = lax.broadcasted_iota(jnp.int32, (8, PACK), 0)

    def row(ref, which, pack):
        return jnp.concatenate(
            [ref[which, pl.ds(2 * pack, 1), :], ref[which, pl.ds(2 * pack + 1, 1), :]], axis=1
        )

    def weights(ids, cells, fraction):
        away = ids - cells
        return jnp.where(away == 0, 1.0 - fraction, jnp.where(away == 1, fraction, 0.0))

    def pack_step(pack, carry):
        cell_y = row(int_ref, 0, pack)
        off_y = row(off_ref, 1, pack)
        weight_x = halves(weights(x_ids, row(int_ref, 2, pack), row(off_ref, 0, pack)))
        tall = [jnp.concatenate([part, part], axis=0) for part in weight_x]
        weight_z = weights(z_ids, row(int_ref, 3, pack), row(off_ref, 2, pack))
        low = low_ref[pack] // 8
        high = (high_ref[pack] + 1) // 8

        def chunk_step(chunk, kicks):
            start = pl.multiple_of(chunk * 8, 8)
            weight_y = weights(y_ids + start, cell_y, off_y)
            fresh = []
            for d in range(3):
                table = field_ref[d, :, pl.ds(start, 8), :].reshape(depth * 8, NG)
                part = jnp.concatenate(halves(table), axis=1)
                lines = mm(part, tall[0]) + mm(part, tall[1])
                total = lines[0:8] * weight_z[0:1]
                for z in range(1, depth):
                    total = total + lines[z * 8 : z * 8 + 8] * weight_z[z : z + 1]
                fresh.append(kicks[d] + jnp.sum(total * weight_y, axis=0, keepdims=True))
            return tuple(fresh)

        zero = jnp.zeros((1, PACK), jnp.float32)
        kicks = lax.fori_loop(low, high + 1, chunk_step, (zero, zero, zero))
        for d in range(3):
            kick_ref[d, pl.ds(2 * pack, 1), :] = kicks[d][:, 0:NG]
            kick_ref[d, pl.ds(2 * pack + 1, 1), :] = kicks[d][:, NG : 2 * NG]
        return carry

    lax.fori_loop(0, low_ref.shape[0], pack_step, 0)
    items = [[int_ref[1, v * 8 : v * 8 + 8, :] for v in range(8)]]
    for d in range(3):
        items.append([kick_ref[d, v * 8 : v * 8 + 8, :] for v in range(8)])
    items = sort_network(items)
    for d in range(3):
        out_ref[d] = laid_out(items[1 + d])


def plane_tables(trk_count, sub_count, unit_charge):
    doubled = 2 * NG
    width = doubled // sub_count
    slots = np.arange(4)[:, None, None] + 4 * np.arange(GROUPS)[None, None, :]
    slots = np.broadcast_to(slots, (4, sub_count, GROUPS))
    freq = width * np.arange(sub_count)[None, :, None] + slots
    used = (slots <= width // 2).astype(np.float64)
    share = used * np.where((slots == 0) | (slots == width // 2), 1.0, 2.0)
    cells = np.arange(NG)
    turn = 2.0 * np.pi / doubled
    angle = turn * ((freq.reshape(-1)[:, None] * cells[None, :]) % doubled)
    used = used.reshape(-1)[:, None]
    share_line = share.reshape(-1)[:, None]
    ty = np.concatenate([np.cos(angle) * used, -np.sin(angle) * used], axis=0) * unit_charge
    back = np.concatenate([np.cos(angle) * share_line, -np.sin(angle) * share_line], axis=0)
    ty_back = back.T / doubled
    pieces = back.reshape(2, 4 * sub_count, GROUPS, NG)
    pieces = np.concatenate([pieces, np.zeros((2, 4 * sub_count, 12 - GROUPS, NG))], axis=2)
    te_back = pieces.reshape(-1, NG).T / doubled
    angle = turn * ((cells[:, None] * np.arange(doubled)[None, :]) % doubled)
    tx = np.concatenate([np.cos(angle), np.sin(angle)], axis=0)
    tx_back = np.concatenate([np.cos(angle).T, np.sin(angle).T], axis=1) / doubled
    slabs = trk_count * sub_count
    angle = turn * ((np.arange(doubled)[:, None] * cells[None, :]) % doubled)
    cos, sin = np.cos(angle), np.sin(angle)
    wf = np.stack(
        [np.stack([cos, sin], axis=2), np.stack([-sin, cos], axis=2)], axis=0
    ).reshape(2 * doubled, 2 * NG)
    slab = np.arange(slabs)
    planes = (
        (slab // sub_count * QUAD * sub_count - 1 + PLANES * (slab % sub_count))[:, None]
        + np.arange(PLANES)[None, :]
    )
    inside = ((planes >= 0) & (planes < NG)).astype(np.float64)[:, :, None] / doubled
    angle = turn * ((planes[:, :, None] * np.arange(doubled)[None, None, :]) % doubled)
    cos, sin = np.cos(angle) * inside, np.sin(angle) * inside
    wb = np.stack([np.concatenate([cos, -sin], axis=2), np.concatenate([sin, cos], axis=2)], axis=2)
    wb = np.concatenate(
        [
            wb[:, :QUAD].reshape(slabs * QUAD * 2, 2 * doubled),
            wb[:, QUAD, 0],
            wb[:, QUAD, 1],
        ],
        axis=0,
    )
    pick = np.zeros((doubled, 2 * doubled))
    line = np.arange(doubled)
    pick[line, line] = 1.0
    pick[line, doubled + (-line) % doubled] = 1.0
    return ty, tx, wf, wb, tx_back, ty_back, te_back, pick


def run(body, shapes, scratch, *args, scalars=0):
    out_shape = tuple(jax.ShapeDtypeStruct(*shape) for shape in shapes)
    space = pl.BlockSpec(memory_space=pltpu.VMEM)
    result = pl.pallas_call(
        body,
        out_shape=out_shape,
        in_specs=[pl.BlockSpec(memory_space=pltpu.SMEM)] * scalars + [space] * (len(args) - scalars),
        out_specs=tuple(space for _ in out_shape),
        scratch_shapes=[pltpu.VMEM(*shape) for shape in scratch],
        compiler_params=pltpu.CompilerParams(vmem_limit_bytes=BIG),
    )(*args)
    return result


def spread_device(particle_cells, offsets, momenta, live_counts, green_hat, orders, strengths):
    f32 = jnp.float32
    trk_count = lax.axis_size("trk")
    sub_count = lax.axis_size("sub")
    slabs = trk_count * sub_count
    slab_depth = NG // trk_count
    count_here = particle_cells.shape[1]
    unit_charge = float(NG**3) / float(count_here * slabs)
    both = ("trk", "sub")
    tables = plane_tables(trk_count, sub_count, unit_charge)
    ty, tx, wf, wb, tx_back, ty_back, te_back = [table_halves(table) for table in tables[:7]]
    pick = jnp.asarray(tables[7].astype(ml_dtypes.bfloat16))

    def flat(t, s):
        return (t % trk_count) * sub_count + s % sub_count

    pairs = [(t, s) for t in range(trk_count) for s in range(sub_count)]
    width = green_hat.shape[2]
    lines = jnp.transpose(green_hat, (0, 2, 1))
    far = lax.ppermute(
        lines[:, width // 2 :, :],
        both,
        [(flat(t, s), flat(trk_count - 1 - t, sub_count - 1 - s)) for t, s in pairs],
    )
    far_row = lax.ppermute(
        lines[0, width // 2 :, :],
        both,
        [(flat(t, s), flat(trk_count - t, sub_count - 1 - s)) for t, s in pairs],
    )
    edge = lax.ppermute(
        lines[:, 0, :],
        both,
        [(flat(t, s), flat(trk_count - 1 - t, sub_count - s)) for t, s in pairs],
    )
    edge_row = lax.ppermute(
        lines[0:1, 0, :],
        both,
        [(flat(t, s), flat(trk_count - t, sub_count - s)) for t, s in pairs],
    )

    trk_id = lax.axis_index("trk")
    place = lax.axis_index("sub").reshape(1)
    local_z = particle_cells[2] - trk_id * slab_depth
    row_ids = jnp.arange(count_here, dtype=jnp.int32)
    live_z = jnp.where(row_ids < live_counts[0], local_z, -100)
    blank = jnp.zeros((2, count_here), f32)
    rows = jnp.concatenate(
        [
            particle_cells[0:2].astype(f32),
            live_z.astype(f32)[None],
            offsets,
            blank,
        ],
        axis=0,
    )
    shared = lax.all_gather(rows, "sub", axis=0, tiled=True)
    acc_shape = ((PLANES * NG, 2 * NG), f32)
    (start,) = run(deposit_own, [acc_shape], [], place, rows, scalars=1)
    (dens,) = run(
        deposit_rest, [((PLANES * NG, NG), f32)], [acc_shape], place, shared, start, scalars=1
    )
    rim = lax.ppermute(
        dens[QUAD * NG :],
        both,
        [(flat(t, sub_count - 1), flat(t + 1, 0)) for t in range(trk_count - 1)],
    )
    (sent,) = run(
        forward_planes,
        [((slabs, FWD_ROWS, NG), f32)],
        [((16 * FWD_ROWS, NG), f32)] * 2,
        dens,
        rim,
        *ty,
        *tx,
    )
    got = lax.all_to_all(sent, both, split_axis=0, concat_axis=0, tiled=True)

    cells_sq = jnp.concatenate([particle_cells[0:2], local_z[None]], axis=0).reshape(3, 64, NG)
    offs_sq = offsets.reshape(3, 64, NG)
    ints, offs = run(
        sort_particles,
        [((4, 64, NG), jnp.int32), ((3, 64, NG), f32)],
        [],
        cells_sq,
        offs_sq,
    )
    packed = ints[0].reshape(count_here // PACK, PACK)
    low, high = jnp.min(packed, axis=1), jnp.max(packed, axis=1)

    far = jnp.concatenate([far_row[None], jnp.flip(far[1:], axis=0)], axis=0)
    edge = jnp.concatenate([edge_row, jnp.flip(edge[1:], axis=0)], axis=0)
    (green,) = run(
        green_pairs,
        [((2 * NG, GROUPS * NG), f32)],
        [((2 * WIDE * WIDE, NG), f32)] * 2 + [((WIDE * WIDE, NG), f32)] * 2,
        lines.reshape(-1, 2 * NG),
        far.reshape(-1, 2 * NG),
        edge,
        pick,
    )
    (sent,) = run(
        spectrum_stage, [((slabs * BACK_ROWS, NG), f32)], [], got, green, *wf, *wb
    )
    got = lax.all_to_all(
        sent.reshape(slabs, BACK_ROWS, NG), both, split_axis=0, concat_axis=0, tiled=True
    )
    (pot,) = run(
        inverse_planes,
        [((PLANES, NG, NG), f32)],
        [((16 * FWD_ROWS, NG), f32)] * 2 + [((16 * (BACK_ROWS - FWD_ROWS), NG), f32)] * 2,
        got,
        *tx_back,
        *ty_back,
        *te_back,
    )
    pot = lax.all_gather(pot, "sub", axis=0, tiled=True)
    (kick,) = run(
        sample,
        [((3, 64, NG), f32)],
        [((3, slab_depth + 1, NG, NG), f32), ((3, 64, NG), f32)],
        low,
        high,
        pot,
        ints,
        offs,
        scalars=2,
    )
    kick = kick.reshape(3, count_here)
    push_x, push_y = multipole_push(particle_cells, offsets, orders, strengths)
    push = jnp.stack([push_x, push_y, jnp.zeros_like(push_x)])
    new_momenta = momenta + kick + push
    new_coords = particle_cells.astype(f32) + offsets + new_momenta
    return (new_coords, new_momenta)


def solution(mesh):
    in_specs = (
        P(None, ("trk", "sub")),
        P(None, ("trk", "sub")),
        P(None, ("trk", "sub")),
        P(("trk", "sub")),
        P("trk", None, "sub"),
        P(),
        P(),
    )
    out_specs = (P(None, ("trk", "sub")), P(None, ("trk", "sub")))
    trk_count, sub_count = mesh.shape["trk"], mesh.shape["sub"]
    fits = sub_count == 4 and trk_count * WIDE == 2 * NG
    body = spread_device if fits else per_device
    return jax.shard_map(
        body, mesh=mesh, in_specs=in_specs, out_specs=out_specs, check_vma=False
    )
```

```python
import math

import jax
import jax.numpy as jnp
import ml_dtypes
import numpy as np
from jax import lax
from jax.experimental import pallas as pl
from jax.experimental.pallas import tpu as pltpu
from jax.sharding import PartitionSpec as P

NG = 128


HIGHEST = lax.Precision.HIGHEST


def multipole_push(particle_cells, offsets, orders, strengths):
    centre = 0.5 * NG
    real_u = (particle_cells[0].astype(jnp.float32) + offsets[0] - centre) / centre
    imag_u = (particle_cells[1].astype(jnp.float32) + offsets[1] - centre) / centre
    power_re = real_u
    power_im = imag_u
    push_x = jnp.zeros_like(real_u)
    push_y = jnp.zeros_like(real_u)
    for degree in range(1, 5):
        coeff = jnp.sum(jnp.where(orders - 1 == degree, strengths, jnp.zeros_like(strengths)))
        push_x = push_x - coeff * power_re
        push_y = push_y + coeff * power_im
        power_re, power_im = (
            power_re * real_u - power_im * imag_u,
            power_re * imag_u + power_im * real_u,
        )
    return (push_x, push_y)


def wave_table(freq_ids, place_ids, length):
    phase_int = freq_ids[:, None] * place_ids[None, :] % length
    angle = 2.0 * math.pi / length * phase_int.astype(jnp.float32)
    return (jnp.cos(angle), jnp.sin(angle))


def tent_weights(cells, fraction, length):
    places = jnp.arange(length, dtype=jnp.int32)
    lower = jnp.where(places[None, :] == cells[:, None], (1.0 - fraction)[:, None], 0.0)
    upper = jnp.where(places[None, :] == cells[:, None] + 1, fraction[:, None], 0.0)
    return lower + upper


def block_weights(cells_x, cells_y, cells_z, frac_x, frac_y, frac_z, depth):
    weight_x = tent_weights(cells_x, frac_x, NG)
    weight_y = tent_weights(cells_y, frac_y, NG)
    weight_z = tent_weights(cells_z, frac_z, depth)
    plane_xz = (weight_x[:, :, None] * weight_z[:, None, :]).reshape(cells_x.shape[0], -1)
    return (plane_xz, weight_y)


def per_device(particle_cells, offsets, momenta, live_counts, green_hat, orders, strengths):
    trk_count = lax.axis_size("trk")
    sub_count = lax.axis_size("sub")
    slab_depth = NG // trk_count
    depth = slab_depth + 1
    doubled = 2 * NG
    count_here = particle_cells.shape[1]
    count_all = count_here * trk_count * sub_count
    row_ids = jnp.arange(count_here, dtype=jnp.int32)
    unit_charge = float(NG**3) / float(count_all)
    charge = jnp.where(
        row_ids < live_counts[0],
        jnp.full((count_here,), unit_charge, jnp.float32),
        jnp.zeros((count_here,), jnp.float32),
    )
    local_z = particle_cells[2] - lax.axis_index("trk") * slab_depth
    block_len = math.gcd(count_here, 512)
    block_count = count_here // block_len
    blocked_x = particle_cells[0].reshape(block_count, block_len)
    blocked_y = particle_cells[1].reshape(block_count, block_len)
    blocked_z = local_z.reshape(block_count, block_len)
    blocked_off = offsets.reshape(3, block_count, block_len).transpose(1, 0, 2)
    blocked_charge = charge.reshape(block_count, block_len)

    def deposit_step(total, items):
        bx, by, bz, boff, bcharge = items
        plane_xz, weight_y = block_weights(bx, by, bz, boff[0], boff[1], boff[2], depth)
        charged = plane_xz * bcharge[:, None]
        return (total + jnp.einsum("pa,py->ay", charged, weight_y, precision=HIGHEST), None)

    start_total = jnp.zeros((NG * depth, NG), jnp.float32)
    deposit, _ = lax.scan(
        deposit_step, start_total, (blocked_x, blocked_y, blocked_z, blocked_off, blocked_charge)
    )
    deposit = deposit.reshape(NG, depth, NG)
    density = lax.psum_scatter(deposit, "sub", scatter_dimension=0, tiled=True)
    freq_all = jnp.arange(doubled, dtype=jnp.int32)
    cell_ids = jnp.arange(NG, dtype=jnp.int32)
    cos_cells, sin_cells = wave_table(freq_all, cell_ids, doubled)
    spec_re = jnp.einsum("xzy,ky->xzk", density, cos_cells, precision=HIGHEST)
    spec_im = -jnp.einsum("xzy,ky->xzk", density, sin_cells, precision=HIGHEST)
    part_re = lax.all_to_all(spec_re, "sub", split_axis=2, concat_axis=0, tiled=True)
    part_im = lax.all_to_all(spec_im, "sub", split_axis=2, concat_axis=0, tiled=True)
    out_re = jnp.einsum("kn,nzq->kzq", cos_cells, part_re, precision=HIGHEST) + jnp.einsum(
        "kn,nzq->kzq", sin_cells, part_im, precision=HIGHEST
    )
    out_im = jnp.einsum("kn,nzq->kzq", cos_cells, part_im, precision=HIGHEST) - jnp.einsum(
        "kn,nzq->kzq", sin_cells, part_re, precision=HIGHEST
    )
    xspec_re = out_re
    xspec_im = out_im
    slab_starts = jnp.arange(trk_count, dtype=jnp.int32)[:, None] * slab_depth
    forward_places = (slab_starts + jnp.arange(slab_depth + 1, dtype=jnp.int32)[None, :]).reshape(
        -1
    )
    cos_fwd, sin_fwd = wave_table(freq_all, forward_places, doubled)
    part_re = lax.all_to_all(xspec_re, "trk", split_axis=0, concat_axis=1, tiled=True)
    part_im = lax.all_to_all(xspec_im, "trk", split_axis=0, concat_axis=1, tiled=True)
    out_re = jnp.einsum("kn,xnq->xkq", cos_fwd, part_re, precision=HIGHEST) + jnp.einsum(
        "kn,xnq->xkq", sin_fwd, part_im, precision=HIGHEST
    )
    out_im = jnp.einsum("kn,xnq->xkq", cos_fwd, part_im, precision=HIGHEST) - jnp.einsum(
        "kn,xnq->xkq", sin_fwd, part_re, precision=HIGHEST
    )
    zspec_re = out_re
    zspec_im = out_im
    scaled_re = zspec_re * green_hat
    scaled_im = zspec_im * green_hat
    back_places = (slab_starts - 1 + jnp.arange(slab_depth + 3, dtype=jnp.int32)[None, :]).reshape(
        -1
    )
    inside = ((back_places >= 0) & (back_places < NG)).astype(jnp.float32) / doubled
    cos_back, sin_back = wave_table(back_places, freq_all, doubled)
    cos_back = cos_back * inside[:, None]
    sin_back = sin_back * inside[:, None]
    plane_re = jnp.einsum("nk,xkq->xnq", cos_back, scaled_re, precision=HIGHEST) - jnp.einsum(
        "nk,xkq->xnq", sin_back, scaled_im, precision=HIGHEST
    )
    plane_im = jnp.einsum("nk,xkq->xnq", sin_back, scaled_re, precision=HIGHEST) + jnp.einsum(
        "nk,xkq->xnq", cos_back, scaled_im, precision=HIGHEST
    )
    cos_inverse = jnp.transpose(cos_cells) / doubled
    sin_inverse = jnp.transpose(sin_cells) / doubled
    part_re = lax.all_to_all(plane_re, "trk", split_axis=1, concat_axis=0, tiled=True)
    part_im = lax.all_to_all(plane_im, "trk", split_axis=1, concat_axis=0, tiled=True)
    out_re = jnp.einsum("nk,kzq->nzq", cos_inverse, part_re, precision=HIGHEST) - jnp.einsum(
        "nk,kzq->nzq", sin_inverse, part_im, precision=HIGHEST
    )
    out_im = jnp.einsum("nk,kzq->nzq", sin_inverse, part_re, precision=HIGHEST) + jnp.einsum(
        "nk,kzq->nzq", cos_inverse, part_im, precision=HIGHEST
    )
    cos_final = cos_cells / doubled
    sin_final = sin_cells / doubled
    part_re = lax.all_to_all(out_re, "sub", split_axis=0, concat_axis=2, tiled=True)
    part_im = lax.all_to_all(out_im, "sub", split_axis=0, concat_axis=2, tiled=True)
    block_rows = jnp.einsum("xzk,ky->xzy", part_re, cos_final, precision=HIGHEST) - jnp.einsum(
        "xzk,ky->xzy", part_im, sin_final, precision=HIGHEST
    )
    potential = lax.all_gather(block_rows, "sub", axis=0, tiled=True)
    middle = potential[:, 1 : slab_depth + 2]
    around_x = jnp.pad(middle, ((1, 1), (0, 0), (0, 0)))
    field_x = -0.5 * (around_x[2:] - around_x[:-2])
    around_y = jnp.pad(middle, ((0, 0), (0, 0), (1, 1)))
    field_y = -0.5 * (around_y[:, :, 2:] - around_y[:, :, :-2])
    field_z = -0.5 * (potential[:, 2 : slab_depth + 3] - potential[:, : slab_depth + 1])
    field_table = jnp.stack([field_x, field_y, field_z], axis=2).reshape(NG * depth, 3 * NG)

    def sample_step(carry, items):
        bx, by, bz, boff = items
        plane_xz, weight_y = block_weights(bx, by, bz, boff[0], boff[1], boff[2], depth)
        lines = jnp.dot(plane_xz, field_table, precision=HIGHEST).reshape(bx.shape[0], 3, NG)
        return (carry, jnp.sum(lines * weight_y[:, None, :], axis=2))

    _, sampled = lax.scan(
        sample_step, jnp.zeros((), jnp.float32), (blocked_x, blocked_y, blocked_z, blocked_off)
    )
    kick = sampled.reshape(count_here, 3).transpose(1, 0)
    push_x, push_y = multipole_push(particle_cells, offsets, orders, strengths)
    push = jnp.stack([push_x, push_y, jnp.zeros_like(push_x)])
    new_momenta = momenta + kick + push
    new_coords = particle_cells.astype(jnp.float32) + offsets + new_momenta
    return (new_coords, new_momenta)


def halves(values):
    upper = values.astype(jnp.bfloat16)
    return (upper, (values - upper.astype(jnp.float32)).astype(jnp.bfloat16))


def table_halves(table):
    upper = table.astype(ml_dtypes.bfloat16)
    lower = (table - upper.astype(np.float64)).astype(ml_dtypes.bfloat16)
    return (jnp.asarray(upper), jnp.asarray(lower))


def mm(left, right):
    return jnp.dot(left, right, preferred_element_type=jnp.float32)


def mm_t(left, right):
    return lax.dot_general(left, right, (((1,), (1,)), ((), ())), preferred_element_type=jnp.float32)


def mm3(left, right):
    return mm(left[0], right[0]) + (mm(left[0], right[1]) + mm(left[1], right[0]))


def turn_blocks(parts):
    lanes = lax.broadcasted_iota(jnp.int32, parts[0].shape, 1)
    low = lanes < 64
    even = (lanes // 32) % 2 == 0
    pairs = []
    for first, second in ((parts[0], parts[2]), (parts[1], parts[3])):
        pairs.append(
            (
                jnp.where(low, first, pltpu.roll(second, 64, 1)),
                jnp.where(low, pltpu.roll(first, 64, 1), second),
            )
        )
    result = []
    for half in (0, 1):
        first, second = pairs[0][half], pairs[1][half]
        result.append(jnp.where(even, first, pltpu.roll(second, 32, 1)))
        result.append(jnp.where(even, pltpu.roll(first, 96, 1), second))
    return result


def tent(places, cells, fraction):
    away = places - cells
    return jnp.where(away == 0, 1.0 - fraction, jnp.where(away == 1, fraction, 0.0))


QUAD = 4
PLANES = 5
WIDE = 32
GROUPS = 9
SLOTS = 4 * GROUPS
FWD_ROWS = GROUPS * 2 * QUAD
BACK_ROWS = FWD_ROWS + 24
LOT = 512
SORT_ROWS = 392
LIST_ROWS = SORT_ROWS + NG
SPAN = 3
PACK = 256
BIG = 56 * 1024 * 1024


def long_row(ref, start, count):
    return jnp.concatenate([ref[pl.ds(start + n, 1), :] for n in range(count)], axis=1)


def deposit_lots(acc_ref, rows_ref, base, ends_ref, me, bottom, top):
    span = LOT // NG
    ids = lax.broadcasted_iota(jnp.int32, (NG, LOT), 0).astype(jnp.float32)

    def step(lot, carry):
        low = ends_ref[0, lot * span].astype(jnp.int32) - me * QUAD
        high = ends_ref[1, lot * span + span - 1].astype(jnp.int32) + 1 - me * QUAD
        low = jnp.maximum(low, bottom)
        high = jnp.minimum(high, top)
        size = min(SPAN, top - bottom + 1)

        @pl.when(low <= high)
        def _():
            cell_x, cell_y, cell_z, off_x, off_y, off_z = [
                long_row(rows_ref, base + which * 64 + lot * span, span) for which in range(6)
            ]
            right = jnp.concatenate(halves(tent(ids, cell_x, off_x)), axis=0)
            weight_y = tent(ids, cell_y, off_y)

            def window(turn, inner):
                start = low + turn * size
                away = (start + me * QUAD).astype(jnp.float32) - cell_z
                left = []
                for z in range(size):
                    left.extend(halves(weight_y * tent(away + float(z), 0.0, off_z)))
                lines = mm_t(jnp.concatenate(left, axis=0), right)
                for z in range(size):
                    place = pl.ds(pl.multiple_of((start + z - bottom) * NG, NG), NG)
                    part = lines[2 * z * NG : (2 * z + 2) * NG]
                    acc_ref[place, :] += part[0:NG] + part[NG : 2 * NG]
                return inner

            lax.fori_loop(0, (high - low) // size + 1, window, 0)

        return carry

    lax.fori_loop(0, 64 // span, step, 0)


ACC_PLANES = QUAD + SPAN - 1
ENDS = slice(6 * 64, 6 * 64 + 8)


def deposit_own(place_ref, rows_ref, acc_ref, ends_ref, sem):
    ends = pltpu.make_async_copy(rows_ref.at[ENDS, :], ends_ref, sem)
    ends.start()
    acc_ref[...] = jnp.zeros_like(acc_ref)
    ends.wait()
    deposit_lots(acc_ref, rows_ref, 0, ends_ref, place_ref[0], 0, QUAD - 1)


def fetch_ends(rows_ref, ends_ref, sem):
    copies = [
        pltpu.make_async_copy(
            rows_ref.at[n * LIST_ROWS + ENDS.start : n * LIST_ROWS + ENDS.stop, :],
            ends_ref.at[n],
            sem.at[n],
        )
        for n in range(4)
    ]
    for copy in copies:
        copy.start()
    return copies


def deposit_rest(place_ref, rows_ref, start_ref, dens_ref, acc_ref, ends_ref, sem):
    copies = fetch_ends(rows_ref, ends_ref, sem)
    acc_ref[...] = start_ref[...]
    for copy in copies:
        copy.wait()
    me = place_ref[0]

    def each(turn, carry):
        n = lax.rem(me + turn, 4)
        deposit_lots(acc_ref, rows_ref, n * LIST_ROWS, ends_ref.at[n], me, 0, QUAD - 1)
        return carry

    lax.fori_loop(1, 4, each, 0)
    live = slice(0, QUAD * NG)
    dens_ref[...] = acc_ref[live, 0:NG] + acc_ref[live, NG : 2 * NG]


def forward_planes(lower_ref, dens_ref, list_ref, ty_hi, ty_lo, tx_hi, tx_lo, out_ref, left_ref, right_ref):
    half = 16 * GROUPS
    for z in range(QUAD):
        plane = dens_ref[z * NG : (z + 1) * NG, :]
        if z == 0:
            rims = [
                list_ref[n * LIST_ROWS + SORT_ROWS : (n + 1) * LIST_ROWS, :] for n in range(4)
            ]
            rim = (rims[0] + rims[1]) + (rims[2] + rims[3])
            plane = plane + jnp.where(lower_ref[0] > 0, rim, 0.0)
        lines = mm3((ty_hi[...], ty_lo[...]), halves(plane))
        real, imag = lines[0:half], lines[half : 2 * half]
        left_ref[pl.ds(2 * z, half, stride=8), :] = real
        right_ref[pl.ds(2 * z, half, stride=8), :] = imag
        left_ref[pl.ds(2 * z + 1, half, stride=8), :] = imag
        right_ref[pl.ds(2 * z + 1, half, stride=8), :] = -real
    for s in range(4):
        whole = []
        for i in range(4):
            start = (i * 4 + s) * FWD_ROWS
            piece = slice(start, start + FWD_ROWS)
            lines = jnp.concatenate([left_ref[piece, :], right_ref[piece, :]], axis=1)
            whole.append(mm3(halves(lines), (tx_hi[...], tx_lo[...])))
        for th in range(2):
            turned = turn_blocks([part[:, th * NG : (th + 1) * NG] for part in whole])
            for t in range(4):
                out_ref[(th * 4 + t) * 4 + s] = turned[t]


def green_send(lines_ref, far_ref, row_ref, edge_ref, last_ref):
    for k in range(1, WIDE):
        far_ref[k] = lines_ref[WIDE - k, WIDE : 2 * WIDE, :]
        edge_ref[k : k + 1, :] = lines_ref[WIDE - k, 0:1, :]
    far_ref[0] = lines_ref[0, WIDE : 2 * WIDE, :]
    edge_ref[0:1, :] = lines_ref[0, 0:1, :]
    row_ref[...] = lines_ref[0, WIDE : 2 * WIDE, :]
    last_ref[...] = lines_ref[0, 0:8, :]


def green_pairs(own_ref, far_ref, row_ref, edge_ref, last_ref, pick_ref, out_ref, *parts):
    for side in range(2):
        lanes = slice(side * NG, (side + 1) * NG)
        parts[side][...] = own_ref[:, lanes]
        parts[2 + side][WIDE : WIDE * WIDE, :] = far_ref[WIDE : WIDE * WIDE, lanes]
        parts[2 + side][0:WIDE, :] = row_ref[:, lanes]
    first = lax.broadcasted_iota(jnp.int32, (WIDE, 2 * NG), 0) == 0
    edge = jnp.where(first, jnp.broadcast_to(last_ref[0:1, :], (WIDE, 2 * NG)), edge_ref[...])

    def pull(refs, start, stride):
        return jnp.concatenate(
            [ref[pl.ds(start, WIDE, stride=stride), :] for ref in refs], axis=1
        )

    for group in range(GROUPS):
        near, away = [], []
        for i in range(4):
            j = group * 4 + i
            if j > WIDE:
                near.append(jnp.zeros((WIDE, 2 * NG), jnp.float32))
                away.append(jnp.zeros((WIDE, 2 * NG), jnp.float32))
                continue
            near.append(pull(parts[0:2], j, 2 * WIDE))
            away.append(edge if j == 0 else pull(parts[2:4], WIDE - j, WIDE))
        both = jnp.concatenate(
            [jnp.concatenate(near, axis=0), jnp.concatenate(away, axis=0)], axis=1
        )
        high = both.astype(jnp.bfloat16)
        left = both - high.astype(jnp.float32)
        mid = left.astype(jnp.bfloat16)
        low = (left - mid.astype(jnp.float32)).astype(jnp.bfloat16)
        pick = pick_ref[...]
        out_ref[:, group * NG : (group + 1) * NG] = 0.5 * (
            mm_t(pick, high) + (mm_t(pick, mid) + mm_t(pick, low))
        )


def spectrum_stage(in_ref, green_ref, wf_hi, wf_lo, wb_hi, wb_lo, out_ref):
    slabs = in_ref.shape[0]
    half = 2 * NG
    for first in range(0, GROUPS, 2):
        groups = [g for g in (first, first + 1) if g < GROUPS]
        data = [in_ref[:, g * 8 : (g + 1) * 8, :].reshape(slabs * 8, NG) for g in groups]
        data = data[0] if len(data) == 1 else jnp.concatenate(data, axis=1)
        spec = mm3((wf_hi[...], wf_lo[...]), halves(data))
        green = green_ref[:, first * NG : (first + len(groups)) * NG]
        scaled = jnp.concatenate([spec[0:half] * green, spec[half : 2 * half] * green], axis=0)
        back = mm3((wb_hi[...], wb_lo[...]), halves(scaled))
        for place, g in enumerate(groups):
            part = back[:, place * NG : (place + 1) * NG]
            for slab in range(slabs):
                row = slab * BACK_ROWS + g * 8
                out_ref[row : row + 8, :] = part[slab * 8 : slab * 8 + 8]
            for c in range(2):
                start = slabs * (8 + c)
                out_ref[pl.ds(FWD_ROWS + 2 * g + c, slabs, stride=BACK_ROWS), :] = part[
                    start : start + slabs
                ]
    for row in range(FWD_ROWS + 2 * GROUPS, BACK_ROWS):
        out_ref[pl.ds(row, slabs, stride=BACK_ROWS), :] = jnp.zeros((slabs, NG), jnp.float32)


def inverse_planes(
    in_ref, tx_hi, tx_lo, ty_hi, ty_lo, te_hi, te_lo, out_ref, mid_cos, mid_sin, top_cos, top_sin
):
    extra = BACK_ROWS - FWD_ROWS
    for s in range(4):
        main, rest = [[], [], [], []], [[], [], [], []]
        for th in range(2):
            parts = [in_ref[(th * 4 + t) * 4 + s, 0:FWD_ROWS, :] for t in range(4)]
            tops = [in_ref[(th * 4 + t) * 4 + s, FWD_ROWS:BACK_ROWS, :] for t in range(4)]
            for i, block in enumerate(turn_blocks(parts)):
                main[i].append(block)
            for i, block in enumerate(turn_blocks(tops)):
                rest[i].append(block)
        for i in range(4):
            row = (i * 4 + s) * FWD_ROWS
            lines = jnp.concatenate(main[i], axis=1)
            lines = mm3(halves(lines), (tx_hi[...], tx_lo[...]))
            mid_cos[row : row + FWD_ROWS, :] = lines[:, 0:NG]
            mid_sin[row : row + FWD_ROWS, :] = lines[:, NG : 2 * NG]
            row = (i * 4 + s) * extra
            lines = jnp.concatenate(rest[i], axis=1)
            lines = mm3(halves(lines), (tx_hi[...], tx_lo[...]))
            top_cos[row : row + extra, :] = lines[:, 0:NG]
            top_sin[row : row + extra, :] = lines[:, NG : 2 * NG]

    def finish(cos_ref, sin_ref, start, count, stride, table):
        real, imag = pl.ds(start, count, stride=stride), pl.ds(start + 1, count, stride=stride)
        lines = jnp.concatenate(
            [cos_ref[real, :] - sin_ref[imag, :], sin_ref[real, :] + cos_ref[imag, :]], axis=0
        )
        return mm3((table[0][...], table[1][...]), halves(lines))

    for z in range(QUAD):
        out_ref[z] = finish(mid_cos, mid_sin, 2 * z, 16 * GROUPS, 8, (ty_hi, ty_lo))
    out_ref[QUAD] = finish(top_cos, top_sin, 0, 8 * extra, 2, (te_hi, te_lo))


SORT_BITS = 13
DEAD = 100


def sort_network(items, rolled=False):
    shape = (8, NG)
    lanes = lax.broadcasted_iota(jnp.int32, shape, 1)
    subs = lax.broadcasted_iota(jnp.int32, shape, 0)
    base = subs * 8 + (lanes // 64) * 64 + (lanes % 64) * 128

    def exchange(items, others, bit, size):
        fresh = [[] for _ in items]
        for v in range(8):
            rank = base + v
            keep = (((rank >> bit) ^ (rank >> (size + 1))) & 1) == 0
            take = (others[0][v] < items[0][v]) == keep
            for n in range(len(items)):
                fresh[n].append(jnp.where(take, others[n][v], items[n][v]))
        return fresh

    def near_stage(items, bit, size):
        others = [[item[v ^ (1 << bit)] for v in range(8)] for item in items]
        return exchange(items, others, bit, size)

    def far_stage(items, bit, size, index, axis):
        others = [[jnp.take_along_axis(value, index, axis=axis) for value in item] for item in items]
        return exchange(items, others, bit, size)

    def far_bit(items, bit, size):
        if bit < 3:
            return near_stage(items, bit, size)
        if bit < 6:
            return far_stage(items, bit, size, subs ^ (1 << (bit - 3)), 0)
        return far_stage(items, bit, size, lanes ^ (64 if bit == 6 else 1 << (bit - 7)), 1)

    for size in range(3 if rolled else SORT_BITS):
        for bit in range(size, -1, -1):
            items = far_bit(items, bit, size)
    if not rolled:
        return items

    def merge(size, items):
        def lane_step(n, items):
            bit = size - n
            index = lanes ^ jnp.where(bit == 6, 64, 1 << jnp.maximum(bit - 7, 0))
            return far_stage(items, bit, size, index, 1)

        def sub_step(n, items):
            bit = jnp.minimum(size, 5) - n
            return far_stage(items, bit, size, subs ^ (1 << (bit - 3)), 0)

        items = lax.fori_loop(0, jnp.maximum(size - 5, 0), lane_step, items)
        items = lax.fori_loop(0, jnp.minimum(size, 5) - 2, sub_step, items)
        for bit in (2, 1, 0):
            items = near_stage(items, bit, size)
        return items

    return lax.fori_loop(3, SORT_BITS, merge, items)


def laid_out(values):
    turned = jnp.transpose(jnp.concatenate(values, axis=0), (1, 0))
    return jnp.concatenate([turned[0:64], turned[64:128]], axis=1)


def sort_labels(v):
    lanes = lax.broadcasted_iota(jnp.int32, (8, NG), 1)
    subs = lax.broadcasted_iota(jnp.int32, (8, NG), 0)
    return (subs + v * 8) * 128 + (lanes // 64) * 64 + (lanes % 8) * 8 + (lanes // 8) % 8


def square_up(cells_ref, offs_ref, ints_ref, flts_ref):
    for k in range(64):
        lanes = slice(k * NG, (k + 1) * NG)
        for d in range(3):
            ints_ref[d, k : k + 1, :] = cells_ref[d : d + 1, lanes]
            flts_ref[d, k : k + 1, :] = offs_ref[d : d + 1, lanes]


def sort_by_z(
    place_ref,
    live_ref,
    cells_ref,
    offs_ref,
    out_ref,
    rim_ref,
    ints_ref,
    flts_ref,
    top_ref,
    ends_ref,
    sem,
):
    square_up(cells_ref, offs_ref, ints_ref, flts_ref)
    lanes = lax.broadcasted_iota(jnp.int32, (8, NG), 1)
    subs = lax.broadcasted_iota(jnp.int32, (8, NG), 0)
    keys, packs, offs = [], [], [[], [], []]
    for v in range(8):
        rows = slice(v * 8, v * 8 + 8)
        alive = (subs + v * 8) * NG + lanes < live_ref[0]
        cell_z = jnp.where(alive, ints_ref[2, rows, :] - place_ref[0], DEAD)
        keys.append(cell_z * 8192 + sort_labels(v))
        packs.append(ints_ref[0, rows, :] * NG + ints_ref[1, rows, :])
        for d in range(3):
            offs[d].append(flts_ref[d, rows, :])
    items = [laid_out(item) for item in sort_network([keys, packs] + offs)]
    cell_z = (items[0] >> 13).astype(jnp.float32)
    out_ref[0:64, :] = (items[1] >> 7).astype(jnp.float32)
    out_ref[64:128, :] = (items[1] & (NG - 1)).astype(jnp.float32)
    out_ref[128:192, :] = cell_z
    for d in range(3):
        out_ref[192 + 64 * d : 256 + 64 * d, :] = items[2 + d]
    ends = jnp.transpose(cell_z, (1, 0))
    ends = jnp.concatenate([ends[0:1], ends[NG - 1 : NG], jnp.zeros((6, 64), jnp.float32)], axis=0)
    out_ref[384:392, :] = jnp.concatenate([ends, ends], axis=1)
    fetch = pltpu.make_async_copy(out_ref.at[ENDS, :], ends_ref, sem)
    fetch.start()
    top_ref[...] = jnp.zeros_like(top_ref)
    fetch.wait()
    deposit_lots(top_ref, out_ref, 0, ends_ref, 0, 4 * QUAD, 4 * QUAD)
    rim_ref[...] = top_ref[:, 0:NG] + top_ref[:, NG : 2 * NG]


def sort_by_y(place_ref, cells_ref, offs_ref, out_int, out_off, ints_ref, flts_ref):
    square_up(cells_ref, offs_ref, ints_ref, flts_ref)
    keys, packs, offs = [], [], [[], [], []]
    for v in range(8):
        rows = slice(v * 8, v * 8 + 8)
        keys.append(ints_ref[1, rows, :] * 8192 + sort_labels(v))
        packs.append(ints_ref[0, rows, :] * 64 + ints_ref[2, rows, :] - place_ref[0])
        for d in range(3):
            offs[d].append(flts_ref[d, rows, :])
    items = [laid_out(item) for item in sort_network([keys, packs] + offs, rolled=True)]
    cell_y = items[0] >> 13
    out_int[0:64, :] = cell_y
    out_int[64:128, :] = items[0] & 8191
    out_int[128:192, :] = items[1] >> 6
    out_int[192:256, :] = items[1] & 63
    for d in range(3):
        out_off[d * 64 : d * 64 + 64, :] = items[2 + d]
    ends = jnp.transpose(cell_y, (1, 0))
    ends = jnp.concatenate([ends[0:1], ends[NG - 1 : NG], jnp.zeros((6, 64), jnp.int32)], axis=0)
    out_int[256:264, :] = jnp.concatenate([ends, ends], axis=1)


def sample(
    place_ref,
    own_ref,
    core_ref,
    chip_ref,
    last_ref,
    int_ref,
    off_ref,
    out_ref,
    pot_ref,
    field_ref,
    kick_ref,
    ends_ref,
    sem,
):
    ends = pltpu.make_async_copy(int_ref.at[256:264, :], ends_ref, sem)
    ends.start()
    me = place_ref[0]
    for turn, ref in enumerate((own_ref, core_ref, chip_ref, last_ref)):
        pot_ref[pl.ds((me ^ turn) * PLANES, PLANES)] = ref[...]
    depth = field_ref.shape[0] // 3
    rows = lax.broadcasted_iota(jnp.int32, (NG, NG), 0)
    lanes = lax.broadcasted_iota(jnp.int32, (NG, NG), 1)
    blank = jnp.zeros((8, NG), jnp.float32)

    def fields(z, carry):
        plane = pot_ref[z + 1]
        right = jnp.where(lanes == NG - 1, 0.0, pltpu.roll(plane, NG - 1, 1))
        left = jnp.where(lanes == 0, 0.0, pltpu.roll(plane, 1, 1))
        field_ref[z, 0:NG, :] = -0.5 * (right - left)
        right = jnp.where(rows == NG - 1, 0.0, pltpu.roll(plane, NG - 1, 0))
        left = jnp.where(rows == 0, 0.0, pltpu.roll(plane, 1, 0))
        field_ref[depth + z, 0:NG, :] = -0.5 * (right - left)
        field_ref[2 * depth + z, 0:NG, :] = -0.5 * (pot_ref[z + 2] - pot_ref[z])
        for d in range(3):
            field_ref[d * depth + z, NG : NG + 8, :] = blank
        return carry

    lax.fori_loop(0, depth, fields, 0)
    x_ids = lax.broadcasted_iota(jnp.int32, (NG, PACK), 0)
    z_ids = lax.broadcasted_iota(jnp.int32, (24, PACK), 0)
    y_ids = lax.broadcasted_iota(jnp.int32, (8, PACK), 0)
    span = PACK // NG
    ends.wait()

    def pack_step(pack, carry):
        first = pack * span
        cell_y, cell_x, cell_z = [
            long_row(int_ref, which * 64 + first, span) for which in (0, 2, 3)
        ]
        off_x, off_y, off_z = [long_row(off_ref, which * 64 + first, span) for which in range(3)]
        weight_x = halves(tent(x_ids, cell_x, off_x))
        tall = [jnp.concatenate([part, part], axis=0) for part in weight_x]
        weight_z = tent(z_ids, cell_z, off_z)
        low = ends_ref[0, first]
        high = ends_ref[1, first + span - 1] + 1

        def chunk_step(chunk, kicks):
            start = low + chunk * 8
            weight_y = tent(y_ids + start, cell_y, off_y)
            table = field_ref[:, pl.ds(start, 8), :].reshape(3 * depth * 8, NG)
            part = jnp.concatenate(halves(table), axis=1)
            lines = mm(part, tall[0]) + mm(part, tall[1])
            fresh = []
            for d in range(3):
                total = lines[d * depth * 8 : d * depth * 8 + 8] * weight_z[0:1]
                for z in range(1, depth):
                    row = (d * depth + z) * 8
                    total = total + lines[row : row + 8] * weight_z[z : z + 1]
                fresh.append(kicks[d] + jnp.sum(total * weight_y, axis=0, keepdims=True))
            return tuple(fresh)

        zero = jnp.zeros((1, PACK), jnp.float32)
        kicks = lax.fori_loop(0, (high - low) // 8 + 1, chunk_step, (zero, zero, zero))
        for d in range(3):
            for n in range(span):
                kick_ref[d, pl.ds(first + n, 1), :] = kicks[d][:, n * NG : (n + 1) * NG]
        return carry

    lax.fori_loop(0, 64 // span, pack_step, 0)
    items = [[int_ref[64 + v * 8 : v * 8 + 72, :] for v in range(8)]]
    for d in range(3):
        items.append([kick_ref[d, v * 8 : v * 8 + 8, :] for v in range(8)])
    items = sort_network(items)
    for d in range(3):
        kick = laid_out(items[1 + d])
        for k in range(64):
            out_ref[d : d + 1, k * NG : (k + 1) * NG] = kick[k : k + 1, :]


def plane_tables(trk_count, sub_count, unit_charge):
    doubled = 2 * NG
    width = doubled // sub_count
    slots = np.arange(4)[:, None, None] + 4 * np.arange(GROUPS)[None, None, :]
    slots = np.broadcast_to(slots, (4, sub_count, GROUPS))
    freq = width * np.arange(sub_count)[None, :, None] + slots
    used = (slots <= width // 2).astype(np.float64)
    share = used * np.where((slots == 0) | (slots == width // 2), 1.0, 2.0)
    cells = np.arange(NG)
    turn = 2.0 * np.pi / doubled
    angle = turn * ((freq.reshape(-1)[:, None] * cells[None, :]) % doubled)
    used = used.reshape(-1)[:, None]
    share_line = share.reshape(-1)[:, None]
    ty = np.concatenate([np.cos(angle) * used, -np.sin(angle) * used], axis=0) * unit_charge
    back = np.concatenate([np.cos(angle) * share_line, -np.sin(angle) * share_line], axis=0)
    ty_back = back.T / doubled
    pieces = back.reshape(2, 4 * sub_count, GROUPS, NG)
    pieces = np.concatenate([pieces, np.zeros((2, 4 * sub_count, 12 - GROUPS, NG))], axis=2)
    te_back = pieces.reshape(-1, NG).T / doubled
    angle = turn * ((cells[:, None] * np.arange(doubled)[None, :]) % doubled)
    tx = np.concatenate([np.cos(angle), np.sin(angle)], axis=0)
    tx_back = np.concatenate([np.cos(angle).T, np.sin(angle).T], axis=1) / doubled
    slabs = trk_count * sub_count
    angle = turn * ((np.arange(doubled)[:, None] * cells[None, :]) % doubled)
    cos, sin = np.cos(angle), np.sin(angle)
    wf = np.stack(
        [np.stack([cos, sin], axis=2), np.stack([-sin, cos], axis=2)], axis=0
    ).reshape(2 * doubled, 2 * NG)
    slab = np.arange(slabs)
    planes = (
        (slab // sub_count * QUAD * sub_count - 1 + PLANES * (slab % sub_count))[:, None]
        + np.arange(PLANES)[None, :]
    )
    inside = ((planes >= 0) & (planes < NG)).astype(np.float64)[:, :, None] / doubled
    angle = turn * ((planes[:, :, None] * np.arange(doubled)[None, None, :]) % doubled)
    cos, sin = np.cos(angle) * inside, np.sin(angle) * inside
    wb = np.stack([np.concatenate([cos, -sin], axis=2), np.concatenate([sin, cos], axis=2)], axis=2)
    wb = np.concatenate(
        [
            wb[:, :QUAD].reshape(slabs * QUAD * 2, 2 * doubled),
            wb[:, QUAD, 0],
            wb[:, QUAD, 1],
        ],
        axis=0,
    )
    pick = np.zeros((doubled, 2 * doubled))
    line = np.arange(doubled)
    pick[line, line] = 1.0
    pick[line, doubled + (-line) % doubled] = 1.0
    return ty, tx, wf, wb, tx_back, ty_back, te_back, pick


def run(body, shapes, scratch, *args, scalars=0):
    out_shape = tuple(jax.ShapeDtypeStruct(*shape) for shape in shapes)
    space = pl.BlockSpec(memory_space=pltpu.VMEM)
    result = pl.pallas_call(
        body,
        out_shape=out_shape,
        in_specs=[pl.BlockSpec(memory_space=pltpu.SMEM)] * scalars + [space] * (len(args) - scalars),
        out_specs=tuple(space for _ in out_shape),
        scratch_shapes=[
            pltpu.VMEM(*shape) if isinstance(shape, tuple) else shape for shape in scratch
        ],
        compiler_params=pltpu.CompilerParams(vmem_limit_bytes=BIG),
    )(*args)
    return result


def spread_device(particle_cells, offsets, momenta, live_counts, green_hat, orders, strengths):
    f32 = jnp.float32
    trk_count = lax.axis_size("trk")
    sub_count = lax.axis_size("sub")
    slabs = trk_count * sub_count
    slab_depth = NG // trk_count
    count_here = particle_cells.shape[1]
    unit_charge = float(NG**3) / float(count_here * slabs)
    both = ("trk", "sub")
    tables = plane_tables(trk_count, sub_count, unit_charge)
    ty, tx, wf, wb, tx_back, ty_back, te_back = [table_halves(table) for table in tables[:7]]
    pick = jnp.asarray(tables[7].astype(ml_dtypes.bfloat16))

    def flat(t, s):
        return (t % trk_count) * sub_count + s % sub_count

    pairs = [(t, s) for t in range(trk_count) for s in range(sub_count)]
    width = green_hat.shape[2]
    lines = jnp.transpose(green_hat, (0, 2, 1))
    half = width // 2
    far, row, edge, last = run(
        green_send,
        [
            ((width // 2, half, 2 * NG), f32),
            ((half, 2 * NG), f32),
            ((width // 2, 2 * NG), f32),
            ((8, 2 * NG), f32),
        ],
        [],
        lines,
    )

    def mirrored(value, trk_shift, sub_shift):
        moves = [
            (flat(t, s), flat(trk_count - trk_shift - t, sub_count - sub_shift - s))
            for t, s in pairs
        ]
        return lax.ppermute(value, both, moves)

    def partner(value, turn):
        return lax.ppermute(value, both, [(flat(t, s), flat(t, s ^ turn)) for t, s in pairs])

    place = lax.axis_index("sub").reshape(1)
    base = (lax.axis_index("trk") * slab_depth).reshape(1)
    square = [((3, 64, NG), jnp.int32), ((3, 64, NG), f32)]
    rows, rim = run(
        sort_by_z,
        [((SORT_ROWS, NG), f32), ((NG, NG), f32)],
        square
        + [((NG, 2 * NG), f32), pltpu.SMEM((8, NG), f32), pltpu.SemaphoreType.DMA],
        base,
        live_counts,
        particle_cells,
        offsets,
        scalars=2,
    )
    rim = lax.ppermute(rim, both, [(flat(t, s), flat(t + 1, s)) for t, s in pairs])
    acc_shape = ((ACC_PLANES * NG, 2 * NG), f32)
    (start,) = run(
        deposit_own,
        [acc_shape],
        [pltpu.SMEM((8, NG), f32), pltpu.SemaphoreType.DMA],
        place,
        rows,
        scalars=1,
    )
    rim, start, far, row, edge, last = lax.optimization_barrier(
        (rim, start, far, row, edge, last)
    )
    shared = lax.all_gather(jnp.concatenate([rows, rim], axis=0), "sub", axis=0, tiled=True)
    far = mirrored(far, 1, 1)
    row = mirrored(row, 0, 1)
    edge = mirrored(edge, 1, 0)
    last = mirrored(last, 0, 0)
    lower = lax.axis_index("trk") > 0
    lower = lower & (lax.axis_index("sub") == 0)
    ends = [pltpu.SMEM((4, 8, NG), f32), pltpu.SemaphoreType.DMA((4,))]
    (dens,) = run(
        deposit_rest,
        [((QUAD * NG, NG), f32)],
        [acc_shape] + ends,
        place,
        shared,
        start,
        scalars=1,
    )
    (sent,) = run(
        forward_planes,
        [((slabs, FWD_ROWS, NG), f32)],
        [((16 * FWD_ROWS, NG), f32)] * 2,
        lower.astype(jnp.int32).reshape(1),
        dens,
        shared,
        *ty,
        *tx,
        scalars=1,
    )
    late_cells, late_offs, far, row, edge, last, _ = lax.optimization_barrier(
        (particle_cells, offsets, far, row, edge, last, sent)
    )
    got = lax.all_to_all(sent, both, split_axis=0, concat_axis=0, tiled=True)
    ints, offs = run(
        sort_by_y,
        [((264, NG), jnp.int32), ((192, NG), f32)],
        square,
        base,
        late_cells,
        late_offs,
        scalars=1,
    )
    push_x, push_y = multipole_push(late_cells, late_offs, orders, strengths)
    push = jnp.stack([push_x, push_y, jnp.zeros_like(push_x)])
    (green,) = run(
        green_pairs,
        [((2 * NG, GROUPS * NG), f32)],
        [((2 * WIDE * WIDE, NG), f32)] * 2 + [((WIDE * WIDE, NG), f32)] * 2,
        lines.reshape(-1, 2 * NG),
        far.reshape(-1, 2 * NG),
        row,
        edge,
        last,
        pick,
    )
    got, ints, offs, push = lax.optimization_barrier((got, ints, offs, push))
    (sent,) = run(
        spectrum_stage, [((slabs * BACK_ROWS, NG), f32)], [], got, green, *wf, *wb
    )
    got = lax.all_to_all(
        sent.reshape(slabs, BACK_ROWS, NG), both, split_axis=0, concat_axis=0, tiled=True
    )
    (pot,) = run(
        inverse_planes,
        [((PLANES, NG, NG), f32)],
        [((16 * FWD_ROWS, NG), f32)] * 2 + [((16 * (BACK_ROWS - FWD_ROWS), NG), f32)] * 2,
        got,
        *tx_back,
        *ty_back,
        *te_back,
    )
    chip_pot = partner(pot, 2)
    core_pot = partner(pot, 1)
    last_pot = partner(chip_pot, 1)
    depth = slab_depth + 1
    (kick,) = run(
        sample,
        [((3, count_here), f32)],
        [
            ((sub_count * PLANES, NG, NG), f32),
            ((3 * depth, NG + 8, NG), f32),
            ((3, 64, NG), f32),
            pltpu.SMEM((8, NG), jnp.int32),
            pltpu.SemaphoreType.DMA,
        ],
        place,
        pot,
        core_pot,
        chip_pot,
        last_pot,
        ints,
        offs,
        scalars=1,
    )
    new_momenta = momenta + kick + push
    new_coords = particle_cells.astype(f32) + offsets + new_momenta
    return (new_coords, new_momenta)


def solution(mesh):
    in_specs = (
        P(None, ("trk", "sub")),
        P(None, ("trk", "sub")),
        P(None, ("trk", "sub")),
        P(("trk", "sub")),
        P("trk", None, "sub"),
        P(),
        P(),
    )
    out_specs = (P(None, ("trk", "sub")), P(None, ("trk", "sub")))
    trk_count, sub_count = mesh.shape["trk"], mesh.shape["sub"]
    fits = sub_count == 4 and trk_count * WIDE == 2 * NG
    body = spread_device if fits else per_device
    return jax.shard_map(
        body, mesh=mesh, in_specs=in_specs, out_specs=out_specs, check_vma=False
    )
```

```python
import math

import jax
import jax.numpy as jnp
import ml_dtypes
import numpy as np
from jax import lax
from jax.experimental import pallas as pl
from jax.experimental.pallas import tpu as pltpu
from jax.sharding import PartitionSpec as P

NG = 128


HIGHEST = lax.Precision.HIGHEST


def multipole_push(particle_cells, offsets, orders, strengths):
    centre = 0.5 * NG
    real_u = (particle_cells[0].astype(jnp.float32) + offsets[0] - centre) / centre
    imag_u = (particle_cells[1].astype(jnp.float32) + offsets[1] - centre) / centre
    power_re = real_u
    power_im = imag_u
    push_x = jnp.zeros_like(real_u)
    push_y = jnp.zeros_like(real_u)
    for degree in range(1, 5):
        coeff = jnp.sum(jnp.where(orders - 1 == degree, strengths, jnp.zeros_like(strengths)))
        push_x = push_x - coeff * power_re
        push_y = push_y + coeff * power_im
        power_re, power_im = (
            power_re * real_u - power_im * imag_u,
            power_re * imag_u + power_im * real_u,
        )
    return (push_x, push_y)


def wave_table(freq_ids, place_ids, length):
    phase_int = freq_ids[:, None] * place_ids[None, :] % length
    angle = 2.0 * math.pi / length * phase_int.astype(jnp.float32)
    return (jnp.cos(angle), jnp.sin(angle))


def tent_weights(cells, fraction, length):
    places = jnp.arange(length, dtype=jnp.int32)
    lower = jnp.where(places[None, :] == cells[:, None], (1.0 - fraction)[:, None], 0.0)
    upper = jnp.where(places[None, :] == cells[:, None] + 1, fraction[:, None], 0.0)
    return lower + upper


def block_weights(cells_x, cells_y, cells_z, frac_x, frac_y, frac_z, depth):
    weight_x = tent_weights(cells_x, frac_x, NG)
    weight_y = tent_weights(cells_y, frac_y, NG)
    weight_z = tent_weights(cells_z, frac_z, depth)
    plane_xz = (weight_x[:, :, None] * weight_z[:, None, :]).reshape(cells_x.shape[0], -1)
    return (plane_xz, weight_y)


def per_device(particle_cells, offsets, momenta, live_counts, green_hat, orders, strengths):
    trk_count = lax.axis_size("trk")
    sub_count = lax.axis_size("sub")
    slab_depth = NG // trk_count
    depth = slab_depth + 1
    doubled = 2 * NG
    count_here = particle_cells.shape[1]
    count_all = count_here * trk_count * sub_count
    row_ids = jnp.arange(count_here, dtype=jnp.int32)
    unit_charge = float(NG**3) / float(count_all)
    charge = jnp.where(
        row_ids < live_counts[0],
        jnp.full((count_here,), unit_charge, jnp.float32),
        jnp.zeros((count_here,), jnp.float32),
    )
    local_z = particle_cells[2] - lax.axis_index("trk") * slab_depth
    block_len = math.gcd(count_here, 512)
    block_count = count_here // block_len
    blocked_x = particle_cells[0].reshape(block_count, block_len)
    blocked_y = particle_cells[1].reshape(block_count, block_len)
    blocked_z = local_z.reshape(block_count, block_len)
    blocked_off = offsets.reshape(3, block_count, block_len).transpose(1, 0, 2)
    blocked_charge = charge.reshape(block_count, block_len)

    def deposit_step(total, items):
        bx, by, bz, boff, bcharge = items
        plane_xz, weight_y = block_weights(bx, by, bz, boff[0], boff[1], boff[2], depth)
        charged = plane_xz * bcharge[:, None]
        return (total + jnp.einsum("pa,py->ay", charged, weight_y, precision=HIGHEST), None)

    start_total = jnp.zeros((NG * depth, NG), jnp.float32)
    deposit, _ = lax.scan(
        deposit_step, start_total, (blocked_x, blocked_y, blocked_z, blocked_off, blocked_charge)
    )
    deposit = deposit.reshape(NG, depth, NG)
    density = lax.psum_scatter(deposit, "sub", scatter_dimension=0, tiled=True)
    freq_all = jnp.arange(doubled, dtype=jnp.int32)
    cell_ids = jnp.arange(NG, dtype=jnp.int32)
    cos_cells, sin_cells = wave_table(freq_all, cell_ids, doubled)
    spec_re = jnp.einsum("xzy,ky->xzk", density, cos_cells, precision=HIGHEST)
    spec_im = -jnp.einsum("xzy,ky->xzk", density, sin_cells, precision=HIGHEST)
    part_re = lax.all_to_all(spec_re, "sub", split_axis=2, concat_axis=0, tiled=True)
    part_im = lax.all_to_all(spec_im, "sub", split_axis=2, concat_axis=0, tiled=True)
    out_re = jnp.einsum("kn,nzq->kzq", cos_cells, part_re, precision=HIGHEST) + jnp.einsum(
        "kn,nzq->kzq", sin_cells, part_im, precision=HIGHEST
    )
    out_im = jnp.einsum("kn,nzq->kzq", cos_cells, part_im, precision=HIGHEST) - jnp.einsum(
        "kn,nzq->kzq", sin_cells, part_re, precision=HIGHEST
    )
    xspec_re = out_re
    xspec_im = out_im
    slab_starts = jnp.arange(trk_count, dtype=jnp.int32)[:, None] * slab_depth
    forward_places = (slab_starts + jnp.arange(slab_depth + 1, dtype=jnp.int32)[None, :]).reshape(
        -1
    )
    cos_fwd, sin_fwd = wave_table(freq_all, forward_places, doubled)
    part_re = lax.all_to_all(xspec_re, "trk", split_axis=0, concat_axis=1, tiled=True)
    part_im = lax.all_to_all(xspec_im, "trk", split_axis=0, concat_axis=1, tiled=True)
    out_re = jnp.einsum("kn,xnq->xkq", cos_fwd, part_re, precision=HIGHEST) + jnp.einsum(
        "kn,xnq->xkq", sin_fwd, part_im, precision=HIGHEST
    )
    out_im = jnp.einsum("kn,xnq->xkq", cos_fwd, part_im, precision=HIGHEST) - jnp.einsum(
        "kn,xnq->xkq", sin_fwd, part_re, precision=HIGHEST
    )
    zspec_re = out_re
    zspec_im = out_im
    scaled_re = zspec_re * green_hat
    scaled_im = zspec_im * green_hat
    back_places = (slab_starts - 1 + jnp.arange(slab_depth + 3, dtype=jnp.int32)[None, :]).reshape(
        -1
    )
    inside = ((back_places >= 0) & (back_places < NG)).astype(jnp.float32) / doubled
    cos_back, sin_back = wave_table(back_places, freq_all, doubled)
    cos_back = cos_back * inside[:, None]
    sin_back = sin_back * inside[:, None]
    plane_re = jnp.einsum("nk,xkq->xnq", cos_back, scaled_re, precision=HIGHEST) - jnp.einsum(
        "nk,xkq->xnq", sin_back, scaled_im, precision=HIGHEST
    )
    plane_im = jnp.einsum("nk,xkq->xnq", sin_back, scaled_re, precision=HIGHEST) + jnp.einsum(
        "nk,xkq->xnq", cos_back, scaled_im, precision=HIGHEST
    )
    cos_inverse = jnp.transpose(cos_cells) / doubled
    sin_inverse = jnp.transpose(sin_cells) / doubled
    part_re = lax.all_to_all(plane_re, "trk", split_axis=1, concat_axis=0, tiled=True)
    part_im = lax.all_to_all(plane_im, "trk", split_axis=1, concat_axis=0, tiled=True)
    out_re = jnp.einsum("nk,kzq->nzq", cos_inverse, part_re, precision=HIGHEST) - jnp.einsum(
        "nk,kzq->nzq", sin_inverse, part_im, precision=HIGHEST
    )
    out_im = jnp.einsum("nk,kzq->nzq", sin_inverse, part_re, precision=HIGHEST) + jnp.einsum(
        "nk,kzq->nzq", cos_inverse, part_im, precision=HIGHEST
    )
    cos_final = cos_cells / doubled
    sin_final = sin_cells / doubled
    part_re = lax.all_to_all(out_re, "sub", split_axis=0, concat_axis=2, tiled=True)
    part_im = lax.all_to_all(out_im, "sub", split_axis=0, concat_axis=2, tiled=True)
    block_rows = jnp.einsum("xzk,ky->xzy", part_re, cos_final, precision=HIGHEST) - jnp.einsum(
        "xzk,ky->xzy", part_im, sin_final, precision=HIGHEST
    )
    potential = lax.all_gather(block_rows, "sub", axis=0, tiled=True)
    middle = potential[:, 1 : slab_depth + 2]
    around_x = jnp.pad(middle, ((1, 1), (0, 0), (0, 0)))
    field_x = -0.5 * (around_x[2:] - around_x[:-2])
    around_y = jnp.pad(middle, ((0, 0), (0, 0), (1, 1)))
    field_y = -0.5 * (around_y[:, :, 2:] - around_y[:, :, :-2])
    field_z = -0.5 * (potential[:, 2 : slab_depth + 3] - potential[:, : slab_depth + 1])
    field_table = jnp.stack([field_x, field_y, field_z], axis=2).reshape(NG * depth, 3 * NG)

    def sample_step(carry, items):
        bx, by, bz, boff = items
        plane_xz, weight_y = block_weights(bx, by, bz, boff[0], boff[1], boff[2], depth)
        lines = jnp.dot(plane_xz, field_table, precision=HIGHEST).reshape(bx.shape[0], 3, NG)
        return (carry, jnp.sum(lines * weight_y[:, None, :], axis=2))

    _, sampled = lax.scan(
        sample_step, jnp.zeros((), jnp.float32), (blocked_x, blocked_y, blocked_z, blocked_off)
    )
    kick = sampled.reshape(count_here, 3).transpose(1, 0)
    push_x, push_y = multipole_push(particle_cells, offsets, orders, strengths)
    push = jnp.stack([push_x, push_y, jnp.zeros_like(push_x)])
    new_momenta = momenta + kick + push
    new_coords = particle_cells.astype(jnp.float32) + offsets + new_momenta
    return (new_coords, new_momenta)


def halves(values):
    upper = values.astype(jnp.bfloat16)
    return (upper, (values - upper.astype(jnp.float32)).astype(jnp.bfloat16))


def table_halves(table):
    upper = table.astype(ml_dtypes.bfloat16)
    lower = (table - upper.astype(np.float64)).astype(ml_dtypes.bfloat16)
    return (jnp.asarray(upper), jnp.asarray(lower))


def mm(left, right):
    return jnp.dot(left, right, preferred_element_type=jnp.float32)


def mm_t(left, right):
    return lax.dot_general(left, right, (((1,), (1,)), ((), ())), preferred_element_type=jnp.float32)


def mm3(left, right):
    return mm(left[0], right[0]) + (mm(left[0], right[1]) + mm(left[1], right[0]))


def turn_blocks(parts):
    lanes = lax.broadcasted_iota(jnp.int32, parts[0].shape, 1)
    low = lanes < 64
    even = (lanes // 32) % 2 == 0
    pairs = []
    for first, second in ((parts[0], parts[2]), (parts[1], parts[3])):
        pairs.append(
            (
                jnp.where(low, first, pltpu.roll(second, 64, 1)),
                jnp.where(low, pltpu.roll(first, 64, 1), second),
            )
        )
    result = []
    for half in (0, 1):
        first, second = pairs[0][half], pairs[1][half]
        result.append(jnp.where(even, first, pltpu.roll(second, 32, 1)))
        result.append(jnp.where(even, pltpu.roll(first, 96, 1), second))
    return result


def tent(places, cells, fraction):
    away = places - cells
    return jnp.where(away == 0, 1.0 - fraction, jnp.where(away == 1, fraction, 0.0))


QUAD = 4
PLANES = 5
WIDE = 32
GROUPS = 9
SLOTS = 4 * GROUPS
FWD_ROWS = GROUPS * 2 * QUAD
BACK_ROWS = FWD_ROWS + 24
LOT = 512
CUTS = (0, 12, WIDE)
SORT_ROWS = 392
LIST_ROWS = SORT_ROWS + NG
SPAN = 3
PACK = 256
BIG = 56 * 1024 * 1024


def long_row(ref, start, count):
    return jnp.concatenate([ref[pl.ds(start + n, 1), :] for n in range(count)], axis=1)


def deposit_lots(acc_ref, rows_ref, base, ends_ref, me, bottom, top):
    span = LOT // NG
    ids = lax.broadcasted_iota(jnp.int32, (NG, LOT), 0).astype(jnp.float32)

    def step(lot, carry):
        low = ends_ref[0, lot * span].astype(jnp.int32) - me * QUAD
        high = ends_ref[1, lot * span + span - 1].astype(jnp.int32) + 1 - me * QUAD
        low = jnp.maximum(low, bottom)
        high = jnp.minimum(high, top)
        size = min(SPAN, top - bottom + 1)

        @pl.when(low <= high)
        def _():
            cell_x, cell_y, cell_z, off_x, off_y, off_z = [
                long_row(rows_ref, base + which * 64 + lot * span, span) for which in range(6)
            ]
            right = jnp.concatenate(halves(tent(ids, cell_x, off_x)), axis=0)
            weight_y = tent(ids, cell_y, off_y)

            def window(turn, inner):
                start = low + turn * size
                away = (start + me * QUAD).astype(jnp.float32) - cell_z
                left = []
                for z in range(size):
                    left.extend(halves(weight_y * tent(away + float(z), 0.0, off_z)))
                lines = mm_t(jnp.concatenate(left, axis=0), right)
                for z in range(size):
                    place = pl.ds(pl.multiple_of((start + z - bottom) * NG, NG), NG)
                    part = lines[2 * z * NG : (2 * z + 2) * NG]
                    acc_ref[place, :] += part[0:NG] + part[NG : 2 * NG]
                return inner

            lax.fori_loop(0, (high - low) // size + 1, window, 0)

        return carry

    lax.fori_loop(0, 64 // span, step, 0)


ACC_PLANES = QUAD + SPAN - 1
ENDS = slice(6 * 64, 6 * 64 + 8)


def deposit_own(place_ref, rows_ref, acc_ref, ends_ref, sem):
    ends = pltpu.make_async_copy(rows_ref.at[ENDS, :], ends_ref, sem)
    ends.start()
    acc_ref[...] = jnp.zeros_like(acc_ref)
    ends.wait()
    deposit_lots(acc_ref, rows_ref, 0, ends_ref, place_ref[0], 0, QUAD - 1)


def fetch_ends(rows_ref, ends_ref, sem):
    copies = [
        pltpu.make_async_copy(
            rows_ref.at[n * LIST_ROWS + ENDS.start : n * LIST_ROWS + ENDS.stop, :],
            ends_ref.at[n],
            sem.at[n],
        )
        for n in range(4)
    ]
    for copy in copies:
        copy.start()
    return copies


def deposit_rest(place_ref, rows_ref, start_ref, dens_ref, acc_ref, ends_ref, sem):
    copies = fetch_ends(rows_ref, ends_ref, sem)
    acc_ref[...] = start_ref[...]
    for copy in copies:
        copy.wait()
    me = place_ref[0]

    def each(turn, carry):
        n = lax.rem(me + turn, 4)
        deposit_lots(acc_ref, rows_ref, n * LIST_ROWS, ends_ref.at[n], me, 0, QUAD - 1)
        return carry

    lax.fori_loop(1, 4, each, 0)
    live = slice(0, QUAD * NG)
    dens_ref[...] = acc_ref[live, 0:NG] + acc_ref[live, NG : 2 * NG]


def forward_planes(lower_ref, dens_ref, list_ref, ty_hi, ty_lo, tx_hi, tx_lo, out_ref, left_ref, right_ref):
    half = 16 * GROUPS
    for z in range(QUAD):
        plane = dens_ref[z * NG : (z + 1) * NG, :]
        if z == 0:
            rims = [
                list_ref[n * LIST_ROWS + SORT_ROWS : (n + 1) * LIST_ROWS, :] for n in range(4)
            ]
            rim = (rims[0] + rims[1]) + (rims[2] + rims[3])
            plane = plane + jnp.where(lower_ref[0] > 0, rim, 0.0)
        lines = mm3((ty_hi[...], ty_lo[...]), halves(plane))
        real, imag = lines[0:half], lines[half : 2 * half]
        left_ref[pl.ds(2 * z, half, stride=8), :] = real
        right_ref[pl.ds(2 * z, half, stride=8), :] = imag
        left_ref[pl.ds(2 * z + 1, half, stride=8), :] = imag
        right_ref[pl.ds(2 * z + 1, half, stride=8), :] = -real
    for s in range(4):
        whole = []
        for i in range(4):
            start = (i * 4 + s) * FWD_ROWS
            piece = slice(start, start + FWD_ROWS)
            lines = jnp.concatenate([left_ref[piece, :], right_ref[piece, :]], axis=1)
            whole.append(mm3(halves(lines), (tx_hi[...], tx_lo[...])))
        for th in range(2):
            turned = turn_blocks([part[:, th * NG : (th + 1) * NG] for part in whole])
            for t in range(4):
                out_ref[(th * 4 + t) * 4 + s] = turned[t]


def green_send(lines_ref, first_ref, second_ref, row_ref, edge_ref, last_ref):
    fars = (first_ref, second_ref)
    for k in range(1, WIDE):
        piece = int(k >= CUTS[1])
        fars[piece][k - CUTS[piece]] = lines_ref[WIDE - k, WIDE : 2 * WIDE, :]
        edge_ref[k : k + 1, :] = lines_ref[WIDE - k, 0:1, :]
    first_ref[0] = lines_ref[0, WIDE : 2 * WIDE, :]
    edge_ref[0:1, :] = lines_ref[0, 0:1, :]
    row_ref[...] = lines_ref[0, WIDE : 2 * WIDE, :]
    last_ref[...] = lines_ref[0, 0:8, :]


def green_pairs(
    own_ref, first_ref, second_ref, row_ref, edge_ref, last_ref, pick_ref, out_ref, *parts
):
    for side in range(2):
        lanes = slice(side * NG, (side + 1) * NG)
        parts[side][...] = own_ref[:, lanes]
        for piece, ref in enumerate((first_ref, second_ref)):
            parts[2 + side][CUTS[piece] * WIDE : CUTS[piece + 1] * WIDE, :] = ref[:, lanes]
        parts[2 + side][0:WIDE, :] = row_ref[:, lanes]
    first = lax.broadcasted_iota(jnp.int32, (WIDE, 2 * NG), 0) == 0
    edge = jnp.where(first, jnp.broadcast_to(last_ref[0:1, :], (WIDE, 2 * NG)), edge_ref[...])

    def pull(refs, start, stride):
        return jnp.concatenate(
            [ref[pl.ds(start, WIDE, stride=stride), :] for ref in refs], axis=1
        )

    for group in range(GROUPS):
        near, away = [], []
        for i in range(4):
            j = group * 4 + i
            if j > WIDE:
                near.append(jnp.zeros((WIDE, 2 * NG), jnp.float32))
                away.append(jnp.zeros((WIDE, 2 * NG), jnp.float32))
                continue
            near.append(pull(parts[0:2], j, 2 * WIDE))
            away.append(edge if j == 0 else pull(parts[2:4], WIDE - j, WIDE))
        both = jnp.concatenate(
            [jnp.concatenate(near, axis=0), jnp.concatenate(away, axis=0)], axis=1
        )
        high = both.astype(jnp.bfloat16)
        left = both - high.astype(jnp.float32)
        mid = left.astype(jnp.bfloat16)
        low = (left - mid.astype(jnp.float32)).astype(jnp.bfloat16)
        pick = pick_ref[...]
        out_ref[:, group * NG : (group + 1) * NG] = 0.5 * (
            mm_t(pick, high) + (mm_t(pick, mid) + mm_t(pick, low))
        )


def spectrum_stage(in_ref, green_ref, wf_hi, wf_lo, wb_hi, wb_lo, out_ref):
    slabs = in_ref.shape[0]
    half = 2 * NG
    for first in range(0, GROUPS, 2):
        groups = [g for g in (first, first + 1) if g < GROUPS]
        data = [in_ref[:, g * 8 : (g + 1) * 8, :].reshape(slabs * 8, NG) for g in groups]
        data = data[0] if len(data) == 1 else jnp.concatenate(data, axis=1)
        spec = mm3((wf_hi[...], wf_lo[...]), halves(data))
        green = green_ref[:, first * NG : (first + len(groups)) * NG]
        scaled = jnp.concatenate([spec[0:half] * green, spec[half : 2 * half] * green], axis=0)
        back = mm3((wb_hi[...], wb_lo[...]), halves(scaled))
        for place, g in enumerate(groups):
            part = back[:, place * NG : (place + 1) * NG]
            for slab in range(slabs):
                row = slab * BACK_ROWS + g * 8
                out_ref[row : row + 8, :] = part[slab * 8 : slab * 8 + 8]
            for c in range(2):
                start = slabs * (8 + c)
                out_ref[pl.ds(FWD_ROWS + 2 * g + c, slabs, stride=BACK_ROWS), :] = part[
                    start : start + slabs
                ]
    for row in range(FWD_ROWS + 2 * GROUPS, BACK_ROWS):
        out_ref[pl.ds(row, slabs, stride=BACK_ROWS), :] = jnp.zeros((slabs, NG), jnp.float32)


def inverse_planes(
    in_ref, tx_hi, tx_lo, ty_hi, ty_lo, te_hi, te_lo, out_ref, mid_cos, mid_sin, top_cos, top_sin
):
    extra = BACK_ROWS - FWD_ROWS
    for s in range(4):
        main, rest = [[], [], [], []], [[], [], [], []]
        for th in range(2):
            parts = [in_ref[(th * 4 + t) * 4 + s, 0:FWD_ROWS, :] for t in range(4)]
            tops = [in_ref[(th * 4 + t) * 4 + s, FWD_ROWS:BACK_ROWS, :] for t in range(4)]
            for i, block in enumerate(turn_blocks(parts)):
                main[i].append(block)
            for i, block in enumerate(turn_blocks(tops)):
                rest[i].append(block)
        for i in range(4):
            row = (i * 4 + s) * FWD_ROWS
            lines = jnp.concatenate(main[i], axis=1)
            lines = mm3(halves(lines), (tx_hi[...], tx_lo[...]))
            mid_cos[row : row + FWD_ROWS, :] = lines[:, 0:NG]
            mid_sin[row : row + FWD_ROWS, :] = lines[:, NG : 2 * NG]
            row = (i * 4 + s) * extra
            lines = jnp.concatenate(rest[i], axis=1)
            lines = mm3(halves(lines), (tx_hi[...], tx_lo[...]))
            top_cos[row : row + extra, :] = lines[:, 0:NG]
            top_sin[row : row + extra, :] = lines[:, NG : 2 * NG]

    def finish(cos_ref, sin_ref, start, count, stride, table):
        real, imag = pl.ds(start, count, stride=stride), pl.ds(start + 1, count, stride=stride)
        lines = jnp.concatenate(
            [cos_ref[real, :] - sin_ref[imag, :], sin_ref[real, :] + cos_ref[imag, :]], axis=0
        )
        return mm3((table[0][...], table[1][...]), halves(lines))

    for z in range(QUAD):
        out_ref[z] = finish(mid_cos, mid_sin, 2 * z, 16 * GROUPS, 8, (ty_hi, ty_lo))
    out_ref[QUAD] = finish(top_cos, top_sin, 0, 8 * extra, 2, (te_hi, te_lo))


SORT_BITS = 13
DEAD = 100


def sort_network(items, rolled=False):
    shape = (8, NG)
    lanes = lax.broadcasted_iota(jnp.int32, shape, 1)
    subs = lax.broadcasted_iota(jnp.int32, shape, 0)
    base = subs * 8 + (lanes // 64) * 64 + (lanes % 64) * 128

    def exchange(items, others, bit, size):
        fresh = [[] for _ in items]
        for v in range(8):
            rank = base + v
            keep = (((rank >> bit) ^ (rank >> (size + 1))) & 1) == 0
            take = (others[0][v] < items[0][v]) == keep
            for n in range(len(items)):
                fresh[n].append(jnp.where(take, others[n][v], items[n][v]))
        return fresh

    def near_stage(items, bit, size):
        others = [[item[v ^ (1 << bit)] for v in range(8)] for item in items]
        return exchange(items, others, bit, size)

    def far_stage(items, bit, size, index, axis):
        others = [[jnp.take_along_axis(value, index, axis=axis) for value in item] for item in items]
        return exchange(items, others, bit, size)

    def far_bit(items, bit, size):
        if bit < 3:
            return near_stage(items, bit, size)
        if bit < 6:
            return far_stage(items, bit, size, subs ^ (1 << (bit - 3)), 0)
        return far_stage(items, bit, size, lanes ^ (64 if bit == 6 else 1 << (bit - 7)), 1)

    for size in range(3 if rolled else SORT_BITS):
        for bit in range(size, -1, -1):
            items = far_bit(items, bit, size)
    if not rolled:
        return items

    def merge(size, items):
        def lane_step(n, items):
            bit = size - n
            index = lanes ^ jnp.where(bit == 6, 64, 1 << jnp.maximum(bit - 7, 0))
            return far_stage(items, bit, size, index, 1)

        def sub_step(n, items):
            bit = jnp.minimum(size, 5) - n
            return far_stage(items, bit, size, subs ^ (1 << (bit - 3)), 0)

        items = lax.fori_loop(0, jnp.maximum(size - 5, 0), lane_step, items)
        items = lax.fori_loop(0, jnp.minimum(size, 5) - 2, sub_step, items)
        for bit in (2, 1, 0):
            items = near_stage(items, bit, size)
        return items

    return lax.fori_loop(3, SORT_BITS, merge, items)


def laid_out(values):
    turned = jnp.transpose(jnp.concatenate(values, axis=0), (1, 0))
    return jnp.concatenate([turned[0:64], turned[64:128]], axis=1)


def sort_labels(v):
    lanes = lax.broadcasted_iota(jnp.int32, (8, NG), 1)
    subs = lax.broadcasted_iota(jnp.int32, (8, NG), 0)
    return (subs + v * 8) * 128 + (lanes // 64) * 64 + (lanes % 8) * 8 + (lanes // 8) % 8


def square_up(cells_ref, offs_ref, ints_ref, flts_ref):
    for k in range(64):
        lanes = slice(k * NG, (k + 1) * NG)
        for d in range(3):
            ints_ref[d, k : k + 1, :] = cells_ref[d : d + 1, lanes]
            flts_ref[d, k : k + 1, :] = offs_ref[d : d + 1, lanes]


def sort_by_z(
    place_ref,
    live_ref,
    cells_ref,
    offs_ref,
    out_ref,
    rim_ref,
    ints_ref,
    flts_ref,
    top_ref,
    ends_ref,
    sem,
):
    square_up(cells_ref, offs_ref, ints_ref, flts_ref)
    lanes = lax.broadcasted_iota(jnp.int32, (8, NG), 1)
    subs = lax.broadcasted_iota(jnp.int32, (8, NG), 0)
    keys, packs, offs = [], [], [[], [], []]
    for v in range(8):
        rows = slice(v * 8, v * 8 + 8)
        alive = (subs + v * 8) * NG + lanes < live_ref[0]
        cell_z = jnp.where(alive, ints_ref[2, rows, :] - place_ref[0], DEAD)
        keys.append(cell_z * 8192 + sort_labels(v))
        packs.append(ints_ref[0, rows, :] * NG + ints_ref[1, rows, :])
        for d in range(3):
            offs[d].append(flts_ref[d, rows, :])
    items = [laid_out(item) for item in sort_network([keys, packs] + offs)]
    cell_z = (items[0] >> 13).astype(jnp.float32)
    out_ref[0:64, :] = (items[1] >> 7).astype(jnp.float32)
    out_ref[64:128, :] = (items[1] & (NG - 1)).astype(jnp.float32)
    out_ref[128:192, :] = cell_z
    for d in range(3):
        out_ref[192 + 64 * d : 256 + 64 * d, :] = items[2 + d]
    ends = jnp.transpose(cell_z, (1, 0))
    ends = jnp.concatenate([ends[0:1], ends[NG - 1 : NG], jnp.zeros((6, 64), jnp.float32)], axis=0)
    out_ref[384:392, :] = jnp.concatenate([ends, ends], axis=1)
    fetch = pltpu.make_async_copy(out_ref.at[ENDS, :], ends_ref, sem)
    fetch.start()
    top_ref[...] = jnp.zeros_like(top_ref)
    fetch.wait()
    deposit_lots(top_ref, out_ref, 0, ends_ref, 0, 4 * QUAD, 4 * QUAD)
    rim_ref[...] = top_ref[:, 0:NG] + top_ref[:, NG : 2 * NG]


def sort_by_y(place_ref, cells_ref, offs_ref, out_int, out_off, ints_ref, flts_ref):
    square_up(cells_ref, offs_ref, ints_ref, flts_ref)
    keys, packs, offs = [], [], [[], [], []]
    for v in range(8):
        rows = slice(v * 8, v * 8 + 8)
        keys.append(ints_ref[1, rows, :] * 8192 + sort_labels(v))
        packs.append(ints_ref[0, rows, :] * 64 + ints_ref[2, rows, :] - place_ref[0])
        for d in range(3):
            offs[d].append(flts_ref[d, rows, :])
    items = [laid_out(item) for item in sort_network([keys, packs] + offs, rolled=True)]
    cell_y = items[0] >> 13
    out_int[0:64, :] = cell_y
    out_int[64:128, :] = items[0] & 8191
    out_int[128:192, :] = items[1] >> 6
    out_int[192:256, :] = items[1] & 63
    for d in range(3):
        out_off[d * 64 : d * 64 + 64, :] = items[2 + d]
    ends = jnp.transpose(cell_y, (1, 0))
    ends = jnp.concatenate([ends[0:1], ends[NG - 1 : NG], jnp.zeros((6, 64), jnp.int32)], axis=0)
    out_int[256:264, :] = jnp.concatenate([ends, ends], axis=1)


def sample(
    place_ref,
    own_ref,
    core_ref,
    chip_ref,
    last_ref,
    int_ref,
    off_ref,
    mom_ref,
    push_ref,
    home_ref,
    coord_ref,
    out_ref,
    pot_ref,
    field_ref,
    kick_ref,
    ends_ref,
    sem,
):
    ends = pltpu.make_async_copy(int_ref.at[256:264, :], ends_ref, sem)
    ends.start()
    me = place_ref[0]
    for turn, ref in enumerate((own_ref, core_ref, chip_ref, last_ref)):
        pot_ref[pl.ds((me ^ turn) * PLANES, PLANES)] = ref[...]
    depth = field_ref.shape[0] // 3
    rows = lax.broadcasted_iota(jnp.int32, (NG, NG), 0)
    lanes = lax.broadcasted_iota(jnp.int32, (NG, NG), 1)
    blank = jnp.zeros((8, NG), jnp.float32)

    def fields(z, carry):
        plane = pot_ref[z + 1]
        right = jnp.where(lanes == NG - 1, 0.0, pltpu.roll(plane, NG - 1, 1))
        left = jnp.where(lanes == 0, 0.0, pltpu.roll(plane, 1, 1))
        field_ref[z, 0:NG, :] = -0.5 * (right - left)
        right = jnp.where(rows == NG - 1, 0.0, pltpu.roll(plane, NG - 1, 0))
        left = jnp.where(rows == 0, 0.0, pltpu.roll(plane, 1, 0))
        field_ref[depth + z, 0:NG, :] = -0.5 * (right - left)
        field_ref[2 * depth + z, 0:NG, :] = -0.5 * (pot_ref[z + 2] - pot_ref[z])
        for d in range(3):
            field_ref[d * depth + z, NG : NG + 8, :] = blank
        return carry

    lax.fori_loop(0, depth, fields, 0)
    x_ids = lax.broadcasted_iota(jnp.int32, (NG, PACK), 0)
    z_ids = lax.broadcasted_iota(jnp.int32, (24, PACK), 0)
    y_ids = lax.broadcasted_iota(jnp.int32, (8, PACK), 0)
    span = PACK // NG
    ends.wait()

    def pack_step(pack, carry):
        first = pack * span
        cell_y, cell_x, cell_z = [
            long_row(int_ref, which * 64 + first, span) for which in (0, 2, 3)
        ]
        off_x, off_y, off_z = [long_row(off_ref, which * 64 + first, span) for which in range(3)]
        weight_x = halves(tent(x_ids, cell_x, off_x))
        tall = [jnp.concatenate([part, part], axis=0) for part in weight_x]
        weight_z = tent(z_ids, cell_z, off_z)
        low = ends_ref[0, first]
        high = ends_ref[1, first + span - 1] + 1

        def chunk(turn):
            start = low + turn * 8
            weight_y = tent(y_ids + start, cell_y, off_y)
            table = field_ref[:, pl.ds(start, 8), :].reshape(3 * depth * 8, NG)
            part = jnp.concatenate(halves(table), axis=1)
            lines = mm(part, tall[0]) + mm(part, tall[1])
            fresh = []
            for d in range(3):
                total = lines[d * depth * 8 : d * depth * 8 + 8] * weight_z[0:1]
                for z in range(1, depth):
                    row = (d * depth + z) * 8
                    total = total + lines[row : row + 8] * weight_z[z : z + 1]
                fresh.append(jnp.sum(total * weight_y, axis=0, keepdims=True))
            return fresh

        for d, kick in enumerate(chunk(0)):
            for n in range(span):
                kick_ref[d, pl.ds(first + n, 1), :] = kick[:, n * NG : (n + 1) * NG]
        return (low, high, first, chunk)

    def pair_step(pair, carry):
        packs = [pack_step(2 * pair + n, 0) for n in range(2)]
        for low, high, first, chunk in packs:

            def more(turn, inner):
                for d, kick in enumerate(chunk(turn)):
                    for n in range(span):
                        kick_ref[d, pl.ds(first + n, 1), :] += kick[:, n * NG : (n + 1) * NG]
                return inner

            lax.fori_loop(1, (high - low) // 8 + 1, more, 0)
        return carry

    lax.fori_loop(0, 32 // span, pair_step, 0)
    items = [[int_ref[64 + v * 8 : v * 8 + 72, :] for v in range(8)]]
    for d in range(3):
        items.append([kick_ref[d, v * 8 : v * 8 + 8, :] for v in range(8)])
    items = sort_network(items)
    for d in range(3):
        kick = laid_out(items[1 + d])
        for k in range(64):
            out_ref[d : d + 1, k * NG : (k + 1) * NG] = kick[k : k + 1, :]
    fresh = (mom_ref[...] + out_ref[...]) + push_ref[...]
    out_ref[...] = fresh
    coord_ref[...] = home_ref[...] + fresh


def plane_tables(trk_count, sub_count, unit_charge):
    doubled = 2 * NG
    width = doubled // sub_count
    slots = np.arange(4)[:, None, None] + 4 * np.arange(GROUPS)[None, None, :]
    slots = np.broadcast_to(slots, (4, sub_count, GROUPS))
    freq = width * np.arange(sub_count)[None, :, None] + slots
    used = (slots <= width // 2).astype(np.float64)
    share = used * np.where((slots == 0) | (slots == width // 2), 1.0, 2.0)
    cells = np.arange(NG)
    turn = 2.0 * np.pi / doubled
    angle = turn * ((freq.reshape(-1)[:, None] * cells[None, :]) % doubled)
    used = used.reshape(-1)[:, None]
    share_line = share.reshape(-1)[:, None]
    ty = np.concatenate([np.cos(angle) * used, -np.sin(angle) * used], axis=0) * unit_charge
    back = np.concatenate([np.cos(angle) * share_line, -np.sin(angle) * share_line], axis=0)
    ty_back = back.T / doubled
    pieces = back.reshape(2, 4 * sub_count, GROUPS, NG)
    pieces = np.concatenate([pieces, np.zeros((2, 4 * sub_count, 12 - GROUPS, NG))], axis=2)
    te_back = pieces.reshape(-1, NG).T / doubled
    angle = turn * ((cells[:, None] * np.arange(doubled)[None, :]) % doubled)
    tx = np.concatenate([np.cos(angle), np.sin(angle)], axis=0)
    tx_back = np.concatenate([np.cos(angle).T, np.sin(angle).T], axis=1) / doubled
    slabs = trk_count * sub_count
    angle = turn * ((np.arange(doubled)[:, None] * cells[None, :]) % doubled)
    cos, sin = np.cos(angle), np.sin(angle)
    wf = np.stack(
        [np.stack([cos, sin], axis=2), np.stack([-sin, cos], axis=2)], axis=0
    ).reshape(2 * doubled, 2 * NG)
    slab = np.arange(slabs)
    planes = (
        (slab // sub_count * QUAD * sub_count - 1 + PLANES * (slab % sub_count))[:, None]
        + np.arange(PLANES)[None, :]
    )
    inside = ((planes >= 0) & (planes < NG)).astype(np.float64)[:, :, None] / doubled
    angle = turn * ((planes[:, :, None] * np.arange(doubled)[None, None, :]) % doubled)
    cos, sin = np.cos(angle) * inside, np.sin(angle) * inside
    wb = np.stack([np.concatenate([cos, -sin], axis=2), np.concatenate([sin, cos], axis=2)], axis=2)
    wb = np.concatenate(
        [
            wb[:, :QUAD].reshape(slabs * QUAD * 2, 2 * doubled),
            wb[:, QUAD, 0],
            wb[:, QUAD, 1],
        ],
        axis=0,
    )
    pick = np.zeros((doubled, 2 * doubled))
    line = np.arange(doubled)
    pick[line, line] = 1.0
    pick[line, doubled + (-line) % doubled] = 1.0
    return ty, tx, wf, wb, tx_back, ty_back, te_back, pick


def run(body, shapes, scratch, *args, scalars=0):
    out_shape = tuple(jax.ShapeDtypeStruct(*shape) for shape in shapes)
    space = pl.BlockSpec(memory_space=pltpu.VMEM)
    result = pl.pallas_call(
        body,
        out_shape=out_shape,
        in_specs=[pl.BlockSpec(memory_space=pltpu.SMEM)] * scalars + [space] * (len(args) - scalars),
        out_specs=tuple(space for _ in out_shape),
        scratch_shapes=[
            pltpu.VMEM(*shape) if isinstance(shape, tuple) else shape for shape in scratch
        ],
        compiler_params=pltpu.CompilerParams(vmem_limit_bytes=BIG),
    )(*args)
    return result


def spread_device(particle_cells, offsets, momenta, live_counts, green_hat, orders, strengths):
    f32 = jnp.float32
    trk_count = lax.axis_size("trk")
    sub_count = lax.axis_size("sub")
    slabs = trk_count * sub_count
    slab_depth = NG // trk_count
    count_here = particle_cells.shape[1]
    unit_charge = float(NG**3) / float(count_here * slabs)
    both = ("trk", "sub")
    tables = plane_tables(trk_count, sub_count, unit_charge)
    ty, tx, wf, wb, tx_back, ty_back, te_back = [table_halves(table) for table in tables[:7]]
    pick = jnp.asarray(tables[7].astype(ml_dtypes.bfloat16))

    def flat(t, s):
        return (t % trk_count) * sub_count + s % sub_count

    pairs = [(t, s) for t in range(trk_count) for s in range(sub_count)]
    width = green_hat.shape[2]
    lines = jnp.transpose(green_hat, (0, 2, 1))
    half = width // 2
    first, second, row, edge, last = run(
        green_send,
        [((CUTS[n + 1] - CUTS[n], half, 2 * NG), f32) for n in range(2)]
        + [
            ((half, 2 * NG), f32),
            ((width // 2, 2 * NG), f32),
            ((8, 2 * NG), f32),
        ],
        [],
        lines,
    )

    def mirrored(value, trk_shift, sub_shift):
        moves = [
            (flat(t, s), flat(trk_count - trk_shift - t, sub_count - sub_shift - s))
            for t, s in pairs
        ]
        return lax.ppermute(value, both, moves)

    first = mirrored(first, 1, 1)

    def partner(value, turn):
        return lax.ppermute(value, both, [(flat(t, s), flat(t, s ^ turn)) for t, s in pairs])

    place = lax.axis_index("sub").reshape(1)
    base = (lax.axis_index("trk") * slab_depth).reshape(1)
    square = [((3, 64, NG), jnp.int32), ((3, 64, NG), f32)]
    rows, rim = run(
        sort_by_z,
        [((SORT_ROWS, NG), f32), ((NG, NG), f32)],
        square
        + [((NG, 2 * NG), f32), pltpu.SMEM((8, NG), f32), pltpu.SemaphoreType.DMA],
        base,
        live_counts,
        particle_cells,
        offsets,
        scalars=2,
    )
    rim = lax.ppermute(rim, both, [(flat(t, s), flat(t + 1, s)) for t, s in pairs])
    acc_shape = ((ACC_PLANES * NG, 2 * NG), f32)
    (start,) = run(
        deposit_own,
        [acc_shape],
        [pltpu.SMEM((8, NG), f32), pltpu.SemaphoreType.DMA],
        place,
        rows,
        scalars=1,
    )
    rim, start, first, second, row, edge, last = lax.optimization_barrier(
        (rim, start, first, second, row, edge, last)
    )
    shared = lax.all_gather(jnp.concatenate([rows, rim], axis=0), "sub", axis=0, tiled=True)
    second = mirrored(second, 1, 1)
    row = mirrored(row, 0, 1)
    edge = mirrored(edge, 1, 0)
    last = mirrored(last, 0, 0)
    lower = lax.axis_index("trk") > 0
    lower = lower & (lax.axis_index("sub") == 0)
    ends = [pltpu.SMEM((4, 8, NG), f32), pltpu.SemaphoreType.DMA((4,))]
    (dens,) = run(
        deposit_rest,
        [((QUAD * NG, NG), f32)],
        [acc_shape] + ends,
        place,
        shared,
        start,
        scalars=1,
    )
    (sent,) = run(
        forward_planes,
        [((slabs, FWD_ROWS, NG), f32)],
        [((16 * FWD_ROWS, NG), f32)] * 2,
        lower.astype(jnp.int32).reshape(1),
        dens,
        shared,
        *ty,
        *tx,
        scalars=1,
    )
    late_cells, late_offs, first, second, row, edge, last, _ = lax.optimization_barrier(
        (particle_cells, offsets, first, second, row, edge, last, sent)
    )
    got = lax.all_to_all(sent, both, split_axis=0, concat_axis=0, tiled=True)
    ints, offs = run(
        sort_by_y,
        [((264, NG), jnp.int32), ((192, NG), f32)],
        square,
        base,
        late_cells,
        late_offs,
        scalars=1,
    )
    push_x, push_y = multipole_push(late_cells, late_offs, orders, strengths)
    push = jnp.stack([push_x, push_y, jnp.zeros_like(push_x)])
    (green,) = run(
        green_pairs,
        [((2 * NG, GROUPS * NG), f32)],
        [((2 * WIDE * WIDE, NG), f32)] * 2 + [((WIDE * WIDE, NG), f32)] * 2,
        lines.reshape(-1, 2 * NG),
        first.reshape(-1, 2 * NG),
        second.reshape(-1, 2 * NG),
        row,
        edge,
        last,
        pick,
    )
    home = late_cells.astype(f32) + late_offs
    got, ints, offs, push, home = lax.optimization_barrier((got, ints, offs, push, home))
    (sent,) = run(
        spectrum_stage, [((slabs * BACK_ROWS, NG), f32)], [], got, green, *wf, *wb
    )
    got = lax.all_to_all(
        sent.reshape(slabs, BACK_ROWS, NG), both, split_axis=0, concat_axis=0, tiled=True
    )
    (pot,) = run(
        inverse_planes,
        [((PLANES, NG, NG), f32)],
        [((16 * FWD_ROWS, NG), f32)] * 2 + [((16 * (BACK_ROWS - FWD_ROWS), NG), f32)] * 2,
        got,
        *tx_back,
        *ty_back,
        *te_back,
    )
    chip_pot = partner(pot, 2)
    core_pot = partner(pot, 1)
    last_pot = partner(chip_pot, 1)
    depth = slab_depth + 1
    coords, fresh = run(
        sample,
        [((3, count_here), f32)] * 2,
        [
            ((sub_count * PLANES, NG, NG), f32),
            ((3 * depth, NG + 8, NG), f32),
            ((3, 64, NG), f32),
            pltpu.SMEM((8, NG), jnp.int32),
            pltpu.SemaphoreType.DMA,
        ],
        place,
        pot,
        core_pot,
        chip_pot,
        last_pot,
        ints,
        offs,
        momenta,
        push,
        home,
        scalars=1,
    )
    return (coords, fresh)


def solution(mesh):
    in_specs = (
        P(None, ("trk", "sub")),
        P(None, ("trk", "sub")),
        P(None, ("trk", "sub")),
        P(("trk", "sub")),
        P("trk", None, "sub"),
        P(),
        P(),
    )
    out_specs = (P(None, ("trk", "sub")), P(None, ("trk", "sub")))
    trk_count, sub_count = mesh.shape["trk"], mesh.shape["sub"]
    fits = sub_count == 4 and trk_count * WIDE == 2 * NG
    body = spread_device if fits else per_device
    return jax.shard_map(
        body, mesh=mesh, in_specs=in_specs, out_specs=out_specs, check_vma=False
    )
```

```python
import math

import jax
import jax.numpy as jnp
import ml_dtypes
import numpy as np
from jax import lax
from jax.experimental import pallas as pl
from jax.experimental.pallas import tpu as pltpu
from jax.sharding import PartitionSpec as P

NG = 128


HIGHEST = lax.Precision.HIGHEST


def multipole_push(particle_cells, offsets, orders, strengths):
    centre = 0.5 * NG
    real_u = (particle_cells[0].astype(jnp.float32) + offsets[0] - centre) / centre
    imag_u = (particle_cells[1].astype(jnp.float32) + offsets[1] - centre) / centre
    power_re = real_u
    power_im = imag_u
    push_x = jnp.zeros_like(real_u)
    push_y = jnp.zeros_like(real_u)
    for degree in range(1, 5):
        coeff = jnp.sum(jnp.where(orders - 1 == degree, strengths, jnp.zeros_like(strengths)))
        push_x = push_x - coeff * power_re
        push_y = push_y + coeff * power_im
        power_re, power_im = (
            power_re * real_u - power_im * imag_u,
            power_re * imag_u + power_im * real_u,
        )
    return (push_x, push_y)


def wave_table(freq_ids, place_ids, length):
    phase_int = freq_ids[:, None] * place_ids[None, :] % length
    angle = 2.0 * math.pi / length * phase_int.astype(jnp.float32)
    return (jnp.cos(angle), jnp.sin(angle))


def tent_weights(cells, fraction, length):
    places = jnp.arange(length, dtype=jnp.int32)
    lower = jnp.where(places[None, :] == cells[:, None], (1.0 - fraction)[:, None], 0.0)
    upper = jnp.where(places[None, :] == cells[:, None] + 1, fraction[:, None], 0.0)
    return lower + upper


def block_weights(cells_x, cells_y, cells_z, frac_x, frac_y, frac_z, depth):
    weight_x = tent_weights(cells_x, frac_x, NG)
    weight_y = tent_weights(cells_y, frac_y, NG)
    weight_z = tent_weights(cells_z, frac_z, depth)
    plane_xz = (weight_x[:, :, None] * weight_z[:, None, :]).reshape(cells_x.shape[0], -1)
    return (plane_xz, weight_y)


def per_device(particle_cells, offsets, momenta, live_counts, green_hat, orders, strengths):
    trk_count = lax.axis_size("trk")
    sub_count = lax.axis_size("sub")
    slab_depth = NG // trk_count
    depth = slab_depth + 1
    doubled = 2 * NG
    count_here = particle_cells.shape[1]
    count_all = count_here * trk_count * sub_count
    row_ids = jnp.arange(count_here, dtype=jnp.int32)
    unit_charge = float(NG**3) / float(count_all)
    charge = jnp.where(
        row_ids < live_counts[0],
        jnp.full((count_here,), unit_charge, jnp.float32),
        jnp.zeros((count_here,), jnp.float32),
    )
    local_z = particle_cells[2] - lax.axis_index("trk") * slab_depth
    block_len = math.gcd(count_here, 512)
    block_count = count_here // block_len
    blocked_x = particle_cells[0].reshape(block_count, block_len)
    blocked_y = particle_cells[1].reshape(block_count, block_len)
    blocked_z = local_z.reshape(block_count, block_len)
    blocked_off = offsets.reshape(3, block_count, block_len).transpose(1, 0, 2)
    blocked_charge = charge.reshape(block_count, block_len)

    def deposit_step(total, items):
        bx, by, bz, boff, bcharge = items
        plane_xz, weight_y = block_weights(bx, by, bz, boff[0], boff[1], boff[2], depth)
        charged = plane_xz * bcharge[:, None]
        return (total + jnp.einsum("pa,py->ay", charged, weight_y, precision=HIGHEST), None)

    start_total = jnp.zeros((NG * depth, NG), jnp.float32)
    deposit, _ = lax.scan(
        deposit_step, start_total, (blocked_x, blocked_y, blocked_z, blocked_off, blocked_charge)
    )
    deposit = deposit.reshape(NG, depth, NG)
    density = lax.psum_scatter(deposit, "sub", scatter_dimension=0, tiled=True)
    freq_all = jnp.arange(doubled, dtype=jnp.int32)
    cell_ids = jnp.arange(NG, dtype=jnp.int32)
    cos_cells, sin_cells = wave_table(freq_all, cell_ids, doubled)
    spec_re = jnp.einsum("xzy,ky->xzk", density, cos_cells, precision=HIGHEST)
    spec_im = -jnp.einsum("xzy,ky->xzk", density, sin_cells, precision=HIGHEST)
    part_re = lax.all_to_all(spec_re, "sub", split_axis=2, concat_axis=0, tiled=True)
    part_im = lax.all_to_all(spec_im, "sub", split_axis=2, concat_axis=0, tiled=True)
    out_re = jnp.einsum("kn,nzq->kzq", cos_cells, part_re, precision=HIGHEST) + jnp.einsum(
        "kn,nzq->kzq", sin_cells, part_im, precision=HIGHEST
    )
    out_im = jnp.einsum("kn,nzq->kzq", cos_cells, part_im, precision=HIGHEST) - jnp.einsum(
        "kn,nzq->kzq", sin_cells, part_re, precision=HIGHEST
    )
    xspec_re = out_re
    xspec_im = out_im
    slab_starts = jnp.arange(trk_count, dtype=jnp.int32)[:, None] * slab_depth
    forward_places = (slab_starts + jnp.arange(slab_depth + 1, dtype=jnp.int32)[None, :]).reshape(
        -1
    )
    cos_fwd, sin_fwd = wave_table(freq_all, forward_places, doubled)
    part_re = lax.all_to_all(xspec_re, "trk", split_axis=0, concat_axis=1, tiled=True)
    part_im = lax.all_to_all(xspec_im, "trk", split_axis=0, concat_axis=1, tiled=True)
    out_re = jnp.einsum("kn,xnq->xkq", cos_fwd, part_re, precision=HIGHEST) + jnp.einsum(
        "kn,xnq->xkq", sin_fwd, part_im, precision=HIGHEST
    )
    out_im = jnp.einsum("kn,xnq->xkq", cos_fwd, part_im, precision=HIGHEST) - jnp.einsum(
        "kn,xnq->xkq", sin_fwd, part_re, precision=HIGHEST
    )
    zspec_re = out_re
    zspec_im = out_im
    scaled_re = zspec_re * green_hat
    scaled_im = zspec_im * green_hat
    back_places = (slab_starts - 1 + jnp.arange(slab_depth + 3, dtype=jnp.int32)[None, :]).reshape(
        -1
    )
    inside = ((back_places >= 0) & (back_places < NG)).astype(jnp.float32) / doubled
    cos_back, sin_back = wave_table(back_places, freq_all, doubled)
    cos_back = cos_back * inside[:, None]
    sin_back = sin_back * inside[:, None]
    plane_re = jnp.einsum("nk,xkq->xnq", cos_back, scaled_re, precision=HIGHEST) - jnp.einsum(
        "nk,xkq->xnq", sin_back, scaled_im, precision=HIGHEST
    )
    plane_im = jnp.einsum("nk,xkq->xnq", sin_back, scaled_re, precision=HIGHEST) + jnp.einsum(
        "nk,xkq->xnq", cos_back, scaled_im, precision=HIGHEST
    )
    cos_inverse = jnp.transpose(cos_cells) / doubled
    sin_inverse = jnp.transpose(sin_cells) / doubled
    part_re = lax.all_to_all(plane_re, "trk", split_axis=1, concat_axis=0, tiled=True)
    part_im = lax.all_to_all(plane_im, "trk", split_axis=1, concat_axis=0, tiled=True)
    out_re = jnp.einsum("nk,kzq->nzq", cos_inverse, part_re, precision=HIGHEST) - jnp.einsum(
        "nk,kzq->nzq", sin_inverse, part_im, precision=HIGHEST
    )
    out_im = jnp.einsum("nk,kzq->nzq", sin_inverse, part_re, precision=HIGHEST) + jnp.einsum(
        "nk,kzq->nzq", cos_inverse, part_im, precision=HIGHEST
    )
    cos_final = cos_cells / doubled
    sin_final = sin_cells / doubled
    part_re = lax.all_to_all(out_re, "sub", split_axis=0, concat_axis=2, tiled=True)
    part_im = lax.all_to_all(out_im, "sub", split_axis=0, concat_axis=2, tiled=True)
    block_rows = jnp.einsum("xzk,ky->xzy", part_re, cos_final, precision=HIGHEST) - jnp.einsum(
        "xzk,ky->xzy", part_im, sin_final, precision=HIGHEST
    )
    potential = lax.all_gather(block_rows, "sub", axis=0, tiled=True)
    middle = potential[:, 1 : slab_depth + 2]
    around_x = jnp.pad(middle, ((1, 1), (0, 0), (0, 0)))
    field_x = -0.5 * (around_x[2:] - around_x[:-2])
    around_y = jnp.pad(middle, ((0, 0), (0, 0), (1, 1)))
    field_y = -0.5 * (around_y[:, :, 2:] - around_y[:, :, :-2])
    field_z = -0.5 * (potential[:, 2 : slab_depth + 3] - potential[:, : slab_depth + 1])
    field_table = jnp.stack([field_x, field_y, field_z], axis=2).reshape(NG * depth, 3 * NG)

    def sample_step(carry, items):
        bx, by, bz, boff = items
        plane_xz, weight_y = block_weights(bx, by, bz, boff[0], boff[1], boff[2], depth)
        lines = jnp.dot(plane_xz, field_table, precision=HIGHEST).reshape(bx.shape[0], 3, NG)
        return (carry, jnp.sum(lines * weight_y[:, None, :], axis=2))

    _, sampled = lax.scan(
        sample_step, jnp.zeros((), jnp.float32), (blocked_x, blocked_y, blocked_z, blocked_off)
    )
    kick = sampled.reshape(count_here, 3).transpose(1, 0)
    push_x, push_y = multipole_push(particle_cells, offsets, orders, strengths)
    push = jnp.stack([push_x, push_y, jnp.zeros_like(push_x)])
    new_momenta = momenta + kick + push
    new_coords = particle_cells.astype(jnp.float32) + offsets + new_momenta
    return (new_coords, new_momenta)


def halves(values):
    upper = values.astype(jnp.bfloat16)
    return (upper, (values - upper.astype(jnp.float32)).astype(jnp.bfloat16))


def table_halves(table):
    upper = table.astype(ml_dtypes.bfloat16)
    lower = (table - upper.astype(np.float64)).astype(ml_dtypes.bfloat16)
    return (jnp.asarray(upper), jnp.asarray(lower))


def mm(left, right):
    return jnp.dot(left, right, preferred_element_type=jnp.float32)


def mm_t(left, right):
    return lax.dot_general(left, right, (((1,), (1,)), ((), ())), preferred_element_type=jnp.float32)


def mm3(left, right):
    return mm(left[0], right[0]) + (mm(left[0], right[1]) + mm(left[1], right[0]))


def turn_blocks(parts):
    lanes = lax.broadcasted_iota(jnp.int32, parts[0].shape, 1)
    low = lanes < 64
    even = (lanes // 32) % 2 == 0
    pairs = []
    for first, second in ((parts[0], parts[2]), (parts[1], parts[3])):
        pairs.append(
            (
                jnp.where(low, first, pltpu.roll(second, 64, 1)),
                jnp.where(low, pltpu.roll(first, 64, 1), second),
            )
        )
    result = []
    for half in (0, 1):
        first, second = pairs[0][half], pairs[1][half]
        result.append(jnp.where(even, first, pltpu.roll(second, 32, 1)))
        result.append(jnp.where(even, pltpu.roll(first, 96, 1), second))
    return result


def tent(places, cells, fraction):
    away = places - cells
    return jnp.where(away == 0, 1.0 - fraction, jnp.where(away == 1, fraction, 0.0))


QUAD = 4
PLANES = 5
WIDE = 32
GROUPS = 9
SLOTS = 4 * GROUPS
FWD_ROWS = GROUPS * 2 * QUAD
BACK_ROWS = FWD_ROWS + 16
TOP_ROWS = 16 * 16 + 32
LOT = 512
CUTS = (0, 12, WIDE)
SORT_ROWS = 392
LIST_ROWS = SORT_ROWS + NG
SPAN = 3
PACK = 256
BIG = 56 * 1024 * 1024


def long_row(ref, start, count):
    return jnp.concatenate([ref[pl.ds(start + n, 1), :] for n in range(count)], axis=1)


def deposit_lots(acc_ref, rows_ref, base, ends_ref, me, bottom, top):
    span = LOT // NG
    ids = lax.broadcasted_iota(jnp.int32, (NG, LOT), 0).astype(jnp.float32)

    def step(lot, carry):
        low = ends_ref[0, lot * span].astype(jnp.int32) - me * QUAD
        high = ends_ref[1, lot * span + span - 1].astype(jnp.int32) + 1 - me * QUAD
        low = jnp.maximum(low, bottom)
        high = jnp.minimum(high, top)
        size = min(SPAN, top - bottom + 1)

        @pl.when(low <= high)
        def _():
            cell_x, cell_y, cell_z, off_x, off_y, off_z = [
                long_row(rows_ref, base + which * 64 + lot * span, span) for which in range(6)
            ]
            right = jnp.concatenate(halves(tent(ids, cell_x, off_x)), axis=0)
            weight_y = tent(ids, cell_y, off_y)

            def window(turn, inner):
                start = low + turn * size
                away = (start + me * QUAD).astype(jnp.float32) - cell_z
                left = []
                for z in range(size):
                    left.extend(halves(weight_y * tent(away + float(z), 0.0, off_z)))
                lines = mm_t(jnp.concatenate(left, axis=0), right)
                for z in range(size):
                    place = pl.ds(pl.multiple_of((start + z - bottom) * NG, NG), NG)
                    part = lines[2 * z * NG : (2 * z + 2) * NG]
                    acc_ref[place, :] += part[0:NG] + part[NG : 2 * NG]
                return inner

            lax.fori_loop(0, (high - low) // size + 1, window, 0)

        return carry

    lax.fori_loop(0, 64 // span, step, 0)


ACC_PLANES = QUAD + SPAN - 1
ENDS = slice(6 * 64, 6 * 64 + 8)


def deposit_own(place_ref, rows_ref, acc_ref, ends_ref, sem):
    ends = pltpu.make_async_copy(rows_ref.at[ENDS, :], ends_ref, sem)
    ends.start()
    acc_ref[...] = jnp.zeros_like(acc_ref)
    ends.wait()
    deposit_lots(acc_ref, rows_ref, 0, ends_ref, place_ref[0], 0, QUAD - 1)


def fetch_ends(rows_ref, ends_ref, sem):
    copies = [
        pltpu.make_async_copy(
            rows_ref.at[n * LIST_ROWS + ENDS.start : n * LIST_ROWS + ENDS.stop, :],
            ends_ref.at[n],
            sem.at[n],
        )
        for n in range(4)
    ]
    for copy in copies:
        copy.start()
    return copies


def deposit_rest(place_ref, rows_ref, start_ref, dens_ref, acc_ref, ends_ref, sem):
    copies = fetch_ends(rows_ref, ends_ref, sem)
    acc_ref[...] = start_ref[...]
    for copy in copies:
        copy.wait()
    me = place_ref[0]

    def each(turn, carry):
        n = lax.rem(me + turn, 4)
        deposit_lots(acc_ref, rows_ref, n * LIST_ROWS, ends_ref.at[n], me, 0, QUAD - 1)
        return carry

    lax.fori_loop(1, 4, each, 0)
    live = slice(0, QUAD * NG)
    dens_ref[...] = acc_ref[live, 0:NG] + acc_ref[live, NG : 2 * NG]


def forward_planes(lower_ref, dens_ref, list_ref, ty_hi, ty_lo, tx_hi, tx_lo, out_ref, left_ref, right_ref):
    half = 16 * GROUPS
    for z in range(QUAD):
        plane = dens_ref[z * NG : (z + 1) * NG, :]
        if z == 0:
            rims = [
                list_ref[n * LIST_ROWS + SORT_ROWS : (n + 1) * LIST_ROWS, :] for n in range(4)
            ]
            rim = (rims[0] + rims[1]) + (rims[2] + rims[3])
            plane = plane + jnp.where(lower_ref[0] > 0, rim, 0.0)
        lines = mm3((ty_hi[...], ty_lo[...]), halves(plane))
        real, imag = lines[0:half], lines[half : 2 * half]
        left_ref[pl.ds(2 * z, half, stride=8), :] = real
        right_ref[pl.ds(2 * z, half, stride=8), :] = imag
        left_ref[pl.ds(2 * z + 1, half, stride=8), :] = imag
        right_ref[pl.ds(2 * z + 1, half, stride=8), :] = -real
    for s in range(4):
        whole = []
        for i in range(4):
            start = (i * 4 + s) * FWD_ROWS
            piece = slice(start, start + FWD_ROWS)
            lines = jnp.concatenate([left_ref[piece, :], right_ref[piece, :]], axis=1)
            whole.append(mm3(halves(lines), (tx_hi[...], tx_lo[...])))
        for th in range(2):
            turned = turn_blocks([part[:, th * NG : (th + 1) * NG] for part in whole])
            for t in range(4):
                out_ref[(th * 4 + t) * 4 + s] = turned[t]


def green_send(lines_ref, first_ref, second_ref, row_ref, edge_ref, last_ref):
    fars = (first_ref, second_ref)
    for k in range(1, WIDE):
        piece = int(k >= CUTS[1])
        fars[piece][k - CUTS[piece]] = lines_ref[WIDE - k, WIDE : 2 * WIDE, :]
        edge_ref[k : k + 1, :] = lines_ref[WIDE - k, 0:1, :]
    first_ref[0] = lines_ref[0, WIDE : 2 * WIDE, :]
    edge_ref[0:1, :] = lines_ref[0, 0:1, :]
    row_ref[...] = lines_ref[0, WIDE : 2 * WIDE, :]
    last_ref[...] = lines_ref[0, 0:8, :]


def green_pairs(
    own_ref, first_ref, second_ref, row_ref, edge_ref, last_ref, pick_ref, out_ref, *parts
):
    for side in range(2):
        lanes = slice(side * NG, (side + 1) * NG)
        parts[side][...] = own_ref[:, lanes]
        for piece, ref in enumerate((first_ref, second_ref)):
            parts[2 + side][CUTS[piece] * WIDE : CUTS[piece + 1] * WIDE, :] = ref[:, lanes]
        parts[2 + side][0:WIDE, :] = row_ref[:, lanes]
    first = lax.broadcasted_iota(jnp.int32, (WIDE, 2 * NG), 0) == 0
    edge = jnp.where(first, jnp.broadcast_to(last_ref[0:1, :], (WIDE, 2 * NG)), edge_ref[...])

    def pull(refs, start, stride):
        return jnp.concatenate(
            [ref[pl.ds(start, WIDE, stride=stride), :] for ref in refs], axis=1
        )

    for group in range(GROUPS):
        near, away = [], []
        for i in range(4):
            j = group * 4 + i
            if j > WIDE:
                near.append(jnp.zeros((WIDE, 2 * NG), jnp.float32))
                away.append(jnp.zeros((WIDE, 2 * NG), jnp.float32))
                continue
            near.append(pull(parts[0:2], j, 2 * WIDE))
            away.append(edge if j == 0 else pull(parts[2:4], WIDE - j, WIDE))
        both = jnp.concatenate(
            [jnp.concatenate(near, axis=0), jnp.concatenate(away, axis=0)], axis=1
        )
        high = both.astype(jnp.bfloat16)
        left = both - high.astype(jnp.float32)
        mid = left.astype(jnp.bfloat16)
        low = (left - mid.astype(jnp.float32)).astype(jnp.bfloat16)
        pick = pick_ref[...]
        out_ref[:, group * NG : (group + 1) * NG] = 0.5 * (
            mm_t(pick, high) + (mm_t(pick, mid) + mm_t(pick, low))
        )


def spectrum_stage(in_ref, green_ref, wf_hi, wf_lo, wb_hi, wb_lo, out_ref):
    slabs = in_ref.shape[0]
    half = 2 * NG
    for first in range(0, GROUPS, 2):
        groups = [g for g in (first, first + 1) if g < GROUPS]
        data = [in_ref[:, g * 8 : (g + 1) * 8, :].reshape(slabs * 8, NG) for g in groups]
        data = data[0] if len(data) == 1 else jnp.concatenate(data, axis=1)
        spec = mm3((wf_hi[...], wf_lo[...]), halves(data))
        green = green_ref[:, first * NG : (first + len(groups)) * NG]
        scaled = jnp.concatenate([spec[0:half] * green, spec[half : 2 * half] * green], axis=0)
        back = mm3((wb_hi[...], wb_lo[...]), halves(scaled))
        for place, g in enumerate(groups):
            part = back[:, place * NG : (place + 1) * NG]
            for slab in range(slabs):
                row = slab * BACK_ROWS + g * 8
                out_ref[row : row + 8, :] = part[slab * 8 : slab * 8 + 8]
            for c in range(2):
                start = slabs * (8 + c)
                top = part[start : start + slabs]
                if g < GROUPS - 1:
                    out_ref[pl.ds(FWD_ROWS + 2 * g + c, slabs, stride=BACK_ROWS), :] = top
                else:
                    spot = pl.ds(8 * g + c, slabs, stride=BACK_ROWS)
                    lanes = lax.broadcasted_iota(jnp.int32, (slabs, NG), 1)
                    moved = pltpu.roll(top, WIDE, 1)
                    mine = (lanes >= WIDE) & (lanes < 2 * WIDE)
                    out_ref[spot, :] = jnp.where(mine, moved, out_ref[spot, :])


def inverse_planes(
    in_ref, tx_hi, tx_lo, ty_hi, ty_lo, te_hi, te_lo, out_ref, mid_cos, mid_sin, top_cos, top_sin
):
    extra = BACK_ROWS - FWD_ROWS
    for s in range(4):
        main, rest, last = [[], [], [], []], [[], [], [], []], []
        for th in range(2):
            parts = [in_ref[(th * 4 + t) * 4 + s, 0:FWD_ROWS, :] for t in range(4)]
            tops = [in_ref[(th * 4 + t) * 4 + s, FWD_ROWS:BACK_ROWS, :] for t in range(4)]
            for i, block in enumerate(turn_blocks(parts)):
                main[i].append(block)
            for i, block in enumerate(turn_blocks(tops)):
                rest[i].append(block)
            tail = [pltpu.roll(part[FWD_ROWS - 8 :], NG - WIDE, 1) for part in parts]
            last.append(turn_blocks(tail)[0])
        for i in range(4):
            row = (i * 4 + s) * FWD_ROWS
            lines = jnp.concatenate(main[i], axis=1)
            lines = mm3(halves(lines), (tx_hi[...], tx_lo[...]))
            mid_cos[row : row + FWD_ROWS, :] = lines[:, 0:NG]
            mid_sin[row : row + FWD_ROWS, :] = lines[:, NG : 2 * NG]
            row = (i * 4 + s) * extra
            lines = jnp.concatenate(rest[i], axis=1)
            lines = mm3(halves(lines), (tx_hi[...], tx_lo[...]))
            top_cos[row : row + extra, :] = lines[:, 0:NG]
            top_sin[row : row + extra, :] = lines[:, NG : 2 * NG]
        row = 16 * extra + 8 * s
        lines = mm3(halves(jnp.concatenate(last, axis=1)), (tx_hi[...], tx_lo[...]))
        top_cos[row : row + 8, :] = lines[:, 0:NG]
        top_sin[row : row + 8, :] = lines[:, NG : 2 * NG]

    def finish(cos_ref, sin_ref, start, count, stride, table):
        real, imag = pl.ds(start, count, stride=stride), pl.ds(start + 1, count, stride=stride)
        lines = jnp.concatenate(
            [cos_ref[real, :] - sin_ref[imag, :], sin_ref[real, :] + cos_ref[imag, :]], axis=0
        )
        return mm3((table[0][...], table[1][...]), halves(lines))

    for z in range(QUAD):
        out_ref[z] = finish(mid_cos, mid_sin, 2 * z, 16 * GROUPS, 8, (ty_hi, ty_lo))
    out_ref[QUAD] = finish(top_cos, top_sin, 0, TOP_ROWS // 2, 2, (te_hi, te_lo))


SORT_BITS = 13
DEAD = 100


def sort_network(items, rolled=False):
    shape = (8, NG)
    lanes = lax.broadcasted_iota(jnp.int32, shape, 1)
    subs = lax.broadcasted_iota(jnp.int32, shape, 0)
    base = subs * 8 + (lanes // 64) * 64 + (lanes % 64) * 128

    def exchange(items, others, bit, size):
        fresh = [[] for _ in items]
        for v in range(8):
            rank = base + v
            keep = (((rank >> bit) ^ (rank >> (size + 1))) & 1) == 0
            take = (others[0][v] < items[0][v]) == keep
            for n in range(len(items)):
                fresh[n].append(jnp.where(take, others[n][v], items[n][v]))
        return fresh

    def near_stage(items, bit, size):
        others = [[item[v ^ (1 << bit)] for v in range(8)] for item in items]
        return exchange(items, others, bit, size)

    def far_stage(items, bit, size, index, axis):
        others = [[jnp.take_along_axis(value, index, axis=axis) for value in item] for item in items]
        return exchange(items, others, bit, size)

    def far_bit(items, bit, size):
        if bit < 3:
            return near_stage(items, bit, size)
        if bit < 6:
            return far_stage(items, bit, size, subs ^ (1 << (bit - 3)), 0)
        return far_stage(items, bit, size, lanes ^ (64 if bit == 6 else 1 << (bit - 7)), 1)

    for size in range(3 if rolled else SORT_BITS):
        for bit in range(size, -1, -1):
            items = far_bit(items, bit, size)
    if not rolled:
        return items

    def merge(size, items):
        def lane_step(n, items):
            bit = size - n
            index = lanes ^ jnp.where(bit == 6, 64, 1 << jnp.maximum(bit - 7, 0))
            return far_stage(items, bit, size, index, 1)

        def sub_step(n, items):
            bit = jnp.minimum(size, 5) - n
            return far_stage(items, bit, size, subs ^ (1 << (bit - 3)), 0)

        items = lax.fori_loop(0, jnp.maximum(size - 5, 0), lane_step, items)
        items = lax.fori_loop(0, jnp.minimum(size, 5) - 2, sub_step, items)
        for bit in (2, 1, 0):
            items = near_stage(items, bit, size)
        return items

    return lax.fori_loop(3, SORT_BITS, merge, items)


def laid_out(values):
    turned = jnp.transpose(jnp.concatenate(values, axis=0), (1, 0))
    return jnp.concatenate([turned[0:64], turned[64:128]], axis=1)


def sort_labels(v):
    lanes = lax.broadcasted_iota(jnp.int32, (8, NG), 1)
    subs = lax.broadcasted_iota(jnp.int32, (8, NG), 0)
    return (subs + v * 8) * 128 + (lanes // 64) * 64 + (lanes % 8) * 8 + (lanes // 8) % 8


def square_up(cells_ref, offs_ref, ints_ref, flts_ref):
    for k in range(64):
        lanes = slice(k * NG, (k + 1) * NG)
        for d in range(3):
            ints_ref[d, k : k + 1, :] = cells_ref[d : d + 1, lanes]
            flts_ref[d, k : k + 1, :] = offs_ref[d : d + 1, lanes]


def sort_by_z(
    place_ref,
    live_ref,
    cells_ref,
    offs_ref,
    out_ref,
    rim_ref,
    ints_ref,
    flts_ref,
    top_ref,
    ends_ref,
    sem,
):
    square_up(cells_ref, offs_ref, ints_ref, flts_ref)
    lanes = lax.broadcasted_iota(jnp.int32, (8, NG), 1)
    subs = lax.broadcasted_iota(jnp.int32, (8, NG), 0)
    keys, packs, offs = [], [], [[], [], []]
    for v in range(8):
        rows = slice(v * 8, v * 8 + 8)
        alive = (subs + v * 8) * NG + lanes < live_ref[0]
        cell_z = jnp.where(alive, ints_ref[2, rows, :] - place_ref[0], DEAD)
        keys.append(cell_z * 8192 + sort_labels(v))
        packs.append(ints_ref[0, rows, :] * NG + ints_ref[1, rows, :])
        for d in range(3):
            offs[d].append(flts_ref[d, rows, :])
    items = [laid_out(item) for item in sort_network([keys, packs] + offs)]
    cell_z = (items[0] >> 13).astype(jnp.float32)
    out_ref[0:64, :] = (items[1] >> 7).astype(jnp.float32)
    out_ref[64:128, :] = (items[1] & (NG - 1)).astype(jnp.float32)
    out_ref[128:192, :] = cell_z
    for d in range(3):
        out_ref[192 + 64 * d : 256 + 64 * d, :] = items[2 + d]
    ends = jnp.transpose(cell_z, (1, 0))
    ends = jnp.concatenate([ends[0:1], ends[NG - 1 : NG], jnp.zeros((6, 64), jnp.float32)], axis=0)
    out_ref[384:392, :] = jnp.concatenate([ends, ends], axis=1)
    fetch = pltpu.make_async_copy(out_ref.at[ENDS, :], ends_ref, sem)
    fetch.start()
    top_ref[...] = jnp.zeros_like(top_ref)
    fetch.wait()
    deposit_lots(top_ref, out_ref, 0, ends_ref, 0, 4 * QUAD, 4 * QUAD)
    rim_ref[...] = top_ref[:, 0:NG] + top_ref[:, NG : 2 * NG]


def sort_by_y(place_ref, cells_ref, offs_ref, out_int, out_off, ints_ref, flts_ref):
    square_up(cells_ref, offs_ref, ints_ref, flts_ref)
    keys, packs, offs = [], [], [[], [], []]
    for v in range(8):
        rows = slice(v * 8, v * 8 + 8)
        keys.append(ints_ref[1, rows, :] * 8192 + sort_labels(v))
        packs.append(ints_ref[0, rows, :] * 64 + ints_ref[2, rows, :] - place_ref[0])
        for d in range(3):
            offs[d].append(flts_ref[d, rows, :])
    items = [laid_out(item) for item in sort_network([keys, packs] + offs, rolled=True)]
    cell_y = items[0] >> 13
    out_int[0:64, :] = cell_y
    out_int[64:128, :] = items[0] & 8191
    out_int[128:192, :] = items[1] >> 6
    out_int[192:256, :] = items[1] & 63
    for d in range(3):
        out_off[d * 64 : d * 64 + 64, :] = items[2 + d]
    ends = jnp.transpose(cell_y, (1, 0))
    ends = jnp.concatenate([ends[0:1], ends[NG - 1 : NG], jnp.zeros((6, 64), jnp.int32)], axis=0)
    out_int[256:264, :] = jnp.concatenate([ends, ends], axis=1)


def sample(
    place_ref,
    own_ref,
    core_ref,
    chip_ref,
    last_ref,
    int_ref,
    off_ref,
    mom_ref,
    push_ref,
    home_ref,
    coord_ref,
    out_ref,
    pot_ref,
    field_ref,
    kick_ref,
    ends_ref,
    sem,
):
    ends = pltpu.make_async_copy(int_ref.at[256:264, :], ends_ref, sem)
    ends.start()
    me = place_ref[0]
    for turn, ref in enumerate((own_ref, core_ref, chip_ref, last_ref)):
        pot_ref[pl.ds((me ^ turn) * PLANES, PLANES)] = ref[...]
    depth = field_ref.shape[0] // 3
    rows = lax.broadcasted_iota(jnp.int32, (NG, NG), 0)
    lanes = lax.broadcasted_iota(jnp.int32, (NG, NG), 1)
    blank = jnp.zeros((8, NG), jnp.float32)

    def fields(z, carry):
        plane = pot_ref[z + 1]
        right = jnp.where(lanes == NG - 1, 0.0, pltpu.roll(plane, NG - 1, 1))
        left = jnp.where(lanes == 0, 0.0, pltpu.roll(plane, 1, 1))
        field_ref[z, 0:NG, :] = -0.5 * (right - left)
        right = jnp.where(rows == NG - 1, 0.0, pltpu.roll(plane, NG - 1, 0))
        left = jnp.where(rows == 0, 0.0, pltpu.roll(plane, 1, 0))
        field_ref[depth + z, 0:NG, :] = -0.5 * (right - left)
        field_ref[2 * depth + z, 0:NG, :] = -0.5 * (pot_ref[z + 2] - pot_ref[z])
        for d in range(3):
            field_ref[d * depth + z, NG : NG + 8, :] = blank
        return carry

    lax.fori_loop(0, depth, fields, 0)
    x_ids = lax.broadcasted_iota(jnp.int32, (NG, PACK), 0)
    z_ids = lax.broadcasted_iota(jnp.int32, (24, PACK), 0)
    y_ids = lax.broadcasted_iota(jnp.int32, (8, PACK), 0)
    span = PACK // NG
    ends.wait()

    def pack_step(pack, carry):
        first = pack * span
        cell_y, cell_x, cell_z = [
            long_row(int_ref, which * 64 + first, span) for which in (0, 2, 3)
        ]
        off_x, off_y, off_z = [long_row(off_ref, which * 64 + first, span) for which in range(3)]
        weight_x = halves(tent(x_ids, cell_x, off_x))
        tall = [jnp.concatenate([part, part], axis=0) for part in weight_x]
        weight_z = tent(z_ids, cell_z, off_z)
        low = ends_ref[0, first]
        high = ends_ref[1, first + span - 1] + 1

        def chunk(turn):
            start = low + turn * 8
            weight_y = tent(y_ids + start, cell_y, off_y)
            table = field_ref[:, pl.ds(start, 8), :].reshape(3 * depth * 8, NG)
            part = jnp.concatenate(halves(table), axis=1)
            lines = mm(part, tall[0]) + mm(part, tall[1])
            fresh = []
            for d in range(3):
                total = lines[d * depth * 8 : d * depth * 8 + 8] * weight_z[0:1]
                for z in range(1, depth):
                    row = (d * depth + z) * 8
                    total = total + lines[row : row + 8] * weight_z[z : z + 1]
                fresh.append(jnp.sum(total * weight_y, axis=0, keepdims=True))
            return fresh

        for d, kick in enumerate(chunk(0)):
            for n in range(span):
                kick_ref[d, pl.ds(first + n, 1), :] = kick[:, n * NG : (n + 1) * NG]
        return (low, high, first, chunk)

    def pair_step(pair, carry):
        packs = [pack_step(4 * pair + n, 0) for n in range(4)]
        for low, high, first, chunk in packs:

            def more(turn, inner):
                for d, kick in enumerate(chunk(turn)):
                    for n in range(span):
                        kick_ref[d, pl.ds(first + n, 1), :] += kick[:, n * NG : (n + 1) * NG]
                return inner

            lax.fori_loop(1, (high - low) // 8 + 1, more, 0)
        return carry

    lax.fori_loop(0, 16 // span, pair_step, 0)
    items = [[int_ref[64 + v * 8 : v * 8 + 72, :] for v in range(8)]]
    for d in range(3):
        items.append([kick_ref[d, v * 8 : v * 8 + 8, :] for v in range(8)])
    items = sort_network(items)
    for d in range(3):
        kick = laid_out(items[1 + d])
        for k in range(64):
            out_ref[d : d + 1, k * NG : (k + 1) * NG] = kick[k : k + 1, :]
    fresh = (mom_ref[...] + out_ref[...]) + push_ref[...]
    out_ref[...] = fresh
    coord_ref[...] = home_ref[...] + fresh


def plane_tables(trk_count, sub_count, unit_charge):
    doubled = 2 * NG
    width = doubled // sub_count
    slots = np.arange(4)[:, None, None] + 4 * np.arange(GROUPS)[None, None, :]
    slots = np.broadcast_to(slots, (4, sub_count, GROUPS))
    freq = width * np.arange(sub_count)[None, :, None] + slots
    used = (slots <= width // 2).astype(np.float64)
    share = used * np.where((slots == 0) | (slots == width // 2), 1.0, 2.0)
    cells = np.arange(NG)
    turn = 2.0 * np.pi / doubled
    angle = turn * ((freq.reshape(-1)[:, None] * cells[None, :]) % doubled)
    used = used.reshape(-1)[:, None]
    share_line = share.reshape(-1)[:, None]
    ty = np.concatenate([np.cos(angle) * used, -np.sin(angle) * used], axis=0) * unit_charge
    back = np.concatenate([np.cos(angle) * share_line, -np.sin(angle) * share_line], axis=0)
    ty_back = back.T / doubled
    pieces = back.reshape(2, 4 * sub_count, GROUPS, NG)
    tail = np.zeros((2, sub_count, 4, NG))
    tail[:, :, 0] = pieces[:, :sub_count, GROUPS - 1]
    body = pieces[:, :, : GROUPS - 1].reshape(2, -1, NG)
    pieces = np.concatenate([body, tail.reshape(2, -1, NG)], axis=1)
    te_back = pieces.reshape(-1, NG).T / doubled
    angle = turn * ((cells[:, None] * np.arange(doubled)[None, :]) % doubled)
    tx = np.concatenate([np.cos(angle), np.sin(angle)], axis=0)
    tx_back = np.concatenate([np.cos(angle).T, np.sin(angle).T], axis=1) / doubled
    slabs = trk_count * sub_count
    angle = turn * ((np.arange(doubled)[:, None] * cells[None, :]) % doubled)
    cos, sin = np.cos(angle), np.sin(angle)
    wf = np.stack(
        [np.stack([cos, sin], axis=2), np.stack([-sin, cos], axis=2)], axis=0
    ).reshape(2 * doubled, 2 * NG)
    slab = np.arange(slabs)
    planes = (
        (slab // sub_count * QUAD * sub_count - 1 + PLANES * (slab % sub_count))[:, None]
        + np.arange(PLANES)[None, :]
    )
    inside = ((planes >= 0) & (planes < NG)).astype(np.float64)[:, :, None] / doubled
    angle = turn * ((planes[:, :, None] * np.arange(doubled)[None, None, :]) % doubled)
    cos, sin = np.cos(angle) * inside, np.sin(angle) * inside
    wb = np.stack([np.concatenate([cos, -sin], axis=2), np.concatenate([sin, cos], axis=2)], axis=2)
    wb = np.concatenate(
        [
            wb[:, :QUAD].reshape(slabs * QUAD * 2, 2 * doubled),
            wb[:, QUAD, 0],
            wb[:, QUAD, 1],
        ],
        axis=0,
    )
    pick = np.zeros((doubled, 2 * doubled))
    line = np.arange(doubled)
    pick[line, line] = 1.0
    pick[line, doubled + (-line) % doubled] = 1.0
    return ty, tx, wf, wb, tx_back, ty_back, te_back, pick


def run(body, shapes, scratch, *args, scalars=0):
    out_shape = tuple(jax.ShapeDtypeStruct(*shape) for shape in shapes)
    space = pl.BlockSpec(memory_space=pltpu.VMEM)
    result = pl.pallas_call(
        body,
        out_shape=out_shape,
        in_specs=[pl.BlockSpec(memory_space=pltpu.SMEM)] * scalars + [space] * (len(args) - scalars),
        out_specs=tuple(space for _ in out_shape),
        scratch_shapes=[
            pltpu.VMEM(*shape) if isinstance(shape, tuple) else shape for shape in scratch
        ],
        compiler_params=pltpu.CompilerParams(vmem_limit_bytes=BIG),
    )(*args)
    return result


def spread_device(particle_cells, offsets, momenta, live_counts, green_hat, orders, strengths):
    f32 = jnp.float32
    trk_count = lax.axis_size("trk")
    sub_count = lax.axis_size("sub")
    slabs = trk_count * sub_count
    slab_depth = NG // trk_count
    count_here = particle_cells.shape[1]
    unit_charge = float(NG**3) / float(count_here * slabs)
    both = ("trk", "sub")
    tables = plane_tables(trk_count, sub_count, unit_charge)
    ty, tx, wf, wb, tx_back, ty_back, te_back = [table_halves(table) for table in tables[:7]]
    pick = jnp.asarray(tables[7].astype(ml_dtypes.bfloat16))

    def flat(t, s):
        return (t % trk_count) * sub_count + s % sub_count

    pairs = [(t, s) for t in range(trk_count) for s in range(sub_count)]
    width = green_hat.shape[2]
    lines = jnp.transpose(green_hat, (0, 2, 1))
    half = width // 2
    first, second, row, edge, last = run(
        green_send,
        [((CUTS[n + 1] - CUTS[n], half, 2 * NG), f32) for n in range(2)]
        + [
            ((half, 2 * NG), f32),
            ((width // 2, 2 * NG), f32),
            ((8, 2 * NG), f32),
        ],
        [],
        lines,
    )

    def mirrored(value, trk_shift, sub_shift):
        moves = [
            (flat(t, s), flat(trk_count - trk_shift - t, sub_count - sub_shift - s))
            for t, s in pairs
        ]
        return lax.ppermute(value, both, moves)

    first = mirrored(first, 1, 1)

    def partner(value, turn):
        return lax.ppermute(value, both, [(flat(t, s), flat(t, s ^ turn)) for t, s in pairs])

    place = lax.axis_index("sub").reshape(1)
    base = (lax.axis_index("trk") * slab_depth).reshape(1)
    square = [((3, 64, NG), jnp.int32), ((3, 64, NG), f32)]
    rows, rim = run(
        sort_by_z,
        [((SORT_ROWS, NG), f32), ((NG, NG), f32)],
        square
        + [((NG, 2 * NG), f32), pltpu.SMEM((8, NG), f32), pltpu.SemaphoreType.DMA],
        base,
        live_counts,
        particle_cells,
        offsets,
        scalars=2,
    )
    rim = lax.ppermute(rim, both, [(flat(t, s), flat(t + 1, s)) for t, s in pairs])
    acc_shape = ((ACC_PLANES * NG, 2 * NG), f32)
    (start,) = run(
        deposit_own,
        [acc_shape],
        [pltpu.SMEM((8, NG), f32), pltpu.SemaphoreType.DMA],
        place,
        rows,
        scalars=1,
    )
    rim, start, first, second, row, edge, last = lax.optimization_barrier(
        (rim, start, first, second, row, edge, last)
    )
    shared = lax.all_gather(jnp.concatenate([rows, rim], axis=0), "sub", axis=0, tiled=True)
    second = mirrored(second, 1, 1)
    row = mirrored(row, 0, 1)
    edge = mirrored(edge, 1, 0)
    last = mirrored(last, 0, 0)
    lower = lax.axis_index("trk") > 0
    lower = lower & (lax.axis_index("sub") == 0)
    ends = [pltpu.SMEM((4, 8, NG), f32), pltpu.SemaphoreType.DMA((4,))]
    (dens,) = run(
        deposit_rest,
        [((QUAD * NG, NG), f32)],
        [acc_shape] + ends,
        place,
        shared,
        start,
        scalars=1,
    )
    (sent,) = run(
        forward_planes,
        [((slabs, FWD_ROWS, NG), f32)],
        [((16 * FWD_ROWS, NG), f32)] * 2,
        lower.astype(jnp.int32).reshape(1),
        dens,
        shared,
        *ty,
        *tx,
        scalars=1,
    )
    late_cells, late_offs, first, second, row, edge, last, _ = lax.optimization_barrier(
        (particle_cells, offsets, first, second, row, edge, last, sent)
    )
    got = lax.all_to_all(sent, both, split_axis=0, concat_axis=0, tiled=True)
    ints, offs = run(
        sort_by_y,
        [((264, NG), jnp.int32), ((192, NG), f32)],
        square,
        base,
        late_cells,
        late_offs,
        scalars=1,
    )
    push_x, push_y = multipole_push(late_cells, late_offs, orders, strengths)
    push = jnp.stack([push_x, push_y, jnp.zeros_like(push_x)])
    (green,) = run(
        green_pairs,
        [((2 * NG, GROUPS * NG), f32)],
        [((2 * WIDE * WIDE, NG), f32)] * 2 + [((WIDE * WIDE, NG), f32)] * 2,
        lines.reshape(-1, 2 * NG),
        first.reshape(-1, 2 * NG),
        second.reshape(-1, 2 * NG),
        row,
        edge,
        last,
        pick,
    )
    home = late_cells.astype(f32) + late_offs
    got, ints, offs, push, home = lax.optimization_barrier((got, ints, offs, push, home))
    (sent,) = run(
        spectrum_stage, [((slabs * BACK_ROWS, NG), f32)], [], got, green, *wf, *wb
    )
    got = lax.all_to_all(
        sent.reshape(slabs, BACK_ROWS, NG), both, split_axis=0, concat_axis=0, tiled=True
    )
    (pot,) = run(
        inverse_planes,
        [((PLANES, NG, NG), f32)],
        [((16 * FWD_ROWS, NG), f32)] * 2 + [((TOP_ROWS, NG), f32)] * 2,
        got,
        *tx_back,
        *ty_back,
        *te_back,
    )
    chip_pot = partner(pot, 2)
    core_pot = partner(pot, 1)
    last_pot = partner(chip_pot, 1)
    depth = slab_depth + 1
    coords, fresh = run(
        sample,
        [((3, count_here), f32)] * 2,
        [
            ((sub_count * PLANES, NG, NG), f32),
            ((3 * depth, NG + 8, NG), f32),
            ((3, 64, NG), f32),
            pltpu.SMEM((8, NG), jnp.int32),
            pltpu.SemaphoreType.DMA,
        ],
        place,
        pot,
        core_pot,
        chip_pot,
        last_pot,
        ints,
        offs,
        momenta,
        push,
        home,
        scalars=1,
    )
    return (coords, fresh)


def solution(mesh):
    in_specs = (
        P(None, ("trk", "sub")),
        P(None, ("trk", "sub")),
        P(None, ("trk", "sub")),
        P(("trk", "sub")),
        P("trk", None, "sub"),
        P(),
        P(),
    )
    out_specs = (P(None, ("trk", "sub")), P(None, ("trk", "sub")))
    trk_count, sub_count = mesh.shape["trk"], mesh.shape["sub"]
    fits = sub_count == 4 and trk_count * WIDE == 2 * NG
    body = spread_device if fits else per_device
    return jax.shard_map(
        body, mesh=mesh, in_specs=in_specs, out_specs=out_specs, check_vma=False
    )
```

```python
import math

import jax
import jax.numpy as jnp
import ml_dtypes
import numpy as np
from jax import lax
from jax.experimental import pallas as pl
from jax.experimental.pallas import tpu as pltpu
from jax.sharding import PartitionSpec as P

NG = 128


HIGHEST = lax.Precision.HIGHEST


def multipole_push(particle_cells, offsets, orders, strengths):
    centre = 0.5 * NG
    real_u = (particle_cells[0].astype(jnp.float32) + offsets[0] - centre) / centre
    imag_u = (particle_cells[1].astype(jnp.float32) + offsets[1] - centre) / centre
    power_re = real_u
    power_im = imag_u
    push_x = jnp.zeros_like(real_u)
    push_y = jnp.zeros_like(real_u)
    for degree in range(1, 5):
        coeff = jnp.sum(jnp.where(orders - 1 == degree, strengths, jnp.zeros_like(strengths)))
        push_x = push_x - coeff * power_re
        push_y = push_y + coeff * power_im
        power_re, power_im = (
            power_re * real_u - power_im * imag_u,
            power_re * imag_u + power_im * real_u,
        )
    return (push_x, push_y)


def wave_table(freq_ids, place_ids, length):
    phase_int = freq_ids[:, None] * place_ids[None, :] % length
    angle = 2.0 * math.pi / length * phase_int.astype(jnp.float32)
    return (jnp.cos(angle), jnp.sin(angle))


def tent_weights(cells, fraction, length):
    places = jnp.arange(length, dtype=jnp.int32)
    lower = jnp.where(places[None, :] == cells[:, None], (1.0 - fraction)[:, None], 0.0)
    upper = jnp.where(places[None, :] == cells[:, None] + 1, fraction[:, None], 0.0)
    return lower + upper


def block_weights(cells_x, cells_y, cells_z, frac_x, frac_y, frac_z, depth):
    weight_x = tent_weights(cells_x, frac_x, NG)
    weight_y = tent_weights(cells_y, frac_y, NG)
    weight_z = tent_weights(cells_z, frac_z, depth)
    plane_xz = (weight_x[:, :, None] * weight_z[:, None, :]).reshape(cells_x.shape[0], -1)
    return (plane_xz, weight_y)


def per_device(particle_cells, offsets, momenta, live_counts, green_hat, orders, strengths):
    trk_count = lax.axis_size("trk")
    sub_count = lax.axis_size("sub")
    slab_depth = NG // trk_count
    depth = slab_depth + 1
    doubled = 2 * NG
    count_here = particle_cells.shape[1]
    count_all = count_here * trk_count * sub_count
    row_ids = jnp.arange(count_here, dtype=jnp.int32)
    unit_charge = float(NG**3) / float(count_all)
    charge = jnp.where(
        row_ids < live_counts[0],
        jnp.full((count_here,), unit_charge, jnp.float32),
        jnp.zeros((count_here,), jnp.float32),
    )
    local_z = particle_cells[2] - lax.axis_index("trk") * slab_depth
    block_len = math.gcd(count_here, 512)
    block_count = count_here // block_len
    blocked_x = particle_cells[0].reshape(block_count, block_len)
    blocked_y = particle_cells[1].reshape(block_count, block_len)
    blocked_z = local_z.reshape(block_count, block_len)
    blocked_off = offsets.reshape(3, block_count, block_len).transpose(1, 0, 2)
    blocked_charge = charge.reshape(block_count, block_len)

    def deposit_step(total, items):
        bx, by, bz, boff, bcharge = items
        plane_xz, weight_y = block_weights(bx, by, bz, boff[0], boff[1], boff[2], depth)
        charged = plane_xz * bcharge[:, None]
        return (total + jnp.einsum("pa,py->ay", charged, weight_y, precision=HIGHEST), None)

    start_total = jnp.zeros((NG * depth, NG), jnp.float32)
    deposit, _ = lax.scan(
        deposit_step, start_total, (blocked_x, blocked_y, blocked_z, blocked_off, blocked_charge)
    )
    deposit = deposit.reshape(NG, depth, NG)
    density = lax.psum_scatter(deposit, "sub", scatter_dimension=0, tiled=True)
    freq_all = jnp.arange(doubled, dtype=jnp.int32)
    cell_ids = jnp.arange(NG, dtype=jnp.int32)
    cos_cells, sin_cells = wave_table(freq_all, cell_ids, doubled)
    spec_re = jnp.einsum("xzy,ky->xzk", density, cos_cells, precision=HIGHEST)
    spec_im = -jnp.einsum("xzy,ky->xzk", density, sin_cells, precision=HIGHEST)
    part_re = lax.all_to_all(spec_re, "sub", split_axis=2, concat_axis=0, tiled=True)
    part_im = lax.all_to_all(spec_im, "sub", split_axis=2, concat_axis=0, tiled=True)
    out_re = jnp.einsum("kn,nzq->kzq", cos_cells, part_re, precision=HIGHEST) + jnp.einsum(
        "kn,nzq->kzq", sin_cells, part_im, precision=HIGHEST
    )
    out_im = jnp.einsum("kn,nzq->kzq", cos_cells, part_im, precision=HIGHEST) - jnp.einsum(
        "kn,nzq->kzq", sin_cells, part_re, precision=HIGHEST
    )
    xspec_re = out_re
    xspec_im = out_im
    slab_starts = jnp.arange(trk_count, dtype=jnp.int32)[:, None] * slab_depth
    forward_places = (slab_starts + jnp.arange(slab_depth + 1, dtype=jnp.int32)[None, :]).reshape(
        -1
    )
    cos_fwd, sin_fwd = wave_table(freq_all, forward_places, doubled)
    part_re = lax.all_to_all(xspec_re, "trk", split_axis=0, concat_axis=1, tiled=True)
    part_im = lax.all_to_all(xspec_im, "trk", split_axis=0, concat_axis=1, tiled=True)
    out_re = jnp.einsum("kn,xnq->xkq", cos_fwd, part_re, precision=HIGHEST) + jnp.einsum(
        "kn,xnq->xkq", sin_fwd, part_im, precision=HIGHEST
    )
    out_im = jnp.einsum("kn,xnq->xkq", cos_fwd, part_im, precision=HIGHEST) - jnp.einsum(
        "kn,xnq->xkq", sin_fwd, part_re, precision=HIGHEST
    )
    zspec_re = out_re
    zspec_im = out_im
    scaled_re = zspec_re * green_hat
    scaled_im = zspec_im * green_hat
    back_places = (slab_starts - 1 + jnp.arange(slab_depth + 3, dtype=jnp.int32)[None, :]).reshape(
        -1
    )
    inside = ((back_places >= 0) & (back_places < NG)).astype(jnp.float32) / doubled
    cos_back, sin_back = wave_table(back_places, freq_all, doubled)
    cos_back = cos_back * inside[:, None]
    sin_back = sin_back * inside[:, None]
    plane_re = jnp.einsum("nk,xkq->xnq", cos_back, scaled_re, precision=HIGHEST) - jnp.einsum(
        "nk,xkq->xnq", sin_back, scaled_im, precision=HIGHEST
    )
    plane_im = jnp.einsum("nk,xkq->xnq", sin_back, scaled_re, precision=HIGHEST) + jnp.einsum(
        "nk,xkq->xnq", cos_back, scaled_im, precision=HIGHEST
    )
    cos_inverse = jnp.transpose(cos_cells) / doubled
    sin_inverse = jnp.transpose(sin_cells) / doubled
    part_re = lax.all_to_all(plane_re, "trk", split_axis=1, concat_axis=0, tiled=True)
    part_im = lax.all_to_all(plane_im, "trk", split_axis=1, concat_axis=0, tiled=True)
    out_re = jnp.einsum("nk,kzq->nzq", cos_inverse, part_re, precision=HIGHEST) - jnp.einsum(
        "nk,kzq->nzq", sin_inverse, part_im, precision=HIGHEST
    )
    out_im = jnp.einsum("nk,kzq->nzq", sin_inverse, part_re, precision=HIGHEST) + jnp.einsum(
        "nk,kzq->nzq", cos_inverse, part_im, precision=HIGHEST
    )
    cos_final = cos_cells / doubled
    sin_final = sin_cells / doubled
    part_re = lax.all_to_all(out_re, "sub", split_axis=0, concat_axis=2, tiled=True)
    part_im = lax.all_to_all(out_im, "sub", split_axis=0, concat_axis=2, tiled=True)
    block_rows = jnp.einsum("xzk,ky->xzy", part_re, cos_final, precision=HIGHEST) - jnp.einsum(
        "xzk,ky->xzy", part_im, sin_final, precision=HIGHEST
    )
    potential = lax.all_gather(block_rows, "sub", axis=0, tiled=True)
    middle = potential[:, 1 : slab_depth + 2]
    around_x = jnp.pad(middle, ((1, 1), (0, 0), (0, 0)))
    field_x = -0.5 * (around_x[2:] - around_x[:-2])
    around_y = jnp.pad(middle, ((0, 0), (0, 0), (1, 1)))
    field_y = -0.5 * (around_y[:, :, 2:] - around_y[:, :, :-2])
    field_z = -0.5 * (potential[:, 2 : slab_depth + 3] - potential[:, : slab_depth + 1])
    field_table = jnp.stack([field_x, field_y, field_z], axis=2).reshape(NG * depth, 3 * NG)

    def sample_step(carry, items):
        bx, by, bz, boff = items
        plane_xz, weight_y = block_weights(bx, by, bz, boff[0], boff[1], boff[2], depth)
        lines = jnp.dot(plane_xz, field_table, precision=HIGHEST).reshape(bx.shape[0], 3, NG)
        return (carry, jnp.sum(lines * weight_y[:, None, :], axis=2))

    _, sampled = lax.scan(
        sample_step, jnp.zeros((), jnp.float32), (blocked_x, blocked_y, blocked_z, blocked_off)
    )
    kick = sampled.reshape(count_here, 3).transpose(1, 0)
    push_x, push_y = multipole_push(particle_cells, offsets, orders, strengths)
    push = jnp.stack([push_x, push_y, jnp.zeros_like(push_x)])
    new_momenta = momenta + kick + push
    new_coords = particle_cells.astype(jnp.float32) + offsets + new_momenta
    return (new_coords, new_momenta)


def halves(values):
    upper = values.astype(jnp.bfloat16)
    return (upper, (values - upper.astype(jnp.float32)).astype(jnp.bfloat16))


def table_halves(table):
    upper = table.astype(ml_dtypes.bfloat16)
    lower = (table - upper.astype(np.float64)).astype(ml_dtypes.bfloat16)
    return (jnp.asarray(upper), jnp.asarray(lower))


def mm(left, right):
    return jnp.dot(left, right, preferred_element_type=jnp.float32)


def mm_t(left, right):
    return lax.dot_general(left, right, (((1,), (1,)), ((), ())), preferred_element_type=jnp.float32)


def mm3(left, right):
    return mm(left[0], right[0]) + (mm(left[0], right[1]) + mm(left[1], right[0]))


def turn_blocks(parts):
    lanes = lax.broadcasted_iota(jnp.int32, parts[0].shape, 1)
    low = lanes < 64
    even = (lanes // 32) % 2 == 0
    pairs = []
    for first, second in ((parts[0], parts[2]), (parts[1], parts[3])):
        pairs.append(
            (
                jnp.where(low, first, pltpu.roll(second, 64, 1)),
                jnp.where(low, pltpu.roll(first, 64, 1), second),
            )
        )
    result = []
    for half in (0, 1):
        first, second = pairs[0][half], pairs[1][half]
        result.append(jnp.where(even, first, pltpu.roll(second, 32, 1)))
        result.append(jnp.where(even, pltpu.roll(first, 96, 1), second))
    return result


def tent(places, cells, fraction):
    away = places - cells
    return jnp.where(away == 0, 1.0 - fraction, jnp.where(away == 1, fraction, 0.0))


QUAD = 4
PLANES = 5
WIDE = 32
GROUPS = 9
SLOTS = 4 * GROUPS
FWD_ROWS = GROUPS * 2 * QUAD
BACK_ROWS = FWD_ROWS + 16
TOP_ROWS = 16 * 16 + 32
LOT = 512
CUTS = (0, 12, WIDE)
SORT_ROWS = 392
LIST_ROWS = SORT_ROWS + NG
SPAN = 3
PACK = 256
BIG = 56 * 1024 * 1024


def long_row(ref, start, count):
    return jnp.concatenate([ref[pl.ds(start + n, 1), :] for n in range(count)], axis=1)


def deposit_lots(acc_ref, rows_ref, base, ends_ref, me, bottom, top):
    span = LOT // NG
    ids = lax.broadcasted_iota(jnp.int32, (NG, LOT), 0).astype(jnp.float32)

    def step(lot, carry):
        low = ends_ref[0, lot * span].astype(jnp.int32) - me * QUAD
        high = ends_ref[1, lot * span + span - 1].astype(jnp.int32) + 1 - me * QUAD
        low = jnp.maximum(low, bottom)
        high = jnp.minimum(high, top)
        size = min(SPAN, top - bottom + 1)

        @pl.when(low <= high)
        def _():
            cell_x, cell_y, cell_z, off_x, off_y, off_z = [
                long_row(rows_ref, base + which * 64 + lot * span, span) for which in range(6)
            ]
            right = jnp.concatenate(halves(tent(ids, cell_x, off_x)), axis=0)
            weight_y = tent(ids, cell_y, off_y)

            def window(turn, inner):
                start = low + turn * size
                away = (start + me * QUAD).astype(jnp.float32) - cell_z
                left = []
                for z in range(size):
                    left.extend(halves(weight_y * tent(away + float(z), 0.0, off_z)))
                lines = mm_t(jnp.concatenate(left, axis=0), right)
                for z in range(size):
                    place = pl.ds(pl.multiple_of((start + z - bottom) * NG, NG), NG)
                    part = lines[2 * z * NG : (2 * z + 2) * NG]
                    acc_ref[place, :] += part[0:NG] + part[NG : 2 * NG]
                return inner

            lax.fori_loop(0, (high - low) // size + 1, window, 0)

        return carry

    lax.fori_loop(0, 64 // span, step, 0)


ACC_PLANES = QUAD + SPAN - 1
ENDS = slice(6 * 64, 6 * 64 + 8)


def deposit_own(place_ref, rows_ref, acc_ref, ends_ref, sem):
    ends = pltpu.make_async_copy(rows_ref.at[ENDS, :], ends_ref, sem)
    ends.start()
    acc_ref[...] = jnp.zeros_like(acc_ref)
    ends.wait()
    deposit_lots(acc_ref, rows_ref, 0, ends_ref, place_ref[0], 0, QUAD - 1)


def fetch_ends(rows_ref, ends_ref, sem):
    copies = [
        pltpu.make_async_copy(
            rows_ref.at[n * LIST_ROWS + ENDS.start : n * LIST_ROWS + ENDS.stop, :],
            ends_ref.at[n],
            sem.at[n],
        )
        for n in range(4)
    ]
    for copy in copies:
        copy.start()
    return copies


def deposit_rest(place_ref, rows_ref, start_ref, dens_ref, acc_ref, ends_ref, sem):
    copies = fetch_ends(rows_ref, ends_ref, sem)
    acc_ref[...] = start_ref[...]
    for copy in copies:
        copy.wait()
    me = place_ref[0]

    def each(turn, carry):
        n = lax.rem(me + turn, 4)
        deposit_lots(acc_ref, rows_ref, n * LIST_ROWS, ends_ref.at[n], me, 0, QUAD - 1)
        return carry

    lax.fori_loop(1, 4, each, 0)
    live = slice(0, QUAD * NG)
    dens_ref[...] = acc_ref[live, 0:NG] + acc_ref[live, NG : 2 * NG]


def forward_planes(lower_ref, dens_ref, list_ref, ty_hi, ty_lo, tx_hi, tx_lo, out_ref, left_ref, right_ref):
    half = 16 * GROUPS
    for z in range(QUAD):
        plane = dens_ref[z * NG : (z + 1) * NG, :]
        if z == 0:
            rims = [
                list_ref[n * LIST_ROWS + SORT_ROWS : (n + 1) * LIST_ROWS, :] for n in range(4)
            ]
            rim = (rims[0] + rims[1]) + (rims[2] + rims[3])
            plane = plane + jnp.where(lower_ref[0] > 0, rim, 0.0)
        lines = mm3((ty_hi[...], ty_lo[...]), halves(plane))
        real, imag = lines[0:half], lines[half : 2 * half]
        left_ref[pl.ds(2 * z, half, stride=8), :] = real
        right_ref[pl.ds(2 * z, half, stride=8), :] = imag
        left_ref[pl.ds(2 * z + 1, half, stride=8), :] = imag
        right_ref[pl.ds(2 * z + 1, half, stride=8), :] = -real
    for s in range(4):
        whole = []
        for i in range(4):
            start = (i * 4 + s) * FWD_ROWS
            piece = slice(start, start + FWD_ROWS)
            lines = jnp.concatenate([left_ref[piece, :], right_ref[piece, :]], axis=1)
            whole.append(mm3(halves(lines), (tx_hi[...], tx_lo[...])))
        for th in range(2):
            turned = turn_blocks([part[:, th * NG : (th + 1) * NG] for part in whole])
            for t in range(4):
                out_ref[(th * 4 + t) * 4 + s] = turned[t]


def green_send(lines_ref, first_ref, second_ref, row_ref, edge_ref, last_ref):
    fars = (first_ref, second_ref)
    for k in range(1, WIDE):
        piece = int(k >= CUTS[1])
        fars[piece][k - CUTS[piece]] = lines_ref[WIDE - k, WIDE : 2 * WIDE, :]
        edge_ref[k : k + 1, :] = lines_ref[WIDE - k, 0:1, :]
    first_ref[0] = lines_ref[0, WIDE : 2 * WIDE, :]
    edge_ref[0:1, :] = lines_ref[0, 0:1, :]
    row_ref[...] = lines_ref[0, WIDE : 2 * WIDE, :]
    last_ref[...] = lines_ref[0, 0:8, :]


def green_pairs(
    own_ref, first_ref, second_ref, row_ref, edge_ref, last_ref, pick_ref, out_ref, *parts
):
    for side in range(2):
        lanes = slice(side * NG, (side + 1) * NG)
        parts[side][...] = own_ref[:, lanes]
        for piece, ref in enumerate((first_ref, second_ref)):
            parts[2 + side][CUTS[piece] * WIDE : CUTS[piece + 1] * WIDE, :] = ref[:, lanes]
        parts[2 + side][0:WIDE, :] = row_ref[:, lanes]
    first = lax.broadcasted_iota(jnp.int32, (WIDE, 2 * NG), 0) == 0
    edge = jnp.where(first, jnp.broadcast_to(last_ref[0:1, :], (WIDE, 2 * NG)), edge_ref[...])

    def pull(refs, start, stride):
        return jnp.concatenate(
            [ref[pl.ds(start, WIDE, stride=stride), :] for ref in refs], axis=1
        )

    for group in range(GROUPS):
        near, away = [], []
        for i in range(4):
            j = group * 4 + i
            if j > WIDE:
                near.append(jnp.zeros((WIDE, 2 * NG), jnp.float32))
                away.append(jnp.zeros((WIDE, 2 * NG), jnp.float32))
                continue
            near.append(pull(parts[0:2], j, 2 * WIDE))
            away.append(edge if j == 0 else pull(parts[2:4], WIDE - j, WIDE))
        both = jnp.concatenate(
            [jnp.concatenate(near, axis=0), jnp.concatenate(away, axis=0)], axis=1
        )
        high = both.astype(jnp.bfloat16)
        left = both - high.astype(jnp.float32)
        mid = left.astype(jnp.bfloat16)
        low = (left - mid.astype(jnp.float32)).astype(jnp.bfloat16)
        pick = pick_ref[...]
        out_ref[:, group * NG : (group + 1) * NG] = 0.5 * (
            mm_t(pick, high) + (mm_t(pick, mid) + mm_t(pick, low))
        )


def spectrum_stage(in_ref, green_ref, wf_hi, wf_lo, wb_hi, wb_lo, out_ref):
    slabs = in_ref.shape[0]
    half = 2 * NG
    for first in range(0, GROUPS, 2):
        groups = [g for g in (first, first + 1) if g < GROUPS]
        data = [in_ref[:, g * 8 : (g + 1) * 8, :].reshape(slabs * 8, NG) for g in groups]
        data = data[0] if len(data) == 1 else jnp.concatenate(data, axis=1)
        spec = mm3((wf_hi[...], wf_lo[...]), halves(data))
        green = green_ref[:, first * NG : (first + len(groups)) * NG]
        scaled = jnp.concatenate([spec[0:half] * green, spec[half : 2 * half] * green], axis=0)
        back = mm3((wb_hi[...], wb_lo[...]), halves(scaled))
        for place, g in enumerate(groups):
            part = back[:, place * NG : (place + 1) * NG]
            for slab in range(slabs):
                row = slab * BACK_ROWS + g * 8
                out_ref[row : row + 8, :] = part[slab * 8 : slab * 8 + 8]
            for c in range(2):
                start = slabs * (8 + c)
                top = part[start : start + slabs]
                if g < GROUPS - 1:
                    out_ref[pl.ds(FWD_ROWS + 2 * g + c, slabs, stride=BACK_ROWS), :] = top
                else:
                    spot = pl.ds(8 * g + c, slabs, stride=BACK_ROWS)
                    lanes = lax.broadcasted_iota(jnp.int32, (slabs, NG), 1)
                    moved = pltpu.roll(top, WIDE, 1)
                    mine = (lanes >= WIDE) & (lanes < 2 * WIDE)
                    out_ref[spot, :] = jnp.where(mine, moved, out_ref[spot, :])


def inverse_planes(
    in_ref, tx_hi, tx_lo, ty_hi, ty_lo, te_hi, te_lo, out_ref, mid_cos, mid_sin, top_cos, top_sin
):
    extra = BACK_ROWS - FWD_ROWS
    for s in range(4):
        main, rest, last = [[], [], [], []], [[], [], [], []], []
        for th in range(2):
            parts = [in_ref[(th * 4 + t) * 4 + s, 0:FWD_ROWS, :] for t in range(4)]
            tops = [in_ref[(th * 4 + t) * 4 + s, FWD_ROWS:BACK_ROWS, :] for t in range(4)]
            for i, block in enumerate(turn_blocks(parts)):
                main[i].append(block)
            for i, block in enumerate(turn_blocks(tops)):
                rest[i].append(block)
            tail = [pltpu.roll(part[FWD_ROWS - 8 :], NG - WIDE, 1) for part in parts]
            last.append(turn_blocks(tail)[0])
        for i in range(4):
            row = (i * 4 + s) * FWD_ROWS
            lines = jnp.concatenate(main[i], axis=1)
            lines = mm3(halves(lines), (tx_hi[...], tx_lo[...]))
            mid_cos[row : row + FWD_ROWS, :] = lines[:, 0:NG]
            mid_sin[row : row + FWD_ROWS, :] = lines[:, NG : 2 * NG]
            row = (i * 4 + s) * extra
            lines = jnp.concatenate(rest[i], axis=1)
            lines = mm3(halves(lines), (tx_hi[...], tx_lo[...]))
            top_cos[row : row + extra, :] = lines[:, 0:NG]
            top_sin[row : row + extra, :] = lines[:, NG : 2 * NG]
        row = 16 * extra + 8 * s
        lines = mm3(halves(jnp.concatenate(last, axis=1)), (tx_hi[...], tx_lo[...]))
        top_cos[row : row + 8, :] = lines[:, 0:NG]
        top_sin[row : row + 8, :] = lines[:, NG : 2 * NG]

    def finish(cos_ref, sin_ref, start, count, stride, table):
        real, imag = pl.ds(start, count, stride=stride), pl.ds(start + 1, count, stride=stride)
        lines = jnp.concatenate(
            [cos_ref[real, :] - sin_ref[imag, :], sin_ref[real, :] + cos_ref[imag, :]], axis=0
        )
        return mm3((table[0][...], table[1][...]), halves(lines))

    for z in range(QUAD):
        out_ref[z] = finish(mid_cos, mid_sin, 2 * z, 16 * GROUPS, 8, (ty_hi, ty_lo))
    out_ref[QUAD] = finish(top_cos, top_sin, 0, TOP_ROWS // 2, 2, (te_hi, te_lo))


SORT_BITS = 13
DEAD = 100


def sort_network(items, rolled=False):
    shape = (8, NG)
    lanes = lax.broadcasted_iota(jnp.int32, shape, 1)
    subs = lax.broadcasted_iota(jnp.int32, shape, 0)
    base = subs * 8 + (lanes // 64) * 64 + (lanes % 64) * 128

    def exchange(items, others, bit, size):
        fresh = [[] for _ in items]
        for v in range(8):
            rank = base + v
            keep = (((rank >> bit) ^ (rank >> (size + 1))) & 1) == 0
            take = (others[0][v] < items[0][v]) == keep
            for n in range(len(items)):
                fresh[n].append(jnp.where(take, others[n][v], items[n][v]))
        return fresh

    def near_stage(items, bit, size):
        others = [[item[v ^ (1 << bit)] for v in range(8)] for item in items]
        return exchange(items, others, bit, size)

    def far_stage(items, bit, size, index, axis):
        others = [[jnp.take_along_axis(value, index, axis=axis) for value in item] for item in items]
        return exchange(items, others, bit, size)

    def far_bit(items, bit, size):
        if bit < 3:
            return near_stage(items, bit, size)
        if bit < 6:
            return far_stage(items, bit, size, subs ^ (1 << (bit - 3)), 0)
        return far_stage(items, bit, size, lanes ^ (64 if bit == 6 else 1 << (bit - 7)), 1)

    for size in range(3 if rolled else SORT_BITS):
        for bit in range(size, -1, -1):
            items = far_bit(items, bit, size)
    if not rolled:
        return items

    def merge(size, items):
        def lane_step(n, items):
            bit = size - n
            index = lanes ^ jnp.where(bit == 6, 64, 1 << jnp.maximum(bit - 7, 0))
            return far_stage(items, bit, size, index, 1)

        def sub_step(n, items):
            bit = jnp.minimum(size, 5) - n
            return far_stage(items, bit, size, subs ^ (1 << (bit - 3)), 0)

        items = lax.fori_loop(0, jnp.maximum(size - 5, 0), lane_step, items)
        items = lax.fori_loop(0, jnp.minimum(size, 5) - 2, sub_step, items)
        for bit in (2, 1, 0):
            items = near_stage(items, bit, size)
        return items

    return lax.fori_loop(3, SORT_BITS, merge, items)


def laid_out(values):
    turned = jnp.transpose(jnp.concatenate(values, axis=0), (1, 0))
    return jnp.concatenate([turned[0:64], turned[64:128]], axis=1)


def sort_labels(v):
    lanes = lax.broadcasted_iota(jnp.int32, (8, NG), 1)
    subs = lax.broadcasted_iota(jnp.int32, (8, NG), 0)
    return (subs + v * 8) * 128 + (lanes // 64) * 64 + (lanes % 8) * 8 + (lanes // 8) % 8


def square_up(cells_ref, offs_ref, ints_ref, flts_ref):
    for k in range(64):
        lanes = slice(k * NG, (k + 1) * NG)
        for d in range(3):
            ints_ref[d, k : k + 1, :] = cells_ref[d : d + 1, lanes]
            flts_ref[d, k : k + 1, :] = offs_ref[d : d + 1, lanes]


def sort_by_z(
    place_ref,
    live_ref,
    cells_ref,
    offs_ref,
    out_ref,
    rim_ref,
    ints_ref,
    flts_ref,
    top_ref,
    ends_ref,
    sem,
):
    square_up(cells_ref, offs_ref, ints_ref, flts_ref)
    lanes = lax.broadcasted_iota(jnp.int32, (8, NG), 1)
    subs = lax.broadcasted_iota(jnp.int32, (8, NG), 0)
    keys, packs, offs = [], [], [[], [], []]
    for v in range(8):
        rows = slice(v * 8, v * 8 + 8)
        alive = (subs + v * 8) * NG + lanes < live_ref[0]
        cell_z = jnp.where(alive, ints_ref[2, rows, :] - place_ref[0], DEAD)
        keys.append(cell_z * 8192 + sort_labels(v))
        packs.append(ints_ref[0, rows, :] * NG + ints_ref[1, rows, :])
        for d in range(3):
            offs[d].append(flts_ref[d, rows, :])
    items = [laid_out(item) for item in sort_network([keys, packs] + offs)]
    cell_z = (items[0] >> 13).astype(jnp.float32)
    out_ref[0:64, :] = (items[1] >> 7).astype(jnp.float32)
    out_ref[64:128, :] = (items[1] & (NG - 1)).astype(jnp.float32)
    out_ref[128:192, :] = cell_z
    for d in range(3):
        out_ref[192 + 64 * d : 256 + 64 * d, :] = items[2 + d]
    ends = jnp.transpose(cell_z, (1, 0))
    ends = jnp.concatenate([ends[0:1], ends[NG - 1 : NG], jnp.zeros((6, 64), jnp.float32)], axis=0)
    out_ref[384:392, :] = jnp.concatenate([ends, ends], axis=1)
    fetch = pltpu.make_async_copy(out_ref.at[ENDS, :], ends_ref, sem)
    fetch.start()
    top_ref[...] = jnp.zeros_like(top_ref)
    fetch.wait()
    deposit_lots(top_ref, out_ref, 0, ends_ref, 0, 4 * QUAD, 4 * QUAD)
    rim_ref[...] = top_ref[:, 0:NG] + top_ref[:, NG : 2 * NG]


def sort_by_y(place_ref, cells_ref, offs_ref, out_int, out_off, ints_ref, flts_ref):
    square_up(cells_ref, offs_ref, ints_ref, flts_ref)
    keys, packs, offs = [], [], [[], [], []]
    for v in range(8):
        rows = slice(v * 8, v * 8 + 8)
        keys.append(ints_ref[1, rows, :] * 8192 + sort_labels(v))
        packs.append(ints_ref[0, rows, :] * 64 + ints_ref[2, rows, :] - place_ref[0])
        for d in range(3):
            offs[d].append(flts_ref[d, rows, :])
    items = [laid_out(item) for item in sort_network([keys, packs] + offs, rolled=True)]
    cell_y = items[0] >> 13
    out_int[0:64, :] = cell_y
    out_int[64:128, :] = items[0] & 8191
    out_int[128:192, :] = items[1] >> 6
    out_int[192:256, :] = items[1] & 63
    for d in range(3):
        out_off[d * 64 : d * 64 + 64, :] = items[2 + d]
    ends = jnp.transpose(cell_y, (1, 0))
    ends = jnp.concatenate([ends[0:1], ends[NG - 1 : NG], jnp.zeros((6, 64), jnp.int32)], axis=0)
    out_int[256:264, :] = jnp.concatenate([ends, ends], axis=1)


def sample(
    place_ref,
    own_ref,
    core_ref,
    chip_ref,
    last_ref,
    int_ref,
    off_ref,
    mom_ref,
    push_ref,
    home_ref,
    coord_ref,
    out_ref,
    pot_ref,
    field_ref,
    kick_ref,
    ends_ref,
    sem,
):
    ends = pltpu.make_async_copy(int_ref.at[256:264, :], ends_ref, sem)
    ends.start()
    me = place_ref[0]
    for turn, ref in enumerate((own_ref, core_ref, chip_ref, last_ref)):
        pot_ref[pl.ds((me ^ turn) * PLANES, PLANES)] = ref[...]
    depth = field_ref.shape[0] // 3
    rows = lax.broadcasted_iota(jnp.int32, (NG, NG), 0)
    lanes = lax.broadcasted_iota(jnp.int32, (NG, NG), 1)
    blank = jnp.zeros((8, NG), jnp.float32)

    def fields(z, carry):
        plane = pot_ref[z + 1]
        right = jnp.where(lanes == NG - 1, 0.0, pltpu.roll(plane, NG - 1, 1))
        left = jnp.where(lanes == 0, 0.0, pltpu.roll(plane, 1, 1))
        field_ref[z, 0:NG, :] = -0.5 * (right - left)
        right = jnp.where(rows == NG - 1, 0.0, pltpu.roll(plane, NG - 1, 0))
        left = jnp.where(rows == 0, 0.0, pltpu.roll(plane, 1, 0))
        field_ref[depth + z, 0:NG, :] = -0.5 * (right - left)
        field_ref[2 * depth + z, 0:NG, :] = -0.5 * (pot_ref[z + 2] - pot_ref[z])
        for d in range(3):
            field_ref[d * depth + z, NG : NG + 8, :] = blank
        return carry

    lax.fori_loop(0, depth, fields, 0)
    x_ids = lax.broadcasted_iota(jnp.int32, (NG, PACK), 0)
    z_ids = lax.broadcasted_iota(jnp.int32, (24, PACK), 0)
    y_ids = lax.broadcasted_iota(jnp.int32, (8, PACK), 0)
    span = PACK // NG
    ends.wait()

    def pack_step(pack, carry):
        first = pack * span
        cell_y, cell_x, cell_z = [
            long_row(int_ref, which * 64 + first, span) for which in (0, 2, 3)
        ]
        off_x, off_y, off_z = [long_row(off_ref, which * 64 + first, span) for which in range(3)]
        weight_x = halves(tent(x_ids, cell_x, off_x))
        tall = [jnp.concatenate([part, part], axis=0) for part in weight_x]
        weight_z = tent(z_ids, cell_z, off_z)
        low = ends_ref[0, first]
        high = ends_ref[1, first + span - 1] + 1

        def chunk(turn):
            start = low + turn * 8
            weight_y = tent(y_ids + start, cell_y, off_y)
            table = field_ref[:, pl.ds(start, 8), :].reshape(3 * depth * 8, NG)
            part = jnp.concatenate(halves(table), axis=1)
            lines = mm(part, tall[0]) + mm(part, tall[1])
            fresh = []
            for d in range(3):
                total = lines[d * depth * 8 : d * depth * 8 + 8] * weight_z[0:1]
                for z in range(1, depth):
                    row = (d * depth + z) * 8
                    total = total + lines[row : row + 8] * weight_z[z : z + 1]
                fresh.append(jnp.sum(total * weight_y, axis=0, keepdims=True))
            return fresh

        for d, kick in enumerate(chunk(0)):
            for n in range(span):
                kick_ref[d, pl.ds(first + n, 1), :] = kick[:, n * NG : (n + 1) * NG]
        return (low, high, first, chunk)

    def pair_step(pair, carry):
        packs = [pack_step(8 * pair + n, 0) for n in range(8)]
        for low, high, first, chunk in packs:

            def more(turn, inner):
                for d, kick in enumerate(chunk(turn)):
                    for n in range(span):
                        kick_ref[d, pl.ds(first + n, 1), :] += kick[:, n * NG : (n + 1) * NG]
                return inner

            lax.fori_loop(1, (high - low) // 8 + 1, more, 0)
        return carry

    lax.fori_loop(0, 8 // span, pair_step, 0)
    items = [[int_ref[64 + v * 8 : v * 8 + 72, :] for v in range(8)]]
    for d in range(3):
        items.append([kick_ref[d, v * 8 : v * 8 + 8, :] for v in range(8)])
    items = sort_network(items)
    for d in range(3):
        kick = laid_out(items[1 + d])
        for k in range(64):
            out_ref[d : d + 1, k * NG : (k + 1) * NG] = kick[k : k + 1, :]
    fresh = (mom_ref[...] + out_ref[...]) + push_ref[...]
    out_ref[...] = fresh
    coord_ref[...] = home_ref[...] + fresh


def plane_tables(trk_count, sub_count, unit_charge):
    doubled = 2 * NG
    width = doubled // sub_count
    slots = np.arange(4)[:, None, None] + 4 * np.arange(GROUPS)[None, None, :]
    slots = np.broadcast_to(slots, (4, sub_count, GROUPS))
    freq = width * np.arange(sub_count)[None, :, None] + slots
    used = (slots <= width // 2).astype(np.float64)
    share = used * np.where((slots == 0) | (slots == width // 2), 1.0, 2.0)
    cells = np.arange(NG)
    turn = 2.0 * np.pi / doubled
    angle = turn * ((freq.reshape(-1)[:, None] * cells[None, :]) % doubled)
    used = used.reshape(-1)[:, None]
    share_line = share.reshape(-1)[:, None]
    ty = np.concatenate([np.cos(angle) * used, -np.sin(angle) * used], axis=0) * unit_charge
    back = np.concatenate([np.cos(angle) * share_line, -np.sin(angle) * share_line], axis=0)
    ty_back = back.T / doubled
    pieces = back.reshape(2, 4 * sub_count, GROUPS, NG)
    tail = np.zeros((2, sub_count, 4, NG))
    tail[:, :, 0] = pieces[:, :sub_count, GROUPS - 1]
    body = pieces[:, :, : GROUPS - 1].reshape(2, -1, NG)
    pieces = np.concatenate([body, tail.reshape(2, -1, NG)], axis=1)
    te_back = pieces.reshape(-1, NG).T / doubled
    angle = turn * ((cells[:, None] * np.arange(doubled)[None, :]) % doubled)
    tx = np.concatenate([np.cos(angle), np.sin(angle)], axis=0)
    tx_back = np.concatenate([np.cos(angle).T, np.sin(angle).T], axis=1) / doubled
    slabs = trk_count * sub_count
    angle = turn * ((np.arange(doubled)[:, None] * cells[None, :]) % doubled)
    cos, sin = np.cos(angle), np.sin(angle)
    wf = np.stack(
        [np.stack([cos, sin], axis=2), np.stack([-sin, cos], axis=2)], axis=0
    ).reshape(2 * doubled, 2 * NG)
    slab = np.arange(slabs)
    planes = (
        (slab // sub_count * QUAD * sub_count - 1 + PLANES * (slab % sub_count))[:, None]
        + np.arange(PLANES)[None, :]
    )
    inside = ((planes >= 0) & (planes < NG)).astype(np.float64)[:, :, None] / doubled
    angle = turn * ((planes[:, :, None] * np.arange(doubled)[None, None, :]) % doubled)
    cos, sin = np.cos(angle) * inside, np.sin(angle) * inside
    wb = np.stack([np.concatenate([cos, -sin], axis=2), np.concatenate([sin, cos], axis=2)], axis=2)
    wb = np.concatenate(
        [
            wb[:, :QUAD].reshape(slabs * QUAD * 2, 2 * doubled),
            wb[:, QUAD, 0],
            wb[:, QUAD, 1],
        ],
        axis=0,
    )
    pick = np.zeros((doubled, 2 * doubled))
    line = np.arange(doubled)
    pick[line, line] = 1.0
    pick[line, doubled + (-line) % doubled] = 1.0
    return ty, tx, wf, wb, tx_back, ty_back, te_back, pick


def run(body, shapes, scratch, *args, scalars=0):
    out_shape = tuple(jax.ShapeDtypeStruct(*shape) for shape in shapes)
    space = pl.BlockSpec(memory_space=pltpu.VMEM)
    result = pl.pallas_call(
        body,
        out_shape=out_shape,
        in_specs=[pl.BlockSpec(memory_space=pltpu.SMEM)] * scalars + [space] * (len(args) - scalars),
        out_specs=tuple(space for _ in out_shape),
        scratch_shapes=[
            pltpu.VMEM(*shape) if isinstance(shape, tuple) else shape for shape in scratch
        ],
        compiler_params=pltpu.CompilerParams(vmem_limit_bytes=BIG),
    )(*args)
    return result


def spread_device(particle_cells, offsets, momenta, live_counts, green_hat, orders, strengths):
    f32 = jnp.float32
    trk_count = lax.axis_size("trk")
    sub_count = lax.axis_size("sub")
    slabs = trk_count * sub_count
    slab_depth = NG // trk_count
    count_here = particle_cells.shape[1]
    unit_charge = float(NG**3) / float(count_here * slabs)
    both = ("trk", "sub")
    tables = plane_tables(trk_count, sub_count, unit_charge)
    ty, tx, wf, wb, tx_back, ty_back, te_back = [table_halves(table) for table in tables[:7]]
    pick = jnp.asarray(tables[7].astype(ml_dtypes.bfloat16))

    def flat(t, s):
        return (t % trk_count) * sub_count + s % sub_count

    pairs = [(t, s) for t in range(trk_count) for s in range(sub_count)]
    width = green_hat.shape[2]
    lines = jnp.transpose(green_hat, (0, 2, 1))
    half = width // 2
    first, second, row, edge, last = run(
        green_send,
        [((CUTS[n + 1] - CUTS[n], half, 2 * NG), f32) for n in range(2)]
        + [
            ((half, 2 * NG), f32),
            ((width // 2, 2 * NG), f32),
            ((8, 2 * NG), f32),
        ],
        [],
        lines,
    )

    def mirrored(value, trk_shift, sub_shift):
        moves = [
            (flat(t, s), flat(trk_count - trk_shift - t, sub_count - sub_shift - s))
            for t, s in pairs
        ]
        return lax.ppermute(value, both, moves)

    first = mirrored(first, 1, 1)

    def partner(value, turn):
        return lax.ppermute(value, both, [(flat(t, s), flat(t, s ^ turn)) for t, s in pairs])

    place = lax.axis_index("sub").reshape(1)
    base = (lax.axis_index("trk") * slab_depth).reshape(1)
    square = [((3, 64, NG), jnp.int32), ((3, 64, NG), f32)]
    rows, rim = run(
        sort_by_z,
        [((SORT_ROWS, NG), f32), ((NG, NG), f32)],
        square
        + [((NG, 2 * NG), f32), pltpu.SMEM((8, NG), f32), pltpu.SemaphoreType.DMA],
        base,
        live_counts,
        particle_cells,
        offsets,
        scalars=2,
    )
    rim = lax.ppermute(rim, both, [(flat(t, s), flat(t + 1, s)) for t, s in pairs])
    acc_shape = ((ACC_PLANES * NG, 2 * NG), f32)
    (start,) = run(
        deposit_own,
        [acc_shape],
        [pltpu.SMEM((8, NG), f32), pltpu.SemaphoreType.DMA],
        place,
        rows,
        scalars=1,
    )
    rim, start, first, second, row, edge, last = lax.optimization_barrier(
        (rim, start, first, second, row, edge, last)
    )
    shared = lax.all_gather(jnp.concatenate([rows, rim], axis=0), "sub", axis=0, tiled=True)
    second = mirrored(second, 1, 1)
    row = mirrored(row, 0, 1)
    edge = mirrored(edge, 1, 0)
    last = mirrored(last, 0, 0)
    lower = lax.axis_index("trk") > 0
    lower = lower & (lax.axis_index("sub") == 0)
    ends = [pltpu.SMEM((4, 8, NG), f32), pltpu.SemaphoreType.DMA((4,))]
    (dens,) = run(
        deposit_rest,
        [((QUAD * NG, NG), f32)],
        [acc_shape] + ends,
        place,
        shared,
        start,
        scalars=1,
    )
    (sent,) = run(
        forward_planes,
        [((slabs, FWD_ROWS, NG), f32)],
        [((16 * FWD_ROWS, NG), f32)] * 2,
        lower.astype(jnp.int32).reshape(1),
        dens,
        shared,
        *ty,
        *tx,
        scalars=1,
    )
    late_cells, late_offs, first, second, row, edge, last, _ = lax.optimization_barrier(
        (particle_cells, offsets, first, second, row, edge, last, sent)
    )
    got = lax.all_to_all(sent, both, split_axis=0, concat_axis=0, tiled=True)
    ints, offs = run(
        sort_by_y,
        [((264, NG), jnp.int32), ((192, NG), f32)],
        square,
        base,
        late_cells,
        late_offs,
        scalars=1,
    )
    push_x, push_y = multipole_push(late_cells, late_offs, orders, strengths)
    push = jnp.stack([push_x, push_y, jnp.zeros_like(push_x)])
    (green,) = run(
        green_pairs,
        [((2 * NG, GROUPS * NG), f32)],
        [((2 * WIDE * WIDE, NG), f32)] * 2 + [((WIDE * WIDE, NG), f32)] * 2,
        lines.reshape(-1, 2 * NG),
        first.reshape(-1, 2 * NG),
        second.reshape(-1, 2 * NG),
        row,
        edge,
        last,
        pick,
    )
    home = late_cells.astype(f32) + late_offs
    got, ints, offs, push, home = lax.optimization_barrier((got, ints, offs, push, home))
    (sent,) = run(
        spectrum_stage, [((slabs * BACK_ROWS, NG), f32)], [], got, green, *wf, *wb
    )
    got = lax.all_to_all(
        sent.reshape(slabs, BACK_ROWS, NG), both, split_axis=0, concat_axis=0, tiled=True
    )
    (pot,) = run(
        inverse_planes,
        [((PLANES, NG, NG), f32)],
        [((16 * FWD_ROWS, NG), f32)] * 2 + [((TOP_ROWS, NG), f32)] * 2,
        got,
        *tx_back,
        *ty_back,
        *te_back,
    )
    chip_pot = partner(pot, 2)
    core_pot = partner(pot, 1)
    last_pot = partner(chip_pot, 1)
    depth = slab_depth + 1
    coords, fresh = run(
        sample,
        [((3, count_here), f32)] * 2,
        [
            ((sub_count * PLANES, NG, NG), f32),
            ((3 * depth, NG + 8, NG), f32),
            ((3, 64, NG), f32),
            pltpu.SMEM((8, NG), jnp.int32),
            pltpu.SemaphoreType.DMA,
        ],
        place,
        pot,
        core_pot,
        chip_pot,
        last_pot,
        ints,
        offs,
        momenta,
        push,
        home,
        scalars=1,
    )
    return (coords, fresh)


def solution(mesh):
    in_specs = (
        P(None, ("trk", "sub")),
        P(None, ("trk", "sub")),
        P(None, ("trk", "sub")),
        P(("trk", "sub")),
        P("trk", None, "sub"),
        P(),
        P(),
    )
    out_specs = (P(None, ("trk", "sub")), P(None, ("trk", "sub")))
    trk_count, sub_count = mesh.shape["trk"], mesh.shape["sub"]
    fits = sub_count == 4 and trk_count * WIDE == 2 * NG
    body = spread_device if fits else per_device
    return jax.shard_map(
        body, mesh=mesh, in_specs=in_specs, out_specs=out_specs, check_vma=False
    )
```
